512 devices in a mesh: tm: 64 (over x, z), net: 8 (over y, core).
Axes of the slice: x: 4, y: 4, z: 16, core: 2. Of those that a mesh axis runs over, the one named last changes fastest.
Arguments:
- forcing: float32 [4096, 2, 16384], P('tm', None, 'net'), may hold values from -1.5 to 1.5
- friction_class: int32 [16384], P('net'), may hold values from 0 to 7
- compressor: int32 [16384], P('net'), may hold values 0 or 1
- blocks: float32 [3, 2, 2, 9], replicated, may hold values from -1 to 1, as said below
Outputs:
- solution: float32 [4096, 2, 16384], P('tm', None, 'net')
The draws below stay inside these ranges and needn't reach their ends.
Inputs may be any that keep to these rules, and one draw needn't show every extreme that they name: `blocks`: each 2 x 2 block has operator norm at most 1.
All inputs are finite; a program needn't handle non-finite values. No bound on the sum of `compressor` on one device may be relied on, other than what follows from the above.
Results may differ from the reference program's by a relative error of at most 0.0003.
Values sent between devices are 32-bit elements; how exact they have to be, the bound alone decides.
No kernel may reach another device: no remote copies, remote signals or barrier semaphores. Data moves between devices by JAX's collectives and lax.ppermute only.
A program may use at most 64 MiB of HBM per device.

```python
import jax
import jax.numpy as jnp
from jax import lax

SEGMENTS = 16384
FACTOR = 8
STEPS = 4096
NCLASS = 8
CYCLES = 2


def draw_blocks(key, part):
    rate_key, angle_key = jax.random.split(key)
    kinds_total = NCLASS + 1
    low_rate = 0.5 / STEPS
    high_rate = 1.0 / 40.0
    rates = jnp.exp(jax.random.uniform(rate_key, (kinds_total,), jnp.float32, jnp.log(low_rate), jnp.log(high_rate)))
    angles = jax.random.uniform(angle_key, (kinds_total,), jnp.float32, -0.6, 0.6)
    spans = jnp.array([1.0, FACTOR, FACTOR * FACTOR], jnp.float32)[:, None]
    radius = jnp.exp(-rates[None, :] * spans)
    turned = angles[None, :] * spans
    cosine = radius * jnp.cos(turned)
    sine = radius * jnp.sin(turned)
    upper_row = jnp.stack([cosine, sine], axis=1)
    lower_row = jnp.stack([-sine, cosine], axis=1)
    return jnp.stack([upper_row, lower_row], axis=1)


def place_ends(drawn, own_key, low, largest):
    longest = drawn.shape.index(max(drawn.shape))
    spots = []
    for shift in (0, 1):
        where = [jax.random.randint(jax.random.fold_in(own_key, axis), (), 0, length) for axis, length in enumerate(drawn.shape)]
        where[longest] = (where[longest] + shift) % drawn.shape[longest]
        spots.append(tuple(where))
    return drawn.at[spots[0]].set(low).at[spots[1]].set(largest)


def block_levels(stream_key, extent, cuts, least, high):
    def one(axis_at, shards_of):
        draws = jax.random.uniform(jax.random.fold_in(jax.random.fold_in(stream_key, 6), axis_at), (shards_of,), jnp.float32, least / len(cuts), high / len(cuts))
        return jnp.repeat(jnp.exp(draws), extent[axis_at] // shards_of).reshape((-1,) + (1,) * (len(extent) - axis_at - 1))

    factor_of = one(*cuts[0])
    for cut in cuts[1:]:
        factor_of = factor_of * one(*cut)
    return factor_of


def noise(own_key, shape, scale, limit, cuts=(), kind=jnp.bfloat16):
    gain = block_levels(own_key, shape, cuts, -0.22, 0.18) if cuts else 1.0
    entries = jax.random.normal(own_key, shape, jnp.float32) * scale * gain
    return jnp.minimum(jnp.maximum(entries, -limit), limit).astype(kind)


def setup_inputs(seed: int = 0) -> dict:
    splits = jax.random.split(jax.random.key(seed), 5)
    forcing = noise(splits[0], (STEPS, 2, SEGMENTS), 0.25, 1.5, ((0, 64), (2, 8)), jnp.float32)
    friction_class = place_ends(jax.random.randint(splits[1], (SEGMENTS,), 0, NCLASS), jax.random.fold_in(splits[1], 1), 0, NCLASS - 1).astype(jnp.int32)
    compressor = place_ends((jax.random.randint(splits[2], (SEGMENTS,), 0, 16) < 1).astype(jnp.int32), jax.random.fold_in(splits[2], 1), 0, 1)
    blocks = draw_blocks(jax.random.fold_in(splits[4], 71), 0)
    return {"forcing": forcing, "friction_class": friction_class, "compressor": compressor, "blocks": blocks}


COUPLE = 0.25


def apply_block(first_part, second_part, weights):
    upper_row = weights[0, 0] * first_part + weights[0, 1] * second_part
    lower_row = weights[1, 0] * first_part + weights[1, 1] * second_part
    return jnp.stack([upper_row, lower_row], axis=-2)


def transport(current, weights):
    padded = jnp.pad(current, ((0, 0), (0, 0), (1, 1)))
    pressure = padded[:, 0]
    flowing = padded[:, 1]
    mixed_press = (1.0 - 2.0 * COUPLE) * pressure[:, 1:-1] - COUPLE * flowing[:, :-2] + COUPLE * flowing[:, 2:]
    mixed_flow = (1.0 - 2.0 * COUPLE) * flowing[:, 1:-1] + COUPLE * pressure[:, :-2] - COUPLE * pressure[:, 2:]
    return apply_block(mixed_press, mixed_flow, weights)


def relax_sweep(start, forcings, weights):
    results = []
    current = start
    for position in range(forcings.shape[0]):
        current = transport(current, weights) + forcings[position]
        results.append(current)
    return jnp.stack(results)


def reference(forcing, friction_class, compressor, blocks):
    segment_kind = jnp.where(compressor == 1, NCLASS, friction_class)
    onehot = (segment_kind[None, :] == jnp.arange(NCLASS + 1)[:, None]).astype(jnp.float32)
    weights = [jnp.einsum("abk,ks->abs", blocks[number], onehot, precision=lax.Precision.HIGHEST) for number in range(3)]
    seg_count = forcing.shape[2]
    groups = STEPS // FACTOR
    windows = groups // FACTOR
    solution = jnp.zeros_like(forcing)
    forcing_grouped = forcing.reshape(groups, FACTOR, 2, seg_count)
    for cycle_number in range(CYCLES):
        grouped = solution.reshape(groups, FACTOR, 2, seg_count)
        previous = jnp.concatenate([jnp.zeros((1, 2, seg_count), forcing.dtype), grouped[:-1, FACTOR - 1]], axis=0)
        last_force = forcing_grouped[:, FACTOR - 1] - grouped[:, FACTOR - 1]
        driving = jnp.concatenate([forcing_grouped[:, :FACTOR - 1], last_force[:, None]], axis=1).transpose(1, 0, 2, 3)
        relaxed = relax_sweep(previous, driving, weights[0])
        coarse_rhs = relaxed[FACTOR - 1]
        middle_drive = coarse_rhs.reshape(windows, FACTOR, 2, seg_count).transpose(1, 0, 2, 3)
        middle = relax_sweep(jnp.zeros((windows, 2, seg_count), forcing.dtype), middle_drive, weights[1])
        top_rhs = middle[FACTOR - 1]

        def advance(carried, rhs_row):
            following = apply_block(carried[0], carried[1], weights[2]) + rhs_row
            return following, following

        _, top_values = lax.scan(advance, jnp.zeros((2, seg_count), forcing.dtype), top_rhs)
        previous_top = jnp.concatenate([jnp.zeros((1, 2, seg_count), forcing.dtype), top_values[:-1]], axis=0)
        interp = relax_sweep(previous_top, middle_drive[:FACTOR - 1], weights[1])
        corrections = jnp.concatenate([interp, top_values[None]], axis=0).transpose(1, 0, 2, 3).reshape(groups, 2, seg_count)
        c_points = grouped[:, FACTOR - 1] + corrections
        solution = jnp.concatenate([relaxed[:FACTOR - 1].transpose(1, 0, 2, 3), c_points[:, None]], axis=1).reshape(STEPS, 2, seg_count)
    return solution
```

```python
import jax
import jax.numpy as jnp
from jax import lax
from jax.experimental import pallas as pl
from jax.experimental.pallas import tpu as pltpu
from jax.sharding import PartitionSpec as P

FACTOR = 8
KINDS = 9
LANES = 128
TILES = 16
WINDOWS = 64
PACKED = 24
RIGHT = 16
LEFT = 23
EDGE_ROWS = 136
ROWS_OF = list(range(TILES)) + [RIGHT, LEFT]
LISTED = len(ROWS_OF)
PREV = [LISTED - 1] + list(range(TILES)) + [LISTED - 1]
NEXT = list(range(1, TILES + 1)) + [TILES, 0]
SLAB = 32
MARGIN = 48


def lanes_of(shape):
    return lax.broadcasted_iota(jnp.int32, shape, len(shape) - 1)


def couple(p, q, p_low, p_high, q_low, q_high, w):
    mixed_p = (p + p) + (q_high - q_low)
    mixed_q = (q + q) + (p_low - p_high)
    return w[0] * mixed_p + w[1] * mixed_q, w[2] * mixed_p + w[3] * mixed_q


def apply2(p, q, w):
    return w[0] * p + w[1] * q, w[2] * p + w[3] * q


def phi_tiles(ps, qs, weight_of):
    lane = lanes_of((8, LANES))
    first, last = lane == 0, lane == LANES - 1

    def low(xs, t):
        return pltpu.roll(jnp.where(last, xs[PREV[t]], xs[t]), 1, 1)

    def high(xs, t):
        return pltpu.roll(jnp.where(first, xs[NEXT[t]], xs[t]), LANES - 1, 1)

    new_p, new_q = [], []
    for t in range(LISTED):
        p, q = couple(ps[t], qs[t], low(ps, t), high(ps, t), low(qs, t), high(qs, t), weight_of(t))
        new_p.append(p)
        new_q.append(q)
    return new_p, new_q


def phi_packed(p, q, w):
    lane = lanes_of((PACKED, LANES))
    first, last = lane == 0, lane == LANES - 1

    def low(x):
        return pltpu.roll(jnp.where(last, pltpu.roll(x, 1, 0), x), 1, 1)

    def high(x):
        return pltpu.roll(jnp.where(first, pltpu.roll(x, PACKED - 1, 0), x), LANES - 1, 1)

    return couple(p, q, low(p), high(p), low(q), high(q), w)


def phi_slab(p, q, w):
    return couple(
        p, q, pltpu.roll(p, 1, 1), pltpu.roll(p, LANES - 1, 1), pltpu.roll(q, 1, 1), pltpu.roll(q, LANES - 1, 1), w
    )


def pick(blocks_ref, number, kind):
    scale = 1.0 if number == 2 else 0.25
    masks = [kind == float(k + 1) for k in range(KINDS)]
    picked = []
    for entry in range(4):
        chosen = jnp.zeros_like(kind)
        for k in range(KINDS):
            chosen = jnp.where(masks[k], blocks_ref[(number * 4 + entry) * KINDS + k] * scale, chosen)
        picked.append(chosen)
    return picked


def load_forcing(f_ref, right_ref, left_ref, j, t, field):
    if t < TILES:
        return f_ref[pl.ds(j * 32 + t * 2 + field, 8, stride=256), :]
    edge = right_ref if t == TILES else left_ref
    return edge[pl.ds(j * 2 + field, 8, stride=16), :]


def tile_rows(t):
    return pl.ds(ROWS_OF[t] * 8, 8)


def fine_weights(w_ref):
    def weight_of(t):
        return [jnp.broadcast_to(w_ref[e, ROWS_OF[t] : ROWS_OF[t] + 1, :], (8, LANES)) for e in range(4)]

    return weight_of


def first_kernel(blocks_ref, f_ref, right_ref, left_ref, fc_ref, comp_ref, r1_ref, r2_ref, w_ref, kx_ref, send_ref,
                 prev_ref, c_ref, r1b_ref):
    kx_ref[0:TILES, :] = jnp.where(comp_ref[...] == 1, KINDS, fc_ref[...] + 1).astype(jnp.float32)
    kx_ref[TILES:PACKED, :] = jnp.zeros((PACKED - TILES, LANES), jnp.float32)
    kx_ref[RIGHT : RIGHT + 1, :] = right_ref[128:129, :]
    kx_ref[LEFT : LEFT + 1, :] = left_ref[128:129, :]
    kind = kx_ref[...]
    for number in range(3):
        for entry, chosen in enumerate(pick(blocks_ref, number, kind)):
            w_ref[number * 4 + entry] = chosen
    weight_of = fine_weights(w_ref)
    w1 = [w_ref[4 + e] for e in range(4)]

    def forcing(j, field):
        return [load_forcing(f_ref, right_ref, left_ref, j, t, field) for t in range(LISTED)]

    unused = jnp.zeros(((LEFT - RIGHT - 1) * 8, LANES), jnp.float32)
    for field in range(2):
        for ref in (r1_ref, r1b_ref):
            ref[field, (RIGHT + 1) * 8 : LEFT * 8, :] = unused

    ps, qs = forcing(0, 0), forcing(0, 1)
    for j in range(1, FACTOR):
        ps, qs = phi_tiles(ps, qs, weight_of)
        fp, fq = forcing(j, 0), forcing(j, 1)
        ps = [a + b for a, b in zip(ps, fp)]
        qs = [a + b for a, b in zip(qs, fq)]
    for t in range(LISTED):
        r1_ref[0, tile_rows(t), :] = ps[t]
        r1_ref[1, tile_rows(t), :] = qs[t]

    def sweep(ref, keep):
        p = q = None
        for k in range(FACTOR):
            rp, rq = ref[0, pl.ds(k, PACKED, stride=8), :], ref[1, pl.ds(k, PACKED, stride=8), :]
            if k == 0:
                p, q = rp, rq
            else:
                p, q = phi_packed(p, q, w1)
                p, q = p + rp, q + rq
            if keep:
                c_ref[0, pl.ds(k, PACKED, stride=8), :] = p
                c_ref[1, pl.ds(k, PACKED, stride=8), :] = q
                if k < FACTOR - 1:
                    prev_ref[0, pl.ds(k + 1, PACKED, stride=8), :] = p
                    prev_ref[1, pl.ds(k + 1, PACKED, stride=8), :] = q
        return p, q

    nothing = jnp.zeros((PACKED, LANES), jnp.float32)
    prev_ref[0, pl.ds(0, PACKED, stride=8), :] = nothing
    prev_ref[1, pl.ds(0, PACKED, stride=8), :] = nothing
    r2p, r2q = sweep(r1_ref, True)
    r2_ref[0] = r2p
    r2_ref[1] = r2q

    ps = [prev_ref[0, tile_rows(t), :] for t in range(LISTED)]
    qs = [prev_ref[1, tile_rows(t), :] for t in range(LISTED)]
    for j in range(FACTOR):
        ps, qs = phi_tiles(ps, qs, weight_of)
        fp, fq = forcing(j, 0), forcing(j, 1)
        ps = [a + b for a, b in zip(ps, fp)]
        qs = [a + b for a, b in zip(qs, fq)]
    for t in range(LISTED):
        r1b_ref[0, tile_rows(t), :] = ps[t] - c_ref[0, tile_rows(t), :]
        r1b_ref[1, tile_rows(t), :] = qs[t] - c_ref[1, tile_rows(t), :]
    gp, gq = sweep(r1b_ref, False)

    lane = lanes_of((TILES, LANES))
    for c, x in enumerate((r2p, r2q, gp, gq)):
        here, before, after = x[0:TILES], pltpu.roll(x, 1, 0)[0:TILES], pltpu.roll(x, PACKED - 1, 0)[0:TILES]
        for quarter in range(4):
            start = (SLAB * quarter - MARGIN) % LANES
            a, b = (before, here) if quarter < 2 else (here, after)
            piece = pltpu.roll(jnp.where(lane >= start, a, b), LANES - start, 1)
            send_ref[pl.ds(4 * quarter + c, TILES, stride=16), :] = piece


def slab_kernel(place_ref, blocks_ref, kx_ref, got_ref, send_ref, prev_ref, m_ref):
    place = place_ref[0]
    tile, quarter = place // 4, place % 4
    lane = lanes_of((1, LANES))
    start = (quarter * SLAB + (LANES - MARGIN)) % LANES
    base = jnp.where(quarter < 2, tile - 1, tile)
    base = jnp.where(base < 0, LEFT, base)
    after = jnp.where(base == LEFT, 0, base + 1)
    a, b = kx_ref[pl.ds(base, 1), :], kx_ref[pl.ds(after, 1), :]
    kind = pltpu.roll(jnp.where(lane >= start, a, b), LANES - start, 1)
    kind = jnp.broadcast_to(kind, (8, LANES))
    w0, w1, w2 = (pick(blocks_ref, number, kind) for number in range(3))
    sub = lax.broadcasted_iota(jnp.int32, (8, LANES), 0)

    def square(w):
        return [
            w[0] * w[0] + w[1] * w[2],
            w[0] * w[1] + w[1] * w[3],
            w[2] * w[0] + w[3] * w[2],
            w[2] * w[1] + w[3] * w[3],
        ]

    w_eight = square(square(square(w2)))
    w_jump = [w_eight, square(w_eight), square(square(w_eight))]

    def recurrence(rp, rq):
        tp, tq = rp[0], rq[0]
        for b in range(1, 8):
            tp, tq = apply2(tp, tq, w2)
            tp, tq = tp + rp[b], tq + rq[b]
        for step, w in zip((1, 2, 4), w_jump):
            sp = jnp.where(sub >= step, pltpu.roll(tp, step, 0), 0.0)
            sq = jnp.where(sub >= step, pltpu.roll(tq, step, 0), 0.0)
            sp, sq = apply2(sp, sq, w)
            tp, tq = tp + sp, tq + sq
        dp = [jnp.where(sub >= 1, pltpu.roll(tp, 1, 0), 0.0)]
        dq = [jnp.where(sub >= 1, pltpu.roll(tq, 1, 0), 0.0)]
        for b in range(1, 8):
            p, q = apply2(dp[b - 1], dq[b - 1], w2)
            dp.append(p + rp[b - 1])
            dq.append(q + rq[b - 1])
        return dp, dq

    def rows(b, c):
        return pl.ds(b * 4 + c, 8, stride=32)

    dp, dq = recurrence([got_ref[rows(b, 0), :] for b in range(8)], [got_ref[rows(b, 1), :] for b in range(8)])
    zero = jnp.zeros((8, LANES), jnp.float32)
    for b in range(8):
        send_ref[rows(b, 0), :] = dp[b]
        send_ref[rows(b, 1), :] = dq[b]
        prev_ref[0, b] = dp[b]
        prev_ref[1, b] = dq[b]
        m_ref[0, b] = zero
        m_ref[1, b] = zero

    def block(k, carry):
        ps = [prev_ref[0, b] for b in range(8)]
        qs = [prev_ref[1, b] for b in range(8)]
        for _ in range(FACTOR):
            both = [phi_slab(p, q, w0) for p, q in zip(ps, qs)]
            ps, qs = [x[0] for x in both], [x[1] for x in both]
        for b in range(8):
            np_, nq = phi_slab(prev_ref[0, b], prev_ref[1, b], w1)
            mp, mq = phi_slab(m_ref[0, b], m_ref[1, b], w1)
            m_ref[0, b] = mp + (ps[b] - np_)
            m_ref[1, b] = mq + (qs[b] - nq)
            prev_ref[0, b] = np_
            prev_ref[1, b] = nq
        return carry

    lax.fori_loop(0, FACTOR, block, 0)

    rp, rq = [], []
    for b in range(8):
        cp, cq = apply2(send_ref[rows(b, 0), :], send_ref[rows(b, 1), :], w2)
        rp.append(got_ref[rows(b, 2), :] + (m_ref[0, b] + (prev_ref[0, b] - cp)))
        rq.append(got_ref[rows(b, 3), :] + (m_ref[1, b] + (prev_ref[1, b] - cq)))
    dp, dq = recurrence(rp, rq)
    for b in range(8):
        send_ref[rows(b, 2), :] = dp[b]
        send_ref[rows(b, 3), :] = dq[b]


def last_kernel(f_ref, right_ref, left_ref, r1_ref, r2_ref, w_ref, got_ref, out_ref, prev_ref, c_ref, r1b_ref, d_ref):
    lane = lanes_of((TILES, LANES))
    lane1 = lanes_of((1, LANES))
    for c in range(4):
        whole = jnp.zeros((TILES, LANES), jnp.float32)
        for quarter in range(4):
            piece = got_ref[pl.ds(4 * quarter + c, TILES, stride=16), :]
            piece = pltpu.roll(piece, (SLAB * quarter - MARGIN) % LANES, 1)
            mine = (lane >= SLAB * quarter) & (lane < SLAB * (quarter + 1))
            whole = jnp.where(mine, piece, whole)
        d_ref[c, 0:TILES, :] = whole
        d_ref[c, TILES:PACKED, :] = jnp.zeros((PACKED - TILES, LANES), jnp.float32)
        low = pltpu.roll(got_ref[c : c + 1, :], LANES - MARGIN, 1)
        d_ref[c, LEFT : LEFT + 1, :] = jnp.where(lane1 >= LANES - MARGIN, low, 0.0)
        end = (WINDOWS - 1) * 4 + c
        high = pltpu.roll(got_ref[end : end + 1, :], MARGIN, 1)
        d_ref[c, RIGHT : RIGHT + 1, :] = jnp.where(lane1 < MARGIN, high, 0.0)

    weight_of = fine_weights(w_ref)
    w1 = [w_ref[4 + e] for e in range(4)]
    w2 = [w_ref[8 + e] for e in range(4)]
    unused = jnp.zeros(((LEFT - RIGHT - 1) * 8, LANES), jnp.float32)
    for field in range(2):
        r1b_ref[field, (RIGHT + 1) * 8 : LEFT * 8, :] = unused

    p, q = d_ref[0], d_ref[1]
    last_p, last_q = apply2(p, q, w2)
    c_ref[0, pl.ds(FACTOR - 1, PACKED, stride=8), :] = last_p + r2_ref[0]
    c_ref[1, pl.ds(FACTOR - 1, PACKED, stride=8), :] = last_q + r2_ref[1]
    prev_ref[0, pl.ds(0, PACKED, stride=8), :] = p
    prev_ref[1, pl.ds(0, PACKED, stride=8), :] = q
    for k in range(FACTOR - 1):
        p, q = phi_packed(p, q, w1)
        p = p + r1_ref[0, pl.ds(k, PACKED, stride=8), :]
        q = q + r1_ref[1, pl.ds(k, PACKED, stride=8), :]
        c_ref[0, pl.ds(k, PACKED, stride=8), :] = p
        c_ref[1, pl.ds(k, PACKED, stride=8), :] = q
        prev_ref[0, pl.ds(k + 1, PACKED, stride=8), :] = p
        prev_ref[1, pl.ds(k + 1, PACKED, stride=8), :] = q

    ps = [prev_ref[0, tile_rows(t), :] for t in range(LISTED)]
    qs = [prev_ref[1, tile_rows(t), :] for t in range(LISTED)]
    for j in range(FACTOR):
        ps, qs = phi_tiles(ps, qs, weight_of)
        for t in range(LISTED):
            ps[t] = ps[t] + load_forcing(f_ref, right_ref, left_ref, j, t, 0)
            qs[t] = qs[t] + load_forcing(f_ref, right_ref, left_ref, j, t, 1)
            if j < FACTOR - 1 and t < TILES:
                out_ref[pl.ds(j * 32 + t * 2, 8, stride=256), :] = ps[t]
                out_ref[pl.ds(j * 32 + t * 2 + 1, 8, stride=256), :] = qs[t]
    for t in range(LISTED):
        r1b_ref[0, tile_rows(t), :] = ps[t] - c_ref[0, tile_rows(t), :]
        r1b_ref[1, tile_rows(t), :] = qs[t] - c_ref[1, tile_rows(t), :]

    def finish(k, p, q):
        for field, x in enumerate((p, q)):
            done = c_ref[field, pl.ds(k, PACKED, stride=8), :] + x
            out_ref[pl.ds((8 * k + 7) * 32 + field, TILES, stride=2), :] = done[0:TILES]

    p, q = d_ref[2], d_ref[3]
    last_p, last_q = apply2(p, q, w2)
    mp = mq = None
    for k in range(FACTOR):
        rp, rq = r1b_ref[0, pl.ds(k, PACKED, stride=8), :], r1b_ref[1, pl.ds(k, PACKED, stride=8), :]
        if k == 0:
            mp, mq = rp, rq
        else:
            mp, mq = phi_packed(mp, mq, w1)
            mp, mq = mp + rp, mq + rq
        if k < FACTOR - 1:
            p, q = phi_packed(p, q, w1)
            p, q = p + rp, q + rq
            finish(k, p, q)
    finish(FACTOR - 1, last_p + mp, last_q + mq)


VMEM = pl.BlockSpec(memory_space=pltpu.VMEM)
SMEM = pl.BlockSpec(memory_space=pltpu.SMEM)
STATE = (2, PACKED * 8, LANES)


def shaped(*shape):
    return jax.ShapeDtypeStruct(shape, jnp.float32)


def scratch(*shape):
    return pltpu.VMEM(shape, jnp.float32)


def first_stage(flat_blocks, flat, right, left, friction, compressor):
    return pl.pallas_call(
        first_kernel,
        out_shape=(shaped(*STATE), shaped(2, PACKED, LANES), shaped(12, PACKED, LANES), shaped(PACKED, LANES), shaped(4 * WINDOWS, LANES)),
        in_specs=[SMEM] + [VMEM] * 5,
        out_specs=(VMEM,) * 5,
        scratch_shapes=[scratch(*STATE)] * 3,
        name="first",
    )(flat_blocks, flat, right, left, friction, compressor)


def slab_stage(place, flat_blocks, kinds, got):
    return pl.pallas_call(
        slab_kernel,
        out_shape=shaped(4 * WINDOWS, LANES),
        in_specs=[SMEM, SMEM, VMEM, VMEM],
        out_specs=VMEM,
        scratch_shapes=[scratch(2, 8, 8, LANES)] * 2,
        name="slab",
    )(place, flat_blocks, kinds, got)


def last_stage(flat, right, left, r1, r2, weights, got):
    return pl.pallas_call(
        last_kernel,
        out_shape=shaped(2048, LANES),
        in_specs=[VMEM] * 7,
        out_specs=VMEM,
        scratch_shapes=[scratch(*STATE)] * 3 + [scratch(4, PACKED, LANES)],
        name="last",
    )(flat, right, left, r1, r2, weights, got)


def to_rows(forcing):
    return forcing.reshape(64, 2, TILES, LANES).transpose(0, 2, 1, 3).reshape(2048, LANES)


def from_rows(rows):
    return rows.reshape(64, TILES, 2, LANES).transpose(0, 2, 1, 3).reshape(64, 2, TILES * LANES)


def edge_of(flat, kinds, tile):
    sides = flat.reshape(64, 2 * TILES, LANES)[:, 2 * tile : 2 * tile + 2].reshape(128, LANES)
    return jnp.concatenate([sides, jnp.broadcast_to(kinds[tile : tile + 1], (EDGE_ROWS - 128, LANES))])


def one_based(friction, compressor):
    return jnp.where(compressor == 1, KINDS, friction + 1).astype(jnp.float32)


def transpose_windows(rows):
    return lax.all_to_all(rows.reshape(WINDOWS, 4, LANES), "tm", 0, 0).reshape(4 * WINDOWS, LANES)


def per_device(forcing, friction_class, compressor, blocks):
    flat = to_rows(forcing)
    flat_blocks = blocks.reshape(-1)
    friction = friction_class.reshape(TILES, LANES)
    station = compressor.reshape(TILES, LANES)
    kinds = one_based(friction, station)
    count = lax.axis_size("net")
    left = lax.ppermute(edge_of(flat, kinds, TILES - 1), "net", [(i, i + 1) for i in range(count - 1)])
    right = lax.ppermute(edge_of(flat, kinds, 0), "net", [(i + 1, i) for i in range(count - 1)])
    r1, r2, weights, kinds_wide, send = first_stage(flat_blocks, flat, right, left, friction, station)
    got = transpose_windows(send)
    place = lax.axis_index("tm").astype(jnp.int32).reshape(1)
    send = slab_stage(place, flat_blocks, kinds_wide, got)
    got = transpose_windows(send)
    return from_rows(last_stage(flat, right, left, r1, r2, weights, got))


def solution(mesh):
    placed = (P("tm", None, "net"), P("net"), P("net"), P())
    return jax.shard_map(
        per_device, mesh=mesh, in_specs=placed, out_specs=P("tm", None, "net"), check_vma=False
    )
```

```python
import jax
import jax.numpy as jnp
from jax import lax
from jax.experimental import pallas as pl
from jax.experimental.pallas import tpu as pltpu
from jax.sharding import PartitionSpec as P

FACTOR = 8
KINDS = 9
LANES = 128
TILES = 16
WINDOWS = 64
PACKED = 24
RIGHT = 16
LEFT = 23
EDGE_ROWS = 136
STRIDE = 264
PADDED = FACTOR * STRIDE
ROWS_OF = list(range(TILES)) + [RIGHT, LEFT]
LISTED = len(ROWS_OF)
PREV = [LISTED - 1] + list(range(TILES)) + [LISTED - 1]
NEXT = list(range(1, TILES + 1)) + [TILES, 0]
SLAB = 32
REACH = 22
SPAN = 84
COMB = 48
GROUPS = 2 * COMB // 8
PAIR = 2


def lanes_of(shape):
    return lax.broadcasted_iota(jnp.int32, shape, len(shape) - 1)


def couple(p, q, p_low, p_high, q_low, q_high, w):
    mixed_p = (p + p) + (q_high - q_low)
    mixed_q = (q + q) + (p_low - p_high)
    return w[0] * mixed_p + w[1] * mixed_q, w[2] * mixed_p + w[3] * mixed_q


def apply2(p, q, w):
    return w[0] * p + w[1] * q, w[2] * p + w[3] * q


def phi_tiles(ps, qs, weight_of):
    lane = lanes_of((8, LANES))
    first, last = lane == 0, lane == LANES - 1

    def low(xs, t):
        return pltpu.roll(jnp.where(last, xs[PREV[t]], xs[t]), 1, 1)

    def high(xs, t):
        return pltpu.roll(jnp.where(first, xs[NEXT[t]], xs[t]), LANES - 1, 1)

    new_p, new_q = [], []
    for t in range(LISTED):
        p, q = couple(ps[t], qs[t], low(ps, t), high(ps, t), low(qs, t), high(qs, t), weight_of(t))
        new_p.append(p)
        new_q.append(q)
    return new_p, new_q


def phi_packed(p, q, w):
    lane = lanes_of((PACKED, LANES))
    first, last = lane == 0, lane == LANES - 1

    def low(x):
        return pltpu.roll(jnp.where(last, pltpu.roll(x, 1, 0), x), 1, 1)

    def high(x):
        return pltpu.roll(jnp.where(first, pltpu.roll(x, PACKED - 1, 0), x), LANES - 1, 1)

    return couple(p, q, low(p), high(p), low(q), high(q), w)


def phi_slab(p, q, w):
    return couple(
        p, q, pltpu.roll(p, 1, 1), pltpu.roll(p, LANES - 1, 1), pltpu.roll(q, 1, 1), pltpu.roll(q, LANES - 1, 1), w
    )


def pick(blocks_ref, number, kind):
    scale = 1.0 if number == 2 else 0.25
    masks = [kind == float(k + 1) for k in range(KINDS)]
    picked = []
    for entry in range(4):
        chosen = jnp.zeros_like(kind)
        for k in range(KINDS):
            chosen = jnp.where(masks[k], blocks_ref[(number * 4 + entry) * KINDS + k] * scale, chosen)
        picked.append(chosen)
    return picked


def load_forcing(f_ref, right_ref, left_ref, j, t, field):
    if t < TILES:
        return f_ref[pl.ds(j * 32 + t * 2 + field, 8, stride=STRIDE), :]
    edge = right_ref if t == TILES else left_ref
    return edge[pl.ds((j * 2 + field) * 8, 8), :]


def tile_rows(t):
    return pl.ds(ROWS_OF[t] * 8, 8)


def fine_weights(w_ref):
    def weight_of(t):
        return [jnp.broadcast_to(w_ref[e, ROWS_OF[t] : ROWS_OF[t] + 1, :], (8, LANES)) for e in range(4)]

    return weight_of


def edge_kernel(source_ref, fc_hbm, comp_hbm, f_ref, low_ref, high_ref, kind_ref, fc_ref, comp_ref, sems):
    copies = [
        pltpu.make_async_copy(source_ref.at[pl.ds(k * 256, 256)], f_ref.at[pl.ds(k * STRIDE, 256)], sems.at[k])
        for k in range(FACTOR)
    ]
    labels = [
        pltpu.make_async_copy(fc_hbm, fc_ref, sems.at[FACTOR]),
        pltpu.make_async_copy(comp_hbm, comp_ref, sems.at[FACTOR + 1]),
    ]
    for copy in labels + copies:
        copy.start()
    for copy in labels:
        copy.wait()
    kinds = jnp.where(comp_ref[...] == 1, KINDS, fc_ref[...] + 1).astype(jnp.float32)
    kind_ref[...] = kinds
    low_ref[128:EDGE_ROWS, :] = jnp.broadcast_to(kinds[0:1], (8, LANES))
    high_ref[128:EDGE_ROWS, :] = jnp.broadcast_to(kinds[TILES - 1 : TILES], (8, LANES))
    for copy in copies:
        copy.wait()
    for j in range(FACTOR):
        for field in range(2):
            rows = pl.ds((j * 2 + field) * 8, 8)
            low_ref[rows, :] = f_ref[pl.ds(j * 32 + field, 8, stride=STRIDE), :]
            high_ref[rows, :] = f_ref[pl.ds(j * 32 + 2 * (TILES - 1) + field, 8, stride=STRIDE), :]


def first_kernel(blocks_ref, f_ref, right_ref, left_ref, kind_ref, r1_ref, r2_ref, w_ref, kx_ref, send_ref,
                 prev_ref, c_ref, r1b_ref):
    kx_ref[0:TILES, :] = kind_ref[...]
    kx_ref[TILES:PACKED, :] = jnp.zeros((PACKED - TILES, LANES), jnp.float32)
    kx_ref[RIGHT : RIGHT + 1, :] = right_ref[128:129, :]
    kx_ref[LEFT : LEFT + 1, :] = left_ref[128:129, :]
    kind = kx_ref[...]
    for number in range(3):
        for entry, chosen in enumerate(pick(blocks_ref, number, kind)):
            w_ref[number * 4 + entry] = chosen
    weight_of = fine_weights(w_ref)
    w1 = [w_ref[4 + e] for e in range(4)]

    def forcing(j, field):
        return [load_forcing(f_ref, right_ref, left_ref, j, t, field) for t in range(LISTED)]

    unused = jnp.zeros(((LEFT - RIGHT - 1) * 8, LANES), jnp.float32)
    for field in range(2):
        for ref in (r1_ref, r1b_ref):
            ref[field, (RIGHT + 1) * 8 : LEFT * 8, :] = unused

    ps, qs = forcing(0, 0), forcing(0, 1)
    for j in range(1, FACTOR):
        ps, qs = phi_tiles(ps, qs, weight_of)
        fp, fq = forcing(j, 0), forcing(j, 1)
        ps = [a + b for a, b in zip(ps, fp)]
        qs = [a + b for a, b in zip(qs, fq)]
    for t in range(LISTED):
        r1_ref[0, tile_rows(t), :] = ps[t]
        r1_ref[1, tile_rows(t), :] = qs[t]

    def sweep(ref, keep):
        p = q = None
        for k in range(FACTOR):
            rp, rq = ref[0, pl.ds(k, PACKED, stride=8), :], ref[1, pl.ds(k, PACKED, stride=8), :]
            if k == 0:
                p, q = rp, rq
            else:
                p, q = phi_packed(p, q, w1)
                p, q = p + rp, q + rq
            if keep:
                c_ref[0, pl.ds(k, PACKED, stride=8), :] = p
                c_ref[1, pl.ds(k, PACKED, stride=8), :] = q
                if k < FACTOR - 1:
                    prev_ref[0, pl.ds(k + 1, PACKED, stride=8), :] = p
                    prev_ref[1, pl.ds(k + 1, PACKED, stride=8), :] = q
        return p, q

    nothing = jnp.zeros((PACKED, LANES), jnp.float32)
    prev_ref[0, pl.ds(0, PACKED, stride=8), :] = nothing
    prev_ref[1, pl.ds(0, PACKED, stride=8), :] = nothing
    r2p, r2q = sweep(r1_ref, True)
    r2_ref[0] = r2p
    r2_ref[1] = r2q

    ps = [prev_ref[0, tile_rows(t), :] for t in range(LISTED)]
    qs = [prev_ref[1, tile_rows(t), :] for t in range(LISTED)]
    for j in range(FACTOR):
        ps, qs = phi_tiles(ps, qs, weight_of)
    for field, xs in enumerate((ps, qs)):
        for t in range(LISTED):
            rows = tile_rows(t)
            r1b_ref[field, rows, :] = xs[t] + (r1_ref[field, rows, :] - c_ref[field, rows, :])
    gp, gq = sweep(r1b_ref, False)

    lane = lanes_of((8, LANES))
    for c, (x, g) in enumerate(((r2p, gp), (r2q, gq))):
        for half in range(2):
            shifted = [
                [y[8 * half : 8 * half + 8] for y in (pltpu.roll(z, 1, 0), z, pltpu.roll(z, PACKED - 1, 0))]
                for z in (x, g)
            ]

            def window(which, offset):
                a, b = shifted[which][0:2] if offset < 0 else shifted[which][1:3]
                start = offset % LANES
                return pltpu.roll(jnp.where(lane >= start, a, b), (LANES - start) % LANES, 1)

            for quarter in range(4):
                origin = SLAB * quarter
                near = window(0, origin + window_start(half))
                far = window(1, origin + share_start(half) - SPAN)
                send_ref[pl.ds(64 * half + 2 * quarter + c, 8, stride=8), :] = jnp.where(lane < SPAN, near, far)


def window_start(half):
    return -REACH if half else -REACH - 8


def share_start(half):
    return 0 if half else -8


def prepare_kernel(place_ref, blocks_ref, kx_ref, scan_ref, dense_ref, prev_ref, m_ref):
    place = place_ref[0]
    lane1 = lanes_of((1, LANES))
    origin = place * SLAB + (LANES - REACH - 8) + jnp.where(place >= WINDOWS // 2, 8, 0)
    base = origin // LANES - 1
    start = origin % LANES
    base = jnp.where(base < 0, LEFT, base)
    after = jnp.where(base == LEFT, 0, base + 1)
    a, b = kx_ref[pl.ds(base, 1), :], kx_ref[pl.ds(after, 1), :]
    kind = pltpu.roll(jnp.where(lane1 >= start, a, b), LANES - start, 1)
    kind = jnp.broadcast_to(kind, (8, LANES))
    w0, w1, w2 = (pick(blocks_ref, number, kind) for number in range(3))
    sub = lax.broadcasted_iota(jnp.int32, (8, LANES), 0)
    lane = lanes_of((8, LANES))

    def times(v, w):
        return [
            v[0] * w[0] + v[1] * w[2],
            v[0] * w[1] + v[1] * w[3],
            v[2] * w[0] + v[3] * w[2],
            v[2] * w[1] + v[3] * w[3],
        ]

    one, none = jnp.ones((8, LANES), jnp.float32), jnp.zeros((8, LANES), jnp.float32)
    w = w2
    grown = [one, none, none, one]
    for n, step in enumerate((1, 2, 4)):
        longer = times(grown, w)
        grown = [jnp.where((sub & step) != 0, x, y) for x, y in zip(longer, grown)]
        for e in range(4):
            scan_ref[4 * n + e] = jnp.where(sub >= step, w[e], 0.0)
        w = times(w, w)
    for e in range(4):
        scan_ref[12 + e] = w[e]
        scan_ref[16 + e] = grown[e]

    combs = []
    for n in range(COMB // 8):
        at = sub + 8 * n
        combs.append(jnp.where((lane == at) | (lane == at + COMB), 1.0, 0.0))
    start_p = combs + [none] * (COMB // 8)
    start_q = [none] * (COMB // 8) + combs
    for n in range(GROUPS):
        prev_ref[0, n] = start_p[n]
        prev_ref[1, n] = start_q[n]
        m_ref[0, n] = none
        m_ref[1, n] = none

    def block(k, carry):
        ps, qs, after_p, after_q = [], [], [], []
        for n in range(GROUPS):
            p, q = prev_ref[0, n], prev_ref[1, n]
            for _ in range(PAIR):
                ps.append(p)
                qs.append(q)
                p, q = phi_slab(p, q, w1)
                after_p.append(p)
                after_q.append(q)
            prev_ref[0, n] = p
            prev_ref[1, n] = q
        for _ in range(FACTOR):
            both = [phi_slab(p, q, w0) for p, q in zip(ps, qs)]
            ps, qs = [x[0] for x in both], [x[1] for x in both]
        for n in range(GROUPS):
            p, q = m_ref[0, n], m_ref[1, n]
            for e in range(PAIR * n, PAIR * n + PAIR):
                p, q = phi_slab(p, q, w1)
                p, q = p + (ps[e] - after_p[e]), q + (qs[e] - after_q[e])
            m_ref[0, n] = p
            m_ref[1, n] = q
        return carry

    lax.fori_loop(0, FACTOR // PAIR, block, 0)

    for n in range(GROUPS):
        field, c = divmod(n, COMB // 8)
        cp, cq = apply2(start_p[n], start_q[n], w2)
        answers = m_ref[0, n] + (prev_ref[0, n] - cp), m_ref[1, n] + (prev_ref[1, n] - cq)
        for tooth in range(2):
            at = sub + (8 * c + COMB * tooth)
            near = (lane - at <= REACH) & (at - lane <= REACH)
            rows = pl.ds(field * LANES + COMB * tooth + 8 * c, 8)
            for to in range(2):
                dense_ref[rows, LANES * to : LANES * (to + 1)] = jnp.where(near, answers[to], 0.0)
    for field in range(2):
        dense_ref[field * LANES + 2 * COMB : (field + 1) * LANES, :] = jnp.zeros((LANES - 2 * COMB, 2 * LANES), jnp.float32)


def slab_kernel(scan_ref, dense_ref, got_ref, send_ref, d_ref):
    lane = lanes_of((8, LANES))
    masked = [[scan_ref[4 * n + e] for e in range(4)] for n in range(3)]
    w_eight = [scan_ref[12 + e] for e in range(4)]
    grown = [scan_ref[16 + e] for e in range(4)]
    first = lax.broadcasted_iota(jnp.int32, (8, LANES), 0) == 0

    def recurrence(rp, rq):
        yp, yq = list(rp), list(rq)
        for n, step in enumerate((1, 2, 4)):
            for b in range(8):
                sp, sq = apply2(pltpu.roll(yp[b], step, 0), pltpu.roll(yq[b], step, 0), masked[n])
                yp[b], yq[b] = yp[b] + sp, yq[b] + sq
        dp, dq = [], []
        tp = tq = None
        for b in range(8):
            bp, bq = pltpu.roll(yp[b], 1, 0), pltpu.roll(yq[b], 1, 0)
            bp, bq = jnp.where(first, 0.0, bp), jnp.where(first, 0.0, bq)
            ep, eq = yp[b][7:8], yq[b][7:8]
            ep, eq = jnp.broadcast_to(ep, (8, LANES)), jnp.broadcast_to(eq, (8, LANES))
            if b:
                sp, sq = apply2(tp, tq, grown)
                bp, bq = bp + sp, bq + sq
                sp, sq = apply2(tp, tq, w_eight)
                ep, eq = ep + sp, eq + sq
            tp, tq = ep, eq
            dp.append(bp)
            dq.append(bq)
        return dp, dq

    def rows(b, c):
        return pl.ds(b * 16 + c, 8, stride=2)

    gotten = [[got_ref[rows(b, c), :] for b in range(8)] for c in range(2)]
    dp, dq = recurrence(*gotten)
    for b in range(8):
        d_ref[8 * b : 8 * b + 8, 0:LANES] = dp[b]
        d_ref[8 * b : 8 * b + 8, LANES : 2 * LANES] = dq[b]
    answer = jnp.dot(d_ref[...], dense_ref[...], precision=lax.Precision.HIGHEST, preferred_element_type=jnp.float32)
    back = SPAN - REACH
    residual = [
        [
            answer[8 * b : 8 * b + 8, LANES * c : LANES * (c + 1)] + pltpu.roll(gotten[c][b], LANES - back, 1)
            for b in range(8)
        ]
        for c in range(2)
    ]
    ep, eq = recurrence(*residual)
    for b in range(8):
        send_ref[rows(b, 0), :] = jnp.where(lane < SPAN, dp[b], pltpu.roll(ep[b], back, 1))
        send_ref[rows(b, 1), :] = jnp.where(lane < SPAN, dq[b], pltpu.roll(eq[b], back, 1))


def last_kernel(f_ref, right_ref, left_ref, r1_ref, r2_ref, w_ref, got_ref, out_ref, prev_ref, c_ref, r1b_ref, d_ref,
                o_ref, sems):
    lane = lanes_of((8, LANES))
    lane1 = lanes_of((1, LANES))
    for c in range(2):
        for cycle in range(2):
            for half in range(2):
                begin = (SPAN - share_start(half)) if cycle else -window_start(half)
                whole = jnp.zeros((8, LANES), jnp.float32)
                for quarter in range(4):
                    piece = got_ref[pl.ds(64 * half + 2 * quarter + c, 8, stride=8), :]
                    piece = pltpu.roll(piece, (SLAB * quarter - begin) % LANES, 1)
                    mine = (lane >= SLAB * quarter) & (lane < SLAB * (quarter + 1))
                    whole = jnp.where(mine, piece, whole)
                d_ref[2 * cycle + c, 8 * half : 8 * half + 8, :] = whole
            d_ref[2 * cycle + c, TILES:PACKED, :] = jnp.zeros((PACKED - TILES, LANES), jnp.float32)
            width = 8 if cycle else 24
            begin = (SPAN - share_start(0)) if cycle else -window_start(0)
            low = pltpu.roll(got_ref[c : c + 1, :], LANES - begin, 1)
            d_ref[2 * cycle + c, LEFT : LEFT + 1, :] = jnp.where(lane1 >= LANES - width, low, 0.0)
            begin = (SPAN - share_start(1)) if cycle else -window_start(1)
            end = (WINDOWS - 1) * 2 + c
            high = pltpu.roll(got_ref[end : end + 1, :], LANES - begin - SLAB, 1)
            d_ref[2 * cycle + c, RIGHT : RIGHT + 1, :] = jnp.where(lane1 < width, high, 0.0)

    weight_of = fine_weights(w_ref)
    w1 = [w_ref[4 + e] for e in range(4)]
    w2 = [w_ref[8 + e] for e in range(4)]
    unused = jnp.zeros(((LEFT - RIGHT - 1) * 8, LANES), jnp.float32)
    for field in range(2):
        r1b_ref[field, (RIGHT + 1) * 8 : LEFT * 8, :] = unused

    p, q = d_ref[0], d_ref[1]
    last_p, last_q = apply2(p, q, w2)
    c_ref[0, pl.ds(FACTOR - 1, PACKED, stride=8), :] = last_p + r2_ref[0]
    c_ref[1, pl.ds(FACTOR - 1, PACKED, stride=8), :] = last_q + r2_ref[1]
    prev_ref[0, pl.ds(0, PACKED, stride=8), :] = p
    prev_ref[1, pl.ds(0, PACKED, stride=8), :] = q
    for k in range(FACTOR - 1):
        p, q = phi_packed(p, q, w1)
        p = p + r1_ref[0, pl.ds(k, PACKED, stride=8), :]
        q = q + r1_ref[1, pl.ds(k, PACKED, stride=8), :]
        c_ref[0, pl.ds(k, PACKED, stride=8), :] = p
        c_ref[1, pl.ds(k, PACKED, stride=8), :] = q
        prev_ref[0, pl.ds(k + 1, PACKED, stride=8), :] = p
        prev_ref[1, pl.ds(k + 1, PACKED, stride=8), :] = q

    ps = [prev_ref[0, tile_rows(t), :] for t in range(LISTED)]
    qs = [prev_ref[1, tile_rows(t), :] for t in range(LISTED)]
    for j in range(FACTOR):
        ps, qs = phi_tiles(ps, qs, weight_of)
        if j == FACTOR - 1:
            copies = [
                pltpu.make_async_copy(o_ref.at[pl.ds(k * STRIDE, 224)], out_ref.at[pl.ds(k * 256, 224)], sems.at[k])
                for k in range(FACTOR)
            ]
            for copy in copies:
                copy.start()
        for t in range(LISTED):
            ps[t] = ps[t] + load_forcing(f_ref, right_ref, left_ref, j, t, 0)
            qs[t] = qs[t] + load_forcing(f_ref, right_ref, left_ref, j, t, 1)
            if j < FACTOR - 1 and t < TILES:
                o_ref[pl.ds(j * 32 + t * 2, 8, stride=STRIDE), :] = ps[t]
                o_ref[pl.ds(j * 32 + t * 2 + 1, 8, stride=STRIDE), :] = qs[t]
    for t in range(LISTED):
        r1b_ref[0, tile_rows(t), :] = ps[t] - c_ref[0, tile_rows(t), :]
        r1b_ref[1, tile_rows(t), :] = qs[t] - c_ref[1, tile_rows(t), :]

    def finish(k, p, q):
        for field, x in enumerate((p, q)):
            done = c_ref[field, pl.ds(k, PACKED, stride=8), :] + x
            o_ref[pl.ds(k * STRIDE + 224 + field, TILES, stride=2), :] = done[0:TILES]
        copy = pltpu.make_async_copy(
            o_ref.at[pl.ds(k * STRIDE + 224, 32)], out_ref.at[pl.ds(k * 256 + 224, 32)], sems.at[FACTOR + k]
        )
        copy.start()
        copies.append(copy)

    p, q = d_ref[2], d_ref[3]
    last_p, last_q = apply2(p, q, w2)
    mp = mq = None
    for k in range(FACTOR):
        rp, rq = r1b_ref[0, pl.ds(k, PACKED, stride=8), :], r1b_ref[1, pl.ds(k, PACKED, stride=8), :]
        if k == 0:
            mp, mq = rp, rq
        else:
            mp, mq = phi_packed(mp, mq, w1)
            mp, mq = mp + rp, mq + rq
        if k < FACTOR - 1:
            p, q = phi_packed(p, q, w1)
            p, q = p + rp, q + rq
            finish(k, p, q)
    finish(FACTOR - 1, last_p + mp, last_q + mq)
    for copy in copies:
        copy.wait()


VMEM = pl.BlockSpec(memory_space=pltpu.VMEM)
SMEM = pl.BlockSpec(memory_space=pltpu.SMEM)
STATE = (2, PACKED * 8, LANES)


def shaped(*shape):
    return jax.ShapeDtypeStruct(shape, jnp.float32)


def scratch(*shape):
    return pltpu.VMEM(shape, jnp.float32)


ANY = pl.BlockSpec(memory_space=pl.ANY)
HBM = pl.BlockSpec(memory_space=pltpu.HBM)
SMALL = pltpu.CompilerParams(vmem_limit_bytes=8 << 20)


def edge_stage(flat, friction, compressor):
    return pl.pallas_call(
        edge_kernel,
        out_shape=(shaped(PADDED, LANES), shaped(EDGE_ROWS, LANES), shaped(EDGE_ROWS, LANES), shaped(TILES, LANES)),
        in_specs=[HBM] * 3,
        out_specs=(VMEM,) * 4,
        scratch_shapes=[pltpu.VMEM((TILES, LANES), jnp.int32)] * 2 + [pltpu.SemaphoreType.DMA((FACTOR + 2,))],
        compiler_params=SMALL,
        name="edge",
    )(flat, friction, compressor)


def first_stage(flat_blocks, padded, right, left, kinds):
    return pl.pallas_call(
        first_kernel,
        out_shape=(shaped(*STATE), shaped(2, PACKED, LANES), shaped(12, PACKED, LANES), shaped(PACKED, LANES), shaped(2 * WINDOWS, LANES)),
        in_specs=[SMEM] + [VMEM] * 4,
        out_specs=(VMEM,) * 5,
        scratch_shapes=[scratch(*STATE)] * 3,
        compiler_params=SMALL,
        name="first",
    )(flat_blocks, padded, right, left, kinds)


def prepare_stage(place, flat_blocks, kinds):
    return pl.pallas_call(
        prepare_kernel,
        out_shape=(shaped(20, 8, LANES), shaped(2 * LANES, 2 * LANES)),
        in_specs=[SMEM, SMEM, VMEM],
        out_specs=(VMEM, VMEM),
        scratch_shapes=[scratch(2, GROUPS, 8, LANES)] * 2,
        compiler_params=SMALL,
        name="prepare",
    )(place, flat_blocks, kinds)


def slab_stage(scan, dense, got):
    return pl.pallas_call(
        slab_kernel,
        out_shape=shaped(2 * WINDOWS, LANES),
        in_specs=[VMEM] * 3,
        out_specs=VMEM,
        scratch_shapes=[scratch(WINDOWS, 2 * LANES)],
        compiler_params=SMALL,
        name="slab",
    )(scan, dense, got)


def last_stage(padded, right, left, r1, r2, weights, got):
    return pl.pallas_call(
        last_kernel,
        out_shape=shaped(2048, LANES),
        in_specs=[VMEM] * 7,
        out_specs=ANY,
        scratch_shapes=[scratch(*STATE)] * 3
        + [scratch(4, PACKED, LANES), scratch(PADDED, LANES), pltpu.SemaphoreType.DMA((2 * FACTOR,))],
        compiler_params=SMALL,
        name="last",
    )(padded, right, left, r1, r2, weights, got)


def to_rows(forcing):
    return forcing.reshape(64, 2, TILES, LANES).transpose(0, 2, 1, 3).reshape(2048, LANES)


def from_rows(rows):
    return rows.reshape(64, TILES, 2, LANES).transpose(0, 2, 1, 3).reshape(64, 2, TILES * LANES)


def transpose_windows(rows):
    return lax.all_to_all(rows.reshape(WINDOWS, 2, LANES), "tm", 0, 0).reshape(2 * WINDOWS, LANES)


def per_device(forcing, friction_class, compressor, blocks):
    flat = to_rows(forcing)
    flat_blocks = blocks.reshape(-1)
    friction = friction_class.reshape(TILES, LANES)
    station = compressor.reshape(TILES, LANES)
    count = lax.axis_size("net")
    flat, friction, station = (pltpu.with_memory_space_constraint(x, pltpu.HBM) for x in (flat, friction, station))
    padded, low, high, kinds = edge_stage(flat, friction, station)
    left = lax.ppermute(high, "net", [(i, i + 1) for i in range(count - 1)])
    right = lax.ppermute(low, "net", [(i + 1, i) for i in range(count - 1)])
    r1, r2, weights, kinds_wide, send = first_stage(flat_blocks, padded, right, left, kinds)
    got = transpose_windows(send)
    place = lax.axis_index("tm").astype(jnp.int32).reshape(1)
    scan, dense = prepare_stage(place, flat_blocks, kinds_wide)
    got = transpose_windows(slab_stage(scan, dense, got))
    return from_rows(last_stage(padded, right, left, r1, r2, weights, got))


def solution(mesh):
    placed = (P("tm", None, "net"), P("net"), P("net"), P())
    return jax.shard_map(
        per_device, mesh=mesh, in_specs=placed, out_specs=P("tm", None, "net"), check_vma=False
    )
```

```python
import jax
import jax.numpy as jnp
from jax import lax
from jax.experimental import pallas as pl
from jax.experimental.pallas import tpu as pltpu
from jax.sharding import PartitionSpec as P

FACTOR = 8
KINDS = 9
LANES = 128
TILES = 16
WINDOWS = 64
PACKED = 24
RIGHT = 16
LEFT = 23
EDGE_ROWS = 72
STRIDE = 264
PADDED = FACTOR * STRIDE
HALF = LANES // 2
LISTED = TILES + 1
PREV = [TILES] + list(range(TILES))
NEXT = list(range(1, TILES + 1)) + [0]
SLAB = 32
REACH = 22
SPAN = 84
COMB = 48
GROUPS = 2 * COMB // 8
TEETH = 24


def lanes_of(shape):
    return lax.broadcasted_iota(jnp.int32, shape, len(shape) - 1)


def couple(p, q, p_low, p_high, q_low, q_high, w):
    mixed_p = (p + p) + (q_high - q_low)
    mixed_q = (q + q) + (p_low - p_high)
    return w[0] * mixed_p + w[1] * mixed_q, w[2] * mixed_p + w[3] * mixed_q


def apply2(p, q, w):
    return w[0] * p + w[1] * q, w[2] * p + w[3] * q


def phi_tiles(ps, qs, weight_of):
    lane = lanes_of((8, LANES))
    first, last = lane == 0, lane == LANES - 1

    def low(xs, t):
        return pltpu.roll(jnp.where(last, xs[PREV[t]], xs[t]), 1, 1)

    def high(xs, t):
        return pltpu.roll(jnp.where(first, xs[NEXT[t]], xs[t]), LANES - 1, 1)

    new_p, new_q = [], []
    for t in range(LISTED):
        p, q = couple(ps[t], qs[t], low(ps, t), high(ps, t), low(qs, t), high(qs, t), weight_of(t))
        new_p.append(p)
        new_q.append(q)
    return new_p, new_q


def phi_packed(p, q, w):
    lane = lanes_of((PACKED, LANES))
    first, last = lane == 0, lane == LANES - 1

    def low(x):
        return pltpu.roll(jnp.where(last, pltpu.roll(x, 1, 0), x), 1, 1)

    def high(x):
        return pltpu.roll(jnp.where(first, pltpu.roll(x, PACKED - 1, 0), x), LANES - 1, 1)

    return couple(p, q, low(p), high(p), low(q), high(q), w)


def phi_slab(p, q, w):
    return couple(
        p, q, pltpu.roll(p, 1, 1), pltpu.roll(p, LANES - 1, 1), pltpu.roll(q, 1, 1), pltpu.roll(q, LANES - 1, 1), w
    )


def pick(blocks_ref, number, kind):
    scale = 1.0 if number == 2 else 0.25
    masks = [kind == float(k + 1) for k in range(KINDS)]
    picked = []
    for entry in range(4):
        chosen = jnp.zeros_like(kind)
        for k in range(KINDS):
            chosen = jnp.where(masks[k], blocks_ref[(number * 4 + entry) * KINDS + k] * scale, chosen)
        picked.append(chosen)
    return picked


def load_forcing(f_ref, halo_ref, j, t, field):
    if t < TILES:
        return f_ref[pl.ds(j * 32 + t * 2 + field, 8, stride=STRIDE), :]
    return halo_ref[pl.ds((j * 2 + field) * 8, 8), :]


def tile_rows(row):
    return pl.ds(row * 8, 8)


def tiles_from(ref, field):
    both = jnp.where(lanes_of((8, LANES)) < HALF, ref[field, tile_rows(RIGHT), :], ref[field, tile_rows(LEFT), :])
    return [ref[field, tile_rows(t), :] for t in range(TILES)] + [both]


def spots():
    return [(t, t) for t in range(TILES)] + [(TILES, RIGHT), (TILES, LEFT)]


def fine_weights(w_ref):
    def weight_of(t):
        return [jnp.broadcast_to(w_ref[e, t : t + 1, :], (8, LANES)) for e in range(4)]

    return weight_of


def edge_kernel(source_ref, fc_hbm, comp_hbm, f_ref, low_ref, high_ref, kind_ref, fc_ref, comp_ref, sems):
    copies = [
        pltpu.make_async_copy(source_ref.at[pl.ds(k * 256, 256)], f_ref.at[pl.ds(k * STRIDE, 256)], sems.at[k])
        for k in range(FACTOR)
    ]
    labels = [
        pltpu.make_async_copy(fc_hbm, fc_ref, sems.at[FACTOR]),
        pltpu.make_async_copy(comp_hbm, comp_ref, sems.at[FACTOR + 1]),
    ]
    for copy in labels + copies:
        copy.start()
    for copy in labels:
        copy.wait()
    kinds = jnp.where(comp_ref[...] == 1, KINDS, fc_ref[...] + 1).astype(jnp.float32)
    kind_ref[...] = kinds
    low_ref[64:EDGE_ROWS, :] = jnp.broadcast_to(kinds[0:1], (8, LANES))
    high_ref[64:EDGE_ROWS, :] = jnp.broadcast_to(kinds[TILES - 1 : TILES], (8, LANES))
    left_half = lanes_of((8, LANES)) < HALF
    for copy in copies:
        copy.wait()
    for j in range(FACTOR):
        rows = pl.ds(j * 8, 8)
        p, q = (f_ref[pl.ds(j * 32 + field, 8, stride=STRIDE), :] for field in range(2))
        low_ref[rows, :] = jnp.where(left_half, p, pltpu.roll(q, HALF, 1))
        p, q = (f_ref[pl.ds(j * 32 + 2 * (TILES - 1) + field, 8, stride=STRIDE), :] for field in range(2))
        high_ref[rows, :] = jnp.where(left_half, pltpu.roll(q, HALF, 1), p)


def first_kernel(blocks_ref, f_ref, right_ref, left_ref, kind_ref, r1_ref, r2_ref, w_ref, kx_ref, send_ref,
                 halo_ref, prev_ref, c_ref, r1b_ref):
    kx_ref[0:TILES, :] = kind_ref[...]
    kx_ref[TILES:PACKED, :] = jnp.zeros((PACKED - TILES, LANES), jnp.float32)
    beyond = jnp.where(lanes_of((1, LANES)) < HALF, right_ref[64:65, :], left_ref[64:65, :])
    kx_ref[RIGHT : RIGHT + 1, :] = beyond
    kx_ref[LEFT : LEFT + 1, :] = beyond
    kind = kx_ref[...]
    for number in range(3):
        for entry, chosen in enumerate(pick(blocks_ref, number, kind)):
            w_ref[number * 4 + entry] = chosen
    weight_of = fine_weights(w_ref)
    w1 = [w_ref[4 + e] for e in range(4)]

    left_half = lanes_of((8, LANES)) < HALF
    for j in range(FACTOR):
        x, y = right_ref[pl.ds(j * 8, 8), :], left_ref[pl.ds(j * 8, 8), :]
        halo_ref[pl.ds(j * 16, 8), :] = jnp.where(left_half, x, y)
        halo_ref[pl.ds(j * 16 + 8, 8), :] = pltpu.roll(jnp.where(left_half, y, x), HALF, 1)

    def forcing(j, field):
        return [load_forcing(f_ref, halo_ref, j, t, field) for t in range(LISTED)]

    unused = jnp.zeros(((LEFT - RIGHT - 1) * 8, LANES), jnp.float32)
    for field in range(2):
        for ref in (r1_ref, r1b_ref):
            ref[field, (RIGHT + 1) * 8 : LEFT * 8, :] = unused

    ps, qs = forcing(0, 0), forcing(0, 1)
    for j in range(1, FACTOR):
        ps, qs = phi_tiles(ps, qs, weight_of)
        fp, fq = forcing(j, 0), forcing(j, 1)
        ps = [a + b for a, b in zip(ps, fp)]
        qs = [a + b for a, b in zip(qs, fq)]
    for t, row in spots():
        r1_ref[0, tile_rows(row), :] = ps[t]
        r1_ref[1, tile_rows(row), :] = qs[t]

    def sweep(ref, keep):
        p = q = None
        for k in range(FACTOR):
            rp, rq = ref[0, pl.ds(k, PACKED, stride=8), :], ref[1, pl.ds(k, PACKED, stride=8), :]
            if k == 0:
                p, q = rp, rq
            else:
                p, q = phi_packed(p, q, w1)
                p, q = p + rp, q + rq
            if keep:
                c_ref[0, pl.ds(k, PACKED, stride=8), :] = p
                c_ref[1, pl.ds(k, PACKED, stride=8), :] = q
                if k < FACTOR - 1:
                    prev_ref[0, pl.ds(k + 1, PACKED, stride=8), :] = p
                    prev_ref[1, pl.ds(k + 1, PACKED, stride=8), :] = q
        return p, q

    nothing = jnp.zeros((PACKED, LANES), jnp.float32)
    prev_ref[0, pl.ds(0, PACKED, stride=8), :] = nothing
    prev_ref[1, pl.ds(0, PACKED, stride=8), :] = nothing
    r2p, r2q = sweep(r1_ref, True)
    r2_ref[0] = r2p
    r2_ref[1] = r2q

    ps, qs = tiles_from(prev_ref, 0), tiles_from(prev_ref, 1)
    for j in range(FACTOR):
        ps, qs = phi_tiles(ps, qs, weight_of)
    for field, xs in enumerate((ps, qs)):
        for t, row in spots():
            rows = tile_rows(row)
            r1b_ref[field, rows, :] = xs[t] + (r1_ref[field, rows, :] - c_ref[field, rows, :])
    gp, gq = sweep(r1b_ref, False)

    lane = lanes_of((8, LANES))
    for c, (x, g) in enumerate(((r2p, gp), (r2q, gq))):
        for half in range(2):
            shifted = [
                [y[8 * half : 8 * half + 8] for y in (pltpu.roll(z, 1, 0), z, pltpu.roll(z, PACKED - 1, 0))]
                for z in (x, g)
            ]

            def window(which, offset):
                a, b = shifted[which][0:2] if offset < 0 else shifted[which][1:3]
                start = offset % LANES
                return pltpu.roll(jnp.where(lane >= start, a, b), (LANES - start) % LANES, 1)

            for quarter in range(4):
                origin = SLAB * quarter
                near = window(0, origin + window_start(half))
                far = window(1, origin + share_start(half) - SPAN)
                send_ref[pl.ds(64 * half + 2 * quarter + c, 8, stride=8), :] = jnp.where(lane < SPAN, near, far)


def window_start(half):
    return -REACH if half else -REACH - 8


def share_start(half):
    return 0 if half else -8


def prepare_kernel(place_ref, blocks_ref, kx_ref, scan_ref, dense_ref, fine_ref, states_ref, after_ref):
    place = place_ref[0]
    lane1 = lanes_of((1, LANES))
    origin = place * SLAB + (LANES - REACH - 8) + jnp.where(place >= WINDOWS // 2, 8, 0)
    base = origin // LANES - 1
    start = origin % LANES
    base = jnp.where(base < 0, LEFT, base)
    after = jnp.where(base == LEFT, 0, base + 1)
    a, b = kx_ref[pl.ds(base, 1), :], kx_ref[pl.ds(after, 1), :]
    kind = pltpu.roll(jnp.where(lane1 >= start, a, b), LANES - start, 1)
    kind = jnp.broadcast_to(kind, (8, LANES))
    w0, w1, w2 = (pick(blocks_ref, number, kind) for number in range(3))
    sub = lax.broadcasted_iota(jnp.int32, (8, LANES), 0)
    lane = lanes_of((8, LANES))

    def times(v, w):
        return [
            v[0] * w[0] + v[1] * w[2],
            v[0] * w[1] + v[1] * w[3],
            v[2] * w[0] + v[3] * w[2],
            v[2] * w[1] + v[3] * w[3],
        ]

    one, none = jnp.ones((8, LANES), jnp.float32), jnp.zeros((8, LANES), jnp.float32)
    w = w2
    grown = [one, none, none, one]
    for n, step in enumerate((1, 2, 4)):
        longer = times(grown, w)
        grown = [jnp.where((sub & step) != 0, x, y) for x, y in zip(longer, grown)]
        for e in range(4):
            scan_ref[4 * n + e] = jnp.where(sub >= step, w[e], 0.0)
        w = times(w, w)
    for e in range(4):
        scan_ref[12 + e] = w[e]
        scan_ref[16 + e] = grown[e]

    def combs(gap, teeth):
        made = []
        for n in range(gap // 8):
            hit = lane == sub + 8 * n
            for tooth in range(1, teeth):
                hit = hit | (lane == sub + (8 * n + gap * tooth))
            made.append(jnp.where(hit, 1.0, 0.0))
        blank = [none] * len(made)
        return made + blank, blank + made

    def spread(answers, ref, gap, teeth, reach):
        for n, answer in enumerate(answers):
            field, c = divmod(n, gap // 8)
            for tooth in range(teeth):
                at = sub + (8 * c + gap * tooth)
                near = (lane - at <= reach) & (at - lane <= reach)
                rows = pl.ds(field * LANES + gap * tooth + 8 * c, 8)
                for to in range(2):
                    ref[rows, LANES * to : LANES * (to + 1)] = jnp.where(near, answer[to], 0.0)
        for field in range(2):
            ref[field * LANES + gap * teeth : (field + 1) * LANES, :] = jnp.zeros((LANES - gap * teeth, 2 * LANES), jnp.float32)

    answers = list(zip(*combs(TEETH, 4)))
    for _ in range(FACTOR):
        answers = [phi_slab(p, q, w0) for p, q in answers]
    spread(answers, fine_ref, TEETH, 4, FACTOR)

    def rows_of(k, n):
        return pl.ds((k * GROUPS + n) * 8, 8)

    begin = list(zip(*combs(COMB, 2)))
    states = begin
    for k in range(FACTOR + 1):
        for n, (p, q) in enumerate(states):
            states_ref[rows_of(k, n), 0:LANES] = p
            states_ref[rows_of(k, n), LANES : 2 * LANES] = q
        if k < FACTOR:
            states = [phi_slab(p, q, w1) for p, q in states]
    after_ref[...] = jnp.dot(
        states_ref[0 : FACTOR * GROUPS * 8, :],
        fine_ref[...],
        precision=lax.Precision.HIGHEST,
        preferred_element_type=jnp.float32,
    )

    def residual(k, n):
        return [
            after_ref[rows_of(k, n), LANES * to : LANES * (to + 1)]
            - states_ref[rows_of(k + 1, n), LANES * to : LANES * (to + 1)]
            for to in range(2)
        ]

    m = [residual(0, n) for n in range(GROUPS)]
    for k in range(1, FACTOR):
        stepped = [phi_slab(p, q, w1) for p, q in m]
        m = [[x + y for x, y in zip(stepped[n], residual(k, n))] for n in range(GROUPS)]

    total = []
    for n in range(GROUPS):
        coarse = apply2(*begin[n], w2)
        total.append([m[n][to] + (states[n][to] - coarse[to]) for to in range(2)])
    spread(total, dense_ref, COMB, 2, REACH)


def slab_kernel(scan_ref, dense_ref, got_ref, send_ref, d_ref):
    lane = lanes_of((8, LANES))
    masked = [[scan_ref[4 * n + e] for e in range(4)] for n in range(3)]
    w_eight = [scan_ref[12 + e] for e in range(4)]
    grown = [scan_ref[16 + e] for e in range(4)]
    first = lax.broadcasted_iota(jnp.int32, (8, LANES), 0) == 0

    def recurrence(rp, rq):
        yp, yq = list(rp), list(rq)
        for n, step in enumerate((1, 2, 4)):
            for b in range(8):
                sp, sq = apply2(pltpu.roll(yp[b], step, 0), pltpu.roll(yq[b], step, 0), masked[n])
                yp[b], yq[b] = yp[b] + sp, yq[b] + sq
        dp, dq = [], []
        tp = tq = None
        for b in range(8):
            bp, bq = pltpu.roll(yp[b], 1, 0), pltpu.roll(yq[b], 1, 0)
            bp, bq = jnp.where(first, 0.0, bp), jnp.where(first, 0.0, bq)
            ep, eq = yp[b][7:8], yq[b][7:8]
            ep, eq = jnp.broadcast_to(ep, (8, LANES)), jnp.broadcast_to(eq, (8, LANES))
            if b:
                sp, sq = apply2(tp, tq, grown)
                bp, bq = bp + sp, bq + sq
                sp, sq = apply2(tp, tq, w_eight)
                ep, eq = ep + sp, eq + sq
            tp, tq = ep, eq
            dp.append(bp)
            dq.append(bq)
        return dp, dq

    def rows(b, c):
        return pl.ds(b * 16 + c, 8, stride=2)

    gotten = [[got_ref[rows(b, c), :] for b in range(8)] for c in range(2)]
    dp, dq = recurrence(*gotten)
    for b in range(8):
        d_ref[8 * b : 8 * b + 8, 0:LANES] = dp[b]
        d_ref[8 * b : 8 * b + 8, LANES : 2 * LANES] = dq[b]
    answer = jnp.dot(d_ref[...], dense_ref[...], precision=lax.Precision.HIGHEST, preferred_element_type=jnp.float32)
    back = SPAN - REACH
    residual = [
        [
            answer[8 * b : 8 * b + 8, LANES * c : LANES * (c + 1)] + pltpu.roll(gotten[c][b], LANES - back, 1)
            for b in range(8)
        ]
        for c in range(2)
    ]
    ep, eq = recurrence(*residual)
    for b in range(8):
        send_ref[rows(b, 0), :] = jnp.where(lane < SPAN, dp[b], pltpu.roll(ep[b], back, 1))
        send_ref[rows(b, 1), :] = jnp.where(lane < SPAN, dq[b], pltpu.roll(eq[b], back, 1))


def last_kernel(f_ref, halo_ref, r1_ref, r2_ref, w_ref, got_ref, out_ref, prev_ref, c_ref, r1b_ref, d_ref,
                o_ref, sems):
    lane = lanes_of((8, LANES))
    lane1 = lanes_of((1, LANES))
    for c in range(2):
        for cycle in range(2):
            for half in range(2):
                begin = (SPAN - share_start(half)) if cycle else -window_start(half)
                whole = jnp.zeros((8, LANES), jnp.float32)
                for quarter in range(4):
                    piece = got_ref[pl.ds(64 * half + 2 * quarter + c, 8, stride=8), :]
                    piece = pltpu.roll(piece, (SLAB * quarter - begin) % LANES, 1)
                    mine = (lane >= SLAB * quarter) & (lane < SLAB * (quarter + 1))
                    whole = jnp.where(mine, piece, whole)
                d_ref[2 * cycle + c, 8 * half : 8 * half + 8, :] = whole
            d_ref[2 * cycle + c, TILES:PACKED, :] = jnp.zeros((PACKED - TILES, LANES), jnp.float32)
            width = 8 if cycle else 24
            begin = (SPAN - share_start(0)) if cycle else -window_start(0)
            low = pltpu.roll(got_ref[c : c + 1, :], LANES - begin, 1)
            d_ref[2 * cycle + c, LEFT : LEFT + 1, :] = jnp.where(lane1 >= LANES - width, low, 0.0)
            begin = (SPAN - share_start(1)) if cycle else -window_start(1)
            end = (WINDOWS - 1) * 2 + c
            high = pltpu.roll(got_ref[end : end + 1, :], LANES - begin - SLAB, 1)
            d_ref[2 * cycle + c, RIGHT : RIGHT + 1, :] = jnp.where(lane1 < width, high, 0.0)

    weight_of = fine_weights(w_ref)
    w1 = [w_ref[4 + e] for e in range(4)]
    w2 = [w_ref[8 + e] for e in range(4)]
    unused = jnp.zeros(((LEFT - RIGHT - 1) * 8, LANES), jnp.float32)
    for field in range(2):
        r1b_ref[field, (RIGHT + 1) * 8 : LEFT * 8, :] = unused

    p, q = d_ref[0], d_ref[1]
    last_p, last_q = apply2(p, q, w2)
    c_ref[0, pl.ds(FACTOR - 1, PACKED, stride=8), :] = last_p + r2_ref[0]
    c_ref[1, pl.ds(FACTOR - 1, PACKED, stride=8), :] = last_q + r2_ref[1]
    prev_ref[0, pl.ds(0, PACKED, stride=8), :] = p
    prev_ref[1, pl.ds(0, PACKED, stride=8), :] = q
    for k in range(FACTOR - 1):
        p, q = phi_packed(p, q, w1)
        p = p + r1_ref[0, pl.ds(k, PACKED, stride=8), :]
        q = q + r1_ref[1, pl.ds(k, PACKED, stride=8), :]
        c_ref[0, pl.ds(k, PACKED, stride=8), :] = p
        c_ref[1, pl.ds(k, PACKED, stride=8), :] = q
        prev_ref[0, pl.ds(k + 1, PACKED, stride=8), :] = p
        prev_ref[1, pl.ds(k + 1, PACKED, stride=8), :] = q

    ps, qs = tiles_from(prev_ref, 0), tiles_from(prev_ref, 1)
    for j in range(FACTOR):
        ps, qs = phi_tiles(ps, qs, weight_of)
        if j == FACTOR - 1:
            copies = [
                pltpu.make_async_copy(o_ref.at[pl.ds(k * STRIDE, 224)], out_ref.at[pl.ds(k * 256, 224)], sems.at[k])
                for k in range(FACTOR)
            ]
            for copy in copies:
                copy.start()
        for t in range(LISTED):
            ps[t] = ps[t] + load_forcing(f_ref, halo_ref, j, t, 0)
            qs[t] = qs[t] + load_forcing(f_ref, halo_ref, j, t, 1)
            if j < FACTOR - 1 and t < TILES:
                o_ref[pl.ds(j * 32 + t * 2, 8, stride=STRIDE), :] = ps[t]
                o_ref[pl.ds(j * 32 + t * 2 + 1, 8, stride=STRIDE), :] = qs[t]
    for t, row in spots():
        r1b_ref[0, tile_rows(row), :] = ps[t] - c_ref[0, tile_rows(row), :]
        r1b_ref[1, tile_rows(row), :] = qs[t] - c_ref[1, tile_rows(row), :]

    def finish(k, p, q):
        for field, x in enumerate((p, q)):
            done = c_ref[field, pl.ds(k, PACKED, stride=8), :] + x
            o_ref[pl.ds(k * STRIDE + 224 + field, TILES, stride=2), :] = done[0:TILES]
        copy = pltpu.make_async_copy(
            o_ref.at[pl.ds(k * STRIDE + 224, 32)], out_ref.at[pl.ds(k * 256 + 224, 32)], sems.at[FACTOR + k]
        )
        copy.start()
        copies.append(copy)

    p, q = d_ref[2], d_ref[3]
    last_p, last_q = apply2(p, q, w2)
    mp = mq = None
    for k in range(FACTOR):
        rp, rq = r1b_ref[0, pl.ds(k, PACKED, stride=8), :], r1b_ref[1, pl.ds(k, PACKED, stride=8), :]
        if k == 0:
            mp, mq = rp, rq
        else:
            mp, mq = phi_packed(mp, mq, w1)
            mp, mq = mp + rp, mq + rq
        if k < FACTOR - 1:
            p, q = phi_packed(p, q, w1)
            p, q = p + rp, q + rq
            finish(k, p, q)
    finish(FACTOR - 1, last_p + mp, last_q + mq)
    for copy in copies:
        copy.wait()


VMEM = pl.BlockSpec(memory_space=pltpu.VMEM)
SMEM = pl.BlockSpec(memory_space=pltpu.SMEM)
STATE = (2, PACKED * 8, LANES)


def shaped(*shape):
    return jax.ShapeDtypeStruct(shape, jnp.float32)


def scratch(*shape):
    return pltpu.VMEM(shape, jnp.float32)


ANY = pl.BlockSpec(memory_space=pl.ANY)
HBM = pl.BlockSpec(memory_space=pltpu.HBM)
SMALL = pltpu.CompilerParams(vmem_limit_bytes=8 << 20)
DENSE = pltpu.CompilerParams(vmem_limit_bytes=8 << 20)


def edge_stage(flat, friction, compressor):
    return pl.pallas_call(
        edge_kernel,
        out_shape=(shaped(PADDED, LANES), shaped(EDGE_ROWS, LANES), shaped(EDGE_ROWS, LANES), shaped(TILES, LANES)),
        in_specs=[HBM] * 3,
        out_specs=(VMEM,) * 4,
        scratch_shapes=[pltpu.VMEM((TILES, LANES), jnp.int32)] * 2 + [pltpu.SemaphoreType.DMA((FACTOR + 2,))],
        compiler_params=SMALL,
        name="edge",
    )(flat, friction, compressor)


def first_stage(flat_blocks, padded, right, left, kinds):
    return pl.pallas_call(
        first_kernel,
        out_shape=(shaped(*STATE), shaped(2, PACKED, LANES), shaped(12, PACKED, LANES), shaped(PACKED, LANES), shaped(2 * WINDOWS, LANES), shaped(128, LANES)),
        in_specs=[SMEM] + [VMEM] * 4,
        out_specs=(VMEM,) * 6,
        scratch_shapes=[scratch(*STATE)] * 3,
        compiler_params=DENSE,
        name="first",
    )(flat_blocks, padded, right, left, kinds)


def prepare_stage(place, flat_blocks, kinds):
    return pl.pallas_call(
        prepare_kernel,
        out_shape=(shaped(20, 8, LANES), shaped(2 * LANES, 2 * LANES)),
        in_specs=[SMEM, SMEM, VMEM],
        out_specs=(VMEM, VMEM),
        scratch_shapes=[
            scratch(2 * LANES, 2 * LANES),
            scratch((FACTOR + 1) * GROUPS * 8, 2 * LANES),
            scratch(FACTOR * GROUPS * 8, 2 * LANES),
        ],
        compiler_params=DENSE,
        name="prepare",
    )(place, flat_blocks, kinds)


def slab_stage(scan, dense, got):
    return pl.pallas_call(
        slab_kernel,
        out_shape=shaped(2 * WINDOWS, LANES),
        in_specs=[VMEM] * 3,
        out_specs=VMEM,
        scratch_shapes=[scratch(WINDOWS, 2 * LANES)],
        compiler_params=SMALL,
        name="slab",
    )(scan, dense, got)


def last_stage(padded, halo, r1, r2, weights, got):
    return pl.pallas_call(
        last_kernel,
        out_shape=shaped(2048, LANES),
        in_specs=[VMEM] * 6,
        out_specs=ANY,
        scratch_shapes=[scratch(*STATE)] * 3
        + [scratch(4, PACKED, LANES), scratch(PADDED, LANES), pltpu.SemaphoreType.DMA((2 * FACTOR,))],
        compiler_params=DENSE,
        name="last",
    )(padded, halo, r1, r2, weights, got)


def to_rows(forcing):
    return forcing.reshape(64, 2, TILES, LANES).transpose(0, 2, 1, 3).reshape(2048, LANES)


def from_rows(rows):
    return rows.reshape(64, TILES, 2, LANES).transpose(0, 2, 1, 3).reshape(64, 2, TILES * LANES)


def transpose_windows(rows):
    return lax.all_to_all(rows.reshape(WINDOWS, 2, LANES), "tm", 0, 0).reshape(2 * WINDOWS, LANES)


def per_device(forcing, friction_class, compressor, blocks):
    flat = to_rows(forcing)
    flat_blocks = blocks.reshape(-1)
    friction = friction_class.reshape(TILES, LANES)
    station = compressor.reshape(TILES, LANES)
    count = lax.axis_size("net")
    flat, friction, station = (pltpu.with_memory_space_constraint(x, pltpu.HBM) for x in (flat, friction, station))
    padded, low, high, kinds = edge_stage(flat, friction, station)
    left = lax.ppermute(high, "net", [(i, i + 1) for i in range(count - 1)])
    right = lax.ppermute(low, "net", [(i + 1, i) for i in range(count - 1)])
    r1, r2, weights, kinds_wide, send, halo = first_stage(flat_blocks, padded, right, left, kinds)
    got = transpose_windows(send)
    place = lax.axis_index("tm").astype(jnp.int32).reshape(1)
    scan, dense = prepare_stage(place, flat_blocks, kinds_wide)
    got = transpose_windows(slab_stage(scan, dense, got))
    return from_rows(last_stage(padded, halo, r1, r2, weights, got))


def solution(mesh):
    placed = (P("tm", None, "net"), P("net"), P("net"), P())
    return jax.shard_map(
        per_device, mesh=mesh, in_specs=placed, out_specs=P("tm", None, "net"), check_vma=False
    )
```

```python
import jax
import jax.numpy as jnp
from jax import lax
from jax.experimental import pallas as pl
from jax.experimental.pallas import tpu as pltpu
from jax.sharding import PartitionSpec as P

FACTOR = 8
KINDS = 9
LANES = 128
TILES = 16
WINDOWS = 64
PACKED = 24
RIGHT = 16
LEFT = 23
EDGE_ROWS = 72
STRIDE = 264
PADDED = FACTOR * STRIDE
HALF = LANES // 2
LISTED = TILES + 1
PREV = [TILES] + list(range(TILES))
NEXT = list(range(1, TILES + 1)) + [0]
MEET = 40
ORDER = [(MEET + rank) % WINDOWS for rank in range(WINDOWS)]
SLAB = 32
REACH = 22
SPAN = 84
COMB = 48
GROUPS = 2 * COMB // 8
TEETH = 24


def runs():
    found = []
    for rank, member in enumerate(ORDER):
        if found and found[-1][1] + found[-1][2] == member:
            found[-1][2] += 1
        else:
            found.append([rank, member, 1])
    return found


def by_rank(to_ref, from_ref):
    for rank, member, length in runs():
        to_ref[2 * rank : 2 * (rank + length), :] = from_ref[2 * member : 2 * (member + length), :]


def by_member(to_ref, from_ref):
    for rank, member, length in runs():
        to_ref[2 * member : 2 * (member + length), :] = from_ref[2 * rank : 2 * (rank + length), :]


def lanes_of(shape):
    return lax.broadcasted_iota(jnp.int32, shape, len(shape) - 1)


def couple(p, q, p_low, p_high, q_low, q_high, w):
    mixed_p = (p + p) + (q_high - q_low)
    mixed_q = (q + q) + (p_low - p_high)
    return w[0] * mixed_p + w[1] * mixed_q, w[2] * mixed_p + w[3] * mixed_q


def apply2(p, q, w):
    return w[0] * p + w[1] * q, w[2] * p + w[3] * q


def phi_tiles(ps, qs, weight_of):
    lane = lanes_of((8, LANES))
    first, last = lane == 0, lane == LANES - 1

    def low(xs, t):
        return pltpu.roll(jnp.where(last, xs[PREV[t]], xs[t]), 1, 1)

    def high(xs, t):
        return pltpu.roll(jnp.where(first, xs[NEXT[t]], xs[t]), LANES - 1, 1)

    new_p, new_q = [], []
    for t in range(LISTED):
        p, q = couple(ps[t], qs[t], low(ps, t), high(ps, t), low(qs, t), high(qs, t), weight_of(t))
        new_p.append(p)
        new_q.append(q)
    return new_p, new_q


def phi_packed(p, q, w):
    lane = lanes_of((PACKED, LANES))
    first, last = lane == 0, lane == LANES - 1

    def low(x):
        return pltpu.roll(jnp.where(last, pltpu.roll(x, 1, 0), x), 1, 1)

    def high(x):
        return pltpu.roll(jnp.where(first, pltpu.roll(x, PACKED - 1, 0), x), LANES - 1, 1)

    return couple(p, q, low(p), high(p), low(q), high(q), w)


def phi_slab(p, q, w):
    return couple(
        p, q, pltpu.roll(p, 1, 1), pltpu.roll(p, LANES - 1, 1), pltpu.roll(q, 1, 1), pltpu.roll(q, LANES - 1, 1), w
    )


def pick(blocks_ref, number, kind):
    scale = 1.0 if number == 2 else 0.25
    masks = [kind == float(k + 1) for k in range(KINDS)]
    picked = []
    for entry in range(4):
        chosen = jnp.zeros_like(kind)
        for k in range(KINDS):
            chosen = jnp.where(masks[k], blocks_ref[number, entry // 2, entry % 2, k] * scale, chosen)
        picked.append(chosen)
    return picked


def load_forcing(f_ref, halo_ref, j, t, field):
    if t < TILES:
        return f_ref[pl.ds(j * 32 + t * 2 + field, 8, stride=STRIDE), :]
    return halo_ref[pl.ds((j * 2 + field) * 8, 8), :]


def tile_rows(row):
    return pl.ds(row * 8, 8)


def tiles_from(ref, field):
    both = jnp.where(lanes_of((8, LANES)) < HALF, ref[field, tile_rows(RIGHT), :], ref[field, tile_rows(LEFT), :])
    return [ref[field, tile_rows(t), :] for t in range(TILES)] + [both]


def spots():
    return [(t, t) for t in range(TILES)] + [(TILES, RIGHT), (TILES, LEFT)]


def fine_weights(w_ref):
    def weight_of(t):
        return [jnp.broadcast_to(w_ref[e, t : t + 1, :], (8, LANES)) for e in range(4)]

    return weight_of


def edge_kernel(odd_ref, source_ref, fc_hbm, comp_hbm, f_ref, near_ref, far_ref, kind_ref, fc_ref, comp_ref, sems):
    copies = [
        pltpu.make_async_copy(source_ref.at[pl.ds(k * 256, 256)], f_ref.at[pl.ds(k * STRIDE, 256)], sems.at[k])
        for k in range(FACTOR)
    ]
    labels = [
        pltpu.make_async_copy(fc_hbm, fc_ref, sems.at[FACTOR]),
        pltpu.make_async_copy(comp_hbm, comp_ref, sems.at[FACTOR + 1]),
    ]
    for copy in labels + copies:
        copy.start()
    for copy in labels:
        copy.wait()
    kinds = jnp.where(comp_ref[...] == 1, KINDS, fc_ref[...] + 1).astype(jnp.float32)
    kind_ref[...] = kinds
    odd = is_odd(odd_ref)

    def send(rows, low, high):
        near_ref[rows, :] = jnp.where(odd, low, high)
        far_ref[rows, :] = jnp.where(odd, high, low)

    send(pl.ds(64, 8), *(jnp.broadcast_to(kinds[t : t + 1], (8, LANES)) for t in (0, TILES - 1)))
    left_half = lanes_of((8, LANES)) < HALF
    for copy in copies:
        copy.wait()
    for j in range(FACTOR):
        rows = pl.ds(j * 8, 8)
        p, q = (f_ref[pl.ds(j * 32 + field, 8, stride=STRIDE), :] for field in range(2))
        low = jnp.where(left_half, p, pltpu.roll(q, HALF, 1))
        p, q = (f_ref[pl.ds(j * 32 + 2 * (TILES - 1) + field, 8, stride=STRIDE), :] for field in range(2))
        send(rows, low, jnp.where(left_half, pltpu.roll(q, HALF, 1), p))


def is_odd(odd_ref):
    return jnp.full((8, LANES), odd_ref[0], jnp.int32) == 1


def first_kernel(odd_ref, blocks_ref, f_ref, near_ref, far_ref, kind_ref, r1_ref, r2_ref, w_ref, kx_ref, send_ref,
                 halo_ref, prev_ref, c_ref, r1b_ref, nat_ref):
    kx_ref[0:TILES, :] = kind_ref[...]
    kx_ref[TILES:PACKED, :] = jnp.zeros((PACKED - TILES, LANES), jnp.float32)
    odd = is_odd(odd_ref)
    left_half = lanes_of((8, LANES)) < HALF

    def sides(rows):
        near, far = near_ref[rows, :], far_ref[rows, :]
        return jnp.where(odd, far, near), jnp.where(odd, near, far)

    x, y = sides(pl.ds(64, 8))
    beyond = jnp.where(left_half, x, y)[0:1]
    kx_ref[RIGHT : RIGHT + 1, :] = beyond
    kx_ref[LEFT : LEFT + 1, :] = beyond
    kind = kx_ref[...]
    for number in range(3):
        for entry, chosen in enumerate(pick(blocks_ref, number, kind)):
            w_ref[number * 4 + entry] = chosen
    weight_of = fine_weights(w_ref)
    w1 = [w_ref[4 + e] for e in range(4)]

    for j in range(FACTOR):
        x, y = sides(pl.ds(j * 8, 8))
        halo_ref[pl.ds(j * 16, 8), :] = jnp.where(left_half, x, y)
        halo_ref[pl.ds(j * 16 + 8, 8), :] = pltpu.roll(jnp.where(left_half, y, x), HALF, 1)

    def forcing(j, field):
        return [load_forcing(f_ref, halo_ref, j, t, field) for t in range(LISTED)]

    unused = jnp.zeros(((LEFT - RIGHT - 1) * 8, LANES), jnp.float32)
    for field in range(2):
        for ref in (r1_ref, r1b_ref):
            ref[field, (RIGHT + 1) * 8 : LEFT * 8, :] = unused

    ps, qs = forcing(0, 0), forcing(0, 1)
    for j in range(1, FACTOR):
        ps, qs = phi_tiles(ps, qs, weight_of)
        fp, fq = forcing(j, 0), forcing(j, 1)
        ps = [a + b for a, b in zip(ps, fp)]
        qs = [a + b for a, b in zip(qs, fq)]
    for t, row in spots():
        r1_ref[0, tile_rows(row), :] = ps[t]
        r1_ref[1, tile_rows(row), :] = qs[t]

    def sweep(ref, keep):
        p = q = None
        for k in range(FACTOR):
            rp, rq = ref[0, pl.ds(k, PACKED, stride=8), :], ref[1, pl.ds(k, PACKED, stride=8), :]
            if k == 0:
                p, q = rp, rq
            else:
                p, q = phi_packed(p, q, w1)
                p, q = p + rp, q + rq
            if keep:
                c_ref[0, pl.ds(k, PACKED, stride=8), :] = p
                c_ref[1, pl.ds(k, PACKED, stride=8), :] = q
                if k < FACTOR - 1:
                    prev_ref[0, pl.ds(k + 1, PACKED, stride=8), :] = p
                    prev_ref[1, pl.ds(k + 1, PACKED, stride=8), :] = q
        return p, q

    nothing = jnp.zeros((PACKED, LANES), jnp.float32)
    prev_ref[0, pl.ds(0, PACKED, stride=8), :] = nothing
    prev_ref[1, pl.ds(0, PACKED, stride=8), :] = nothing
    r2p, r2q = sweep(r1_ref, True)
    r2_ref[0] = r2p
    r2_ref[1] = r2q

    ps, qs = tiles_from(prev_ref, 0), tiles_from(prev_ref, 1)
    for j in range(FACTOR):
        ps, qs = phi_tiles(ps, qs, weight_of)
    for field, xs in enumerate((ps, qs)):
        for t, row in spots():
            rows = tile_rows(row)
            r1b_ref[field, rows, :] = xs[t] + (r1_ref[field, rows, :] - c_ref[field, rows, :])
    gp, gq = sweep(r1b_ref, False)

    lane = lanes_of((8, LANES))
    for c, (x, g) in enumerate(((r2p, gp), (r2q, gq))):
        for half in range(2):
            shifted = [
                [y[8 * half : 8 * half + 8] for y in (pltpu.roll(z, 1, 0), z, pltpu.roll(z, PACKED - 1, 0))]
                for z in (x, g)
            ]

            def window(which, offset):
                a, b = shifted[which][0:2] if offset < 0 else shifted[which][1:3]
                start = offset % LANES
                return pltpu.roll(jnp.where(lane >= start, a, b), (LANES - start) % LANES, 1)

            for quarter in range(4):
                origin = SLAB * quarter
                near = window(0, origin + window_start(half))
                far = window(1, origin + share_start(half) - SPAN)
                nat_ref[pl.ds(64 * half + 2 * quarter + c, 8, stride=8), :] = jnp.where(lane < SPAN, near, far)
    by_rank(send_ref, nat_ref)


def window_start(half):
    return -REACH if half else -REACH - 8


def share_start(half):
    return 0 if half else -8


def prepare_kernel(place_ref, blocks_ref, kx_ref, scan_ref, dense_ref, fine_ref, states_ref, after_ref):
    place = place_ref[0]
    lane1 = lanes_of((1, LANES))
    origin = place * SLAB + (LANES - REACH - 8) + jnp.where(place >= WINDOWS // 2, 8, 0)
    base = origin // LANES - 1
    start = origin % LANES
    base = jnp.where(base < 0, LEFT, base)
    after = jnp.where(base == LEFT, 0, base + 1)
    a, b = kx_ref[pl.ds(base, 1), :], kx_ref[pl.ds(after, 1), :]
    kind = pltpu.roll(jnp.where(lane1 >= start, a, b), LANES - start, 1)
    kind = jnp.broadcast_to(kind, (8, LANES))
    w0, w1, w2 = (pick(blocks_ref, number, kind) for number in range(3))
    sub = lax.broadcasted_iota(jnp.int32, (8, LANES), 0)
    lane = lanes_of((8, LANES))

    def times(v, w):
        return [
            v[0] * w[0] + v[1] * w[2],
            v[0] * w[1] + v[1] * w[3],
            v[2] * w[0] + v[3] * w[2],
            v[2] * w[1] + v[3] * w[3],
        ]

    one, none = jnp.ones((8, LANES), jnp.float32), jnp.zeros((8, LANES), jnp.float32)
    w = w2
    grown = [one, none, none, one]
    for n, step in enumerate((1, 2, 4)):
        longer = times(grown, w)
        grown = [jnp.where((sub & step) != 0, x, y) for x, y in zip(longer, grown)]
        for e in range(4):
            scan_ref[4 * n + e] = jnp.where(sub >= step, w[e], 0.0)
        w = times(w, w)
    for e in range(4):
        scan_ref[12 + e] = w[e]
        scan_ref[16 + e] = grown[e]

    def combs(gap, teeth):
        made = []
        for n in range(gap // 8):
            hit = lane == sub + 8 * n
            for tooth in range(1, teeth):
                hit = hit | (lane == sub + (8 * n + gap * tooth))
            made.append(jnp.where(hit, 1.0, 0.0))
        blank = [none] * len(made)
        return made + blank, blank + made

    def spread(answers, ref, gap, teeth, reach):
        for n, answer in enumerate(answers):
            field, c = divmod(n, gap // 8)
            for tooth in range(teeth):
                at = sub + (8 * c + gap * tooth)
                near = (lane - at <= reach) & (at - lane <= reach)
                rows = pl.ds(field * LANES + gap * tooth + 8 * c, 8)
                for to in range(2):
                    ref[rows, LANES * to : LANES * (to + 1)] = jnp.where(near, answer[to], 0.0)
        for field in range(2):
            ref[field * LANES + gap * teeth : (field + 1) * LANES, :] = jnp.zeros((LANES - gap * teeth, 2 * LANES), jnp.float32)

    answers = list(zip(*combs(TEETH, 4)))
    for _ in range(FACTOR):
        answers = [phi_slab(p, q, w0) for p, q in answers]
    spread(answers, fine_ref, TEETH, 4, FACTOR)

    def rows_of(k, n):
        return pl.ds((k * GROUPS + n) * 8, 8)

    begin = list(zip(*combs(COMB, 2)))
    states = begin
    for k in range(FACTOR + 1):
        for n, (p, q) in enumerate(states):
            states_ref[rows_of(k, n), 0:LANES] = p
            states_ref[rows_of(k, n), LANES : 2 * LANES] = q
        if k < FACTOR:
            states = [phi_slab(p, q, w1) for p, q in states]
    after_ref[...] = jnp.dot(
        states_ref[0 : FACTOR * GROUPS * 8, :],
        fine_ref[...],
        precision=lax.Precision.HIGHEST,
        preferred_element_type=jnp.float32,
    )

    def residual(k, n):
        return [
            after_ref[rows_of(k, n), LANES * to : LANES * (to + 1)]
            - states_ref[rows_of(k + 1, n), LANES * to : LANES * (to + 1)]
            for to in range(2)
        ]

    m = [residual(0, n) for n in range(GROUPS)]
    for k in range(1, FACTOR):
        stepped = [phi_slab(p, q, w1) for p, q in m]
        m = [[x + y for x, y in zip(stepped[n], residual(k, n))] for n in range(GROUPS)]

    total = []
    for n in range(GROUPS):
        coarse = apply2(*begin[n], w2)
        total.append([m[n][to] + (states[n][to] - coarse[to]) for to in range(2)])
    spread(total, dense_ref, COMB, 2, REACH)


def slab_kernel(scan_ref, dense_ref, ranked_ref, send_ref, d_ref, got_ref, nat_ref):
    by_member(got_ref, ranked_ref)
    lane = lanes_of((8, LANES))
    masked = [[scan_ref[4 * n + e] for e in range(4)] for n in range(3)]
    w_eight = [scan_ref[12 + e] for e in range(4)]
    grown = [scan_ref[16 + e] for e in range(4)]
    first = lax.broadcasted_iota(jnp.int32, (8, LANES), 0) == 0

    def recurrence(rp, rq):
        yp, yq = list(rp), list(rq)
        for n, step in enumerate((1, 2, 4)):
            for b in range(8):
                sp, sq = apply2(pltpu.roll(yp[b], step, 0), pltpu.roll(yq[b], step, 0), masked[n])
                yp[b], yq[b] = yp[b] + sp, yq[b] + sq
        dp, dq = [], []
        tp = tq = None
        for b in range(8):
            bp, bq = pltpu.roll(yp[b], 1, 0), pltpu.roll(yq[b], 1, 0)
            bp, bq = jnp.where(first, 0.0, bp), jnp.where(first, 0.0, bq)
            ep, eq = yp[b][7:8], yq[b][7:8]
            ep, eq = jnp.broadcast_to(ep, (8, LANES)), jnp.broadcast_to(eq, (8, LANES))
            if b:
                sp, sq = apply2(tp, tq, grown)
                bp, bq = bp + sp, bq + sq
                sp, sq = apply2(tp, tq, w_eight)
                ep, eq = ep + sp, eq + sq
            tp, tq = ep, eq
            dp.append(bp)
            dq.append(bq)
        return dp, dq

    def rows(b, c):
        return pl.ds(b * 16 + c, 8, stride=2)

    gotten = [[got_ref[rows(b, c), :] for b in range(8)] for c in range(2)]
    dp, dq = recurrence(*gotten)
    for b in range(8):
        d_ref[8 * b : 8 * b + 8, 0:LANES] = dp[b]
        d_ref[8 * b : 8 * b + 8, LANES : 2 * LANES] = dq[b]
    answer = jnp.dot(d_ref[...], dense_ref[...], precision=lax.Precision.HIGHEST, preferred_element_type=jnp.float32)
    back = SPAN - REACH
    residual = [
        [
            answer[8 * b : 8 * b + 8, LANES * c : LANES * (c + 1)] + pltpu.roll(gotten[c][b], LANES - back, 1)
            for b in range(8)
        ]
        for c in range(2)
    ]
    ep, eq = recurrence(*residual)
    for b in range(8):
        nat_ref[rows(b, 0), :] = jnp.where(lane < SPAN, dp[b], pltpu.roll(ep[b], back, 1))
        nat_ref[rows(b, 1), :] = jnp.where(lane < SPAN, dq[b], pltpu.roll(eq[b], back, 1))
    by_rank(send_ref, nat_ref)


def last_kernel(f_ref, halo_ref, r1_ref, r2_ref, w_ref, ranked_ref, out_ref, prev_ref, c_ref, r1b_ref, d_ref,
                o_ref, got_ref, sems):
    by_member(got_ref, ranked_ref)

    lane = lanes_of((8, LANES))
    lane1 = lanes_of((1, LANES))
    for c in range(2):
        for cycle in range(2):
            for half in range(2):
                begin = (SPAN - share_start(half)) if cycle else -window_start(half)
                whole = jnp.zeros((8, LANES), jnp.float32)
                for quarter in range(4):
                    piece = got_ref[pl.ds(64 * half + 2 * quarter + c, 8, stride=8), :]
                    piece = pltpu.roll(piece, (SLAB * quarter - begin) % LANES, 1)
                    mine = (lane >= SLAB * quarter) & (lane < SLAB * (quarter + 1))
                    whole = jnp.where(mine, piece, whole)
                d_ref[2 * cycle + c, 8 * half : 8 * half + 8, :] = whole
            d_ref[2 * cycle + c, TILES:PACKED, :] = jnp.zeros((PACKED - TILES, LANES), jnp.float32)
            width = 8 if cycle else 24
            begin = (SPAN - share_start(0)) if cycle else -window_start(0)
            low = pltpu.roll(got_ref[c : c + 1, :], LANES - begin, 1)
            d_ref[2 * cycle + c, LEFT : LEFT + 1, :] = jnp.where(lane1 >= LANES - width, low, 0.0)
            begin = (SPAN - share_start(1)) if cycle else -window_start(1)
            end = (WINDOWS - 1) * 2 + c
            high = pltpu.roll(got_ref[end : end + 1, :], LANES - begin - SLAB, 1)
            d_ref[2 * cycle + c, RIGHT : RIGHT + 1, :] = jnp.where(lane1 < width, high, 0.0)

    weight_of = fine_weights(w_ref)
    w1 = [w_ref[4 + e] for e in range(4)]
    w2 = [w_ref[8 + e] for e in range(4)]
    unused = jnp.zeros(((LEFT - RIGHT - 1) * 8, LANES), jnp.float32)
    for field in range(2):
        r1b_ref[field, (RIGHT + 1) * 8 : LEFT * 8, :] = unused

    p, q = d_ref[0], d_ref[1]
    last_p, last_q = apply2(p, q, w2)
    c_ref[0, pl.ds(FACTOR - 1, PACKED, stride=8), :] = last_p + r2_ref[0]
    c_ref[1, pl.ds(FACTOR - 1, PACKED, stride=8), :] = last_q + r2_ref[1]
    prev_ref[0, pl.ds(0, PACKED, stride=8), :] = p
    prev_ref[1, pl.ds(0, PACKED, stride=8), :] = q
    for k in range(FACTOR - 1):
        p, q = phi_packed(p, q, w1)
        p = p + r1_ref[0, pl.ds(k, PACKED, stride=8), :]
        q = q + r1_ref[1, pl.ds(k, PACKED, stride=8), :]
        c_ref[0, pl.ds(k, PACKED, stride=8), :] = p
        c_ref[1, pl.ds(k, PACKED, stride=8), :] = q
        prev_ref[0, pl.ds(k + 1, PACKED, stride=8), :] = p
        prev_ref[1, pl.ds(k + 1, PACKED, stride=8), :] = q

    ps, qs = tiles_from(prev_ref, 0), tiles_from(prev_ref, 1)
    for j in range(FACTOR):
        ps, qs = phi_tiles(ps, qs, weight_of)
        if j == FACTOR - 1:
            copies = [
                pltpu.make_async_copy(o_ref.at[pl.ds(k * STRIDE, 224)], out_ref.at[pl.ds(k * 256, 224)], sems.at[k])
                for k in range(FACTOR)
            ]
            for copy in copies:
                copy.start()
        for t in range(LISTED):
            ps[t] = ps[t] + load_forcing(f_ref, halo_ref, j, t, 0)
            qs[t] = qs[t] + load_forcing(f_ref, halo_ref, j, t, 1)
            if j < FACTOR - 1 and t < TILES:
                o_ref[pl.ds(j * 32 + t * 2, 8, stride=STRIDE), :] = ps[t]
                o_ref[pl.ds(j * 32 + t * 2 + 1, 8, stride=STRIDE), :] = qs[t]
    for t, row in spots():
        r1b_ref[0, tile_rows(row), :] = ps[t] - c_ref[0, tile_rows(row), :]
        r1b_ref[1, tile_rows(row), :] = qs[t] - c_ref[1, tile_rows(row), :]

    def finish(k, p, q):
        for field, x in enumerate((p, q)):
            done = c_ref[field, pl.ds(k, PACKED, stride=8), :] + x
            o_ref[pl.ds(k * STRIDE + 224 + field, TILES, stride=2), :] = done[0:TILES]
        copy = pltpu.make_async_copy(
            o_ref.at[pl.ds(k * STRIDE + 224, 32)], out_ref.at[pl.ds(k * 256 + 224, 32)], sems.at[FACTOR + k]
        )
        copy.start()
        copies.append(copy)

    p, q = d_ref[2], d_ref[3]
    last_p, last_q = apply2(p, q, w2)
    mp = mq = None
    for k in range(FACTOR):
        rp, rq = r1b_ref[0, pl.ds(k, PACKED, stride=8), :], r1b_ref[1, pl.ds(k, PACKED, stride=8), :]
        if k == 0:
            mp, mq = rp, rq
        else:
            mp, mq = phi_packed(mp, mq, w1)
            mp, mq = mp + rp, mq + rq
        if k < FACTOR - 1:
            p, q = phi_packed(p, q, w1)
            p, q = p + rp, q + rq
            finish(k, p, q)
    finish(FACTOR - 1, last_p + mp, last_q + mq)
    for copy in copies:
        copy.wait()


VMEM = pl.BlockSpec(memory_space=pltpu.VMEM)
SMEM = pl.BlockSpec(memory_space=pltpu.SMEM)
STATE = (2, PACKED * 8, LANES)


def shaped(*shape):
    return jax.ShapeDtypeStruct(shape, jnp.float32)


def scratch(*shape):
    return pltpu.VMEM(shape, jnp.float32)


ANY = pl.BlockSpec(memory_space=pl.ANY)
HBM = pl.BlockSpec(memory_space=pltpu.HBM)
SMALL = pltpu.CompilerParams(vmem_limit_bytes=8 << 20)
DENSE = pltpu.CompilerParams(vmem_limit_bytes=8 << 20)


def edge_stage(odd, flat, friction, compressor):
    return pl.pallas_call(
        edge_kernel,
        out_shape=(shaped(PADDED, LANES), shaped(EDGE_ROWS, LANES), shaped(EDGE_ROWS, LANES), shaped(TILES, LANES)),
        in_specs=[SMEM] + [HBM] * 3,
        out_specs=(VMEM,) * 4,
        scratch_shapes=[pltpu.VMEM((TILES, LANES), jnp.int32)] * 2 + [pltpu.SemaphoreType.DMA((FACTOR + 2,))],
        compiler_params=SMALL,
        name="edge",
    )(odd, flat, friction, compressor)


def first_stage(odd, blocks, padded, near, far, kinds):
    return pl.pallas_call(
        first_kernel,
        out_shape=(shaped(*STATE), shaped(2, PACKED, LANES), shaped(12, PACKED, LANES), shaped(PACKED, LANES), shaped(2 * WINDOWS, LANES), shaped(128, LANES)),
        in_specs=[SMEM] * 2 + [VMEM] * 4,
        out_specs=(VMEM,) * 6,
        scratch_shapes=[scratch(*STATE)] * 3 + [scratch(2 * WINDOWS, LANES)],
        compiler_params=DENSE,
        name="first",
    )(odd, blocks, padded, near, far, kinds)


def prepare_stage(place, blocks, kinds):
    return pl.pallas_call(
        prepare_kernel,
        out_shape=(shaped(20, 8, LANES), shaped(2 * LANES, 2 * LANES)),
        in_specs=[SMEM, SMEM, VMEM],
        out_specs=(VMEM, VMEM),
        scratch_shapes=[
            scratch(2 * LANES, 2 * LANES),
            scratch((FACTOR + 1) * GROUPS * 8, 2 * LANES),
            scratch(FACTOR * GROUPS * 8, 2 * LANES),
        ],
        compiler_params=DENSE,
        name="prepare",
    )(place, blocks, kinds)


def slab_stage(scan, dense, got):
    return pl.pallas_call(
        slab_kernel,
        out_shape=shaped(2 * WINDOWS, LANES),
        in_specs=[VMEM] * 3,
        out_specs=VMEM,
        scratch_shapes=[scratch(WINDOWS, 2 * LANES)] + [scratch(2 * WINDOWS, LANES)] * 2,
        compiler_params=SMALL,
        name="slab",
    )(scan, dense, got)


def last_stage(padded, halo, r1, r2, weights, got):
    return pl.pallas_call(
        last_kernel,
        out_shape=shaped(2048, LANES),
        in_specs=[VMEM] * 6,
        out_specs=ANY,
        scratch_shapes=[scratch(*STATE)] * 3
        + [scratch(4, PACKED, LANES), scratch(PADDED, LANES), scratch(2 * WINDOWS, LANES), pltpu.SemaphoreType.DMA((2 * FACTOR,))],
        compiler_params=DENSE,
        name="last",
    )(padded, halo, r1, r2, weights, got)


def to_rows(forcing):
    return forcing.reshape(64, 2, TILES, LANES).transpose(0, 2, 1, 3).reshape(2048, LANES)


def from_rows(rows):
    return rows.reshape(64, TILES, 2, LANES).transpose(0, 2, 1, 3).reshape(64, 2, TILES * LANES)


def transpose_windows(rows):
    return lax.all_to_all(rows.reshape(WINDOWS, 2, LANES), "tm", 0, 0, axis_index_groups=[ORDER]).reshape(2 * WINDOWS, LANES)


def per_device(forcing, friction_class, compressor, blocks):
    flat = to_rows(forcing)
    friction = friction_class.reshape(TILES, LANES)
    station = compressor.reshape(TILES, LANES)
    count = lax.axis_size("net")
    flat, friction, station = (pltpu.with_memory_space_constraint(x, pltpu.HBM) for x in (flat, friction, station))
    odd = (lax.axis_index("net") % 2).astype(jnp.int32).reshape(1)
    padded, near, far, kinds = edge_stage(odd, flat, friction, station)
    apart = [(i, i + 1 if i % 2 else i - 1) for i in range(count)]
    far = lax.ppermute(far, "net", [(i, k) for i, k in apart if 0 <= k < count])
    near = lax.ppermute(near, "net", [(i, i ^ 1) for i in range(count)])
    r1, r2, weights, kinds_wide, send, halo = first_stage(odd, blocks, padded, near, far, kinds)
    got = transpose_windows(send)
    place = lax.axis_index("tm").astype(jnp.int32).reshape(1)
    scan, dense = prepare_stage(place, blocks, kinds_wide)
    got = transpose_windows(slab_stage(scan, dense, got))
    return from_rows(last_stage(padded, halo, r1, r2, weights, got))


def solution(mesh):
    placed = (P("tm", None, "net"), P("net"), P("net"), P())
    return jax.shard_map(
        per_device, mesh=mesh, in_specs=placed, out_specs=P("tm", None, "net"), check_vma=False
    )
```

```python
import jax
import jax.numpy as jnp
from jax import lax
from jax.experimental import pallas as pl
from jax.experimental.pallas import tpu as pltpu
from jax.sharding import PartitionSpec as P

FACTOR = 8
KINDS = 9
LANES = 128
TILES = 16
WINDOWS = 64
PACKED = 24
RIGHT = 16
LEFT = 23
EDGE_ROWS = 72
STRIDE = 264
PADDED = FACTOR * STRIDE
HALF = LANES // 2
LISTED = TILES + 1
PREV = [TILES] + list(range(TILES))
NEXT = list(range(1, TILES + 1)) + [0]
MEET = 40
ORDER = [(MEET + rank) % WINDOWS for rank in range(WINDOWS)]
EARLY = 32
SLAB = 32
REACH = 22
SPAN = 84
COMB = 48
GROUPS = 2 * COMB // 8
TEETH = 24


def runs():
    found = []
    for rank, member in enumerate(ORDER):
        if found and found[-1][1] + found[-1][2] == member:
            found[-1][2] += 1
        else:
            found.append([rank, member, 1])
    return found


def by_rank(to_ref, from_ref):
    for rank, member, length in runs():
        to_ref[2 * rank : 2 * (rank + length), :] = from_ref[2 * member : 2 * (member + length), :]


def by_member(to_ref, from_ref):
    for rank, member, length in runs():
        to_ref[2 * member : 2 * (member + length), :] = from_ref[2 * rank : 2 * (rank + length), :]


def lanes_of(shape):
    return lax.broadcasted_iota(jnp.int32, shape, len(shape) - 1)


def couple(p, q, p_low, p_high, q_low, q_high, w):
    mixed_p = (p + p) + (q_high - q_low)
    mixed_q = (q + q) + (p_low - p_high)
    return w[0] * mixed_p + w[1] * mixed_q, w[2] * mixed_p + w[3] * mixed_q


def apply2(p, q, w):
    return w[0] * p + w[1] * q, w[2] * p + w[3] * q


def phi_tiles(ps, qs, weight_of):
    lane = lanes_of((8, LANES))
    first, last = lane == 0, lane == LANES - 1

    def low(xs, t):
        return pltpu.roll(jnp.where(last, xs[PREV[t]], xs[t]), 1, 1)

    def high(xs, t):
        return pltpu.roll(jnp.where(first, xs[NEXT[t]], xs[t]), LANES - 1, 1)

    new_p, new_q = [], []
    for t in range(LISTED):
        p, q = couple(ps[t], qs[t], low(ps, t), high(ps, t), low(qs, t), high(qs, t), weight_of(t))
        new_p.append(p)
        new_q.append(q)
    return new_p, new_q


def phi_packed(p, q, w):
    lane = lanes_of((PACKED, LANES))
    first, last = lane == 0, lane == LANES - 1

    def low(x):
        return pltpu.roll(jnp.where(last, pltpu.roll(x, 1, 0), x), 1, 1)

    def high(x):
        return pltpu.roll(jnp.where(first, pltpu.roll(x, PACKED - 1, 0), x), LANES - 1, 1)

    return couple(p, q, low(p), high(p), low(q), high(q), w)


def phi_slab(p, q, w):
    return couple(
        p, q, pltpu.roll(p, 1, 1), pltpu.roll(p, LANES - 1, 1), pltpu.roll(q, 1, 1), pltpu.roll(q, LANES - 1, 1), w
    )


def pick(blocks_ref, number, kind):
    scale = 1.0 if number == 2 else 0.25
    masks = [kind == float(k + 1) for k in range(KINDS)]
    picked = []
    for entry in range(4):
        chosen = jnp.zeros_like(kind)
        for k in range(KINDS):
            chosen = jnp.where(masks[k], blocks_ref[number, entry // 2, entry % 2, k] * scale, chosen)
        picked.append(chosen)
    return picked


def load_forcing(f_ref, halo_ref, j, t, field):
    if t < TILES:
        return f_ref[pl.ds(j * 32 + t * 2 + field, 8, stride=STRIDE), :]
    return halo_ref[pl.ds((j * 2 + field) * 8, 8), :]


def tile_rows(row):
    return pl.ds(row * 8, 8)


def tiles_from(ref, field):
    both = jnp.where(lanes_of((8, LANES)) < HALF, ref[field, tile_rows(RIGHT), :], ref[field, tile_rows(LEFT), :])
    return [ref[field, tile_rows(t), :] for t in range(TILES)] + [both]


def spots():
    return [(t, t) for t in range(TILES)] + [(TILES, RIGHT), (TILES, LEFT)]


def fine_weights(w_ref):
    def weight_of(t):
        return [jnp.broadcast_to(w_ref[e, t : t + 1, :], (8, LANES)) for e in range(4)]

    return weight_of


def edge_kernel(source_ref, fc_hbm, comp_hbm, f_ref, low_ref, high_ref, kind_ref, fc_ref, comp_ref, sems):
    copies = [
        pltpu.make_async_copy(source_ref.at[pl.ds(k * 256, 256)], f_ref.at[pl.ds(k * STRIDE, 256)], sems.at[k])
        for k in range(FACTOR)
    ]
    labels = [
        pltpu.make_async_copy(fc_hbm, fc_ref, sems.at[FACTOR]),
        pltpu.make_async_copy(comp_hbm, comp_ref, sems.at[FACTOR + 1]),
    ]
    for copy in labels + copies:
        copy.start()
    for copy in labels:
        copy.wait()
    kinds = jnp.where(comp_ref[...] == 1, KINDS, fc_ref[...] + 1).astype(jnp.float32)
    kind_ref[...] = kinds
    low_ref[64:EDGE_ROWS, :] = jnp.broadcast_to(kinds[0:1], (8, LANES))
    high_ref[64:EDGE_ROWS, :] = jnp.broadcast_to(kinds[TILES - 1 : TILES], (8, LANES))
    left_half = lanes_of((8, LANES)) < HALF
    for copy in copies:
        copy.wait()
    for j in range(FACTOR):
        rows = pl.ds(j * 8, 8)
        p, q = (f_ref[pl.ds(j * 32 + field, 8, stride=STRIDE), :] for field in range(2))
        low_ref[rows, :] = jnp.where(left_half, p, pltpu.roll(q, HALF, 1))
        p, q = (f_ref[pl.ds(j * 32 + 2 * (TILES - 1) + field, 8, stride=STRIDE), :] for field in range(2))
        high_ref[rows, :] = jnp.where(left_half, pltpu.roll(q, HALF, 1), p)


def first_kernel(place_ref, blocks_ref, f_ref, right_ref, left_ref, kind_ref, r1_ref, r2_ref, w_ref, kx_ref, send_ref,
                 halo_ref, scan_ref, dense_ref, prev_ref, c_ref, r1b_ref, nat_ref, fine_ref, states_ref, after_ref):
    kx_ref[0:TILES, :] = kind_ref[...]
    kx_ref[TILES:PACKED, :] = jnp.zeros((PACKED - TILES, LANES), jnp.float32)
    beyond = jnp.where(lanes_of((1, LANES)) < HALF, right_ref[64:65, :], left_ref[64:65, :])
    kx_ref[RIGHT : RIGHT + 1, :] = beyond
    kx_ref[LEFT : LEFT + 1, :] = beyond
    kind = kx_ref[...]
    for number in range(3):
        for entry, chosen in enumerate(pick(blocks_ref, number, kind)):
            w_ref[number * 4 + entry] = chosen
    weight_of = fine_weights(w_ref)
    w1 = [w_ref[4 + e] for e in range(4)]

    left_half = lanes_of((8, LANES)) < HALF
    for j in range(FACTOR):
        x, y = right_ref[pl.ds(j * 8, 8), :], left_ref[pl.ds(j * 8, 8), :]
        halo_ref[pl.ds(j * 16, 8), :] = jnp.where(left_half, x, y)
        halo_ref[pl.ds(j * 16 + 8, 8), :] = pltpu.roll(jnp.where(left_half, y, x), HALF, 1)

    def forcing(j, field):
        return [load_forcing(f_ref, halo_ref, j, t, field) for t in range(LISTED)]

    unused = jnp.zeros(((LEFT - RIGHT - 1) * 8, LANES), jnp.float32)
    for field in range(2):
        for ref in (r1_ref, r1b_ref):
            ref[field, (RIGHT + 1) * 8 : LEFT * 8, :] = unused

    ps, qs = forcing(0, 0), forcing(0, 1)
    for j in range(1, FACTOR):
        ps, qs = phi_tiles(ps, qs, weight_of)
        fp, fq = forcing(j, 0), forcing(j, 1)
        ps = [a + b for a, b in zip(ps, fp)]
        qs = [a + b for a, b in zip(qs, fq)]
    for t, row in spots():
        r1_ref[0, tile_rows(row), :] = ps[t]
        r1_ref[1, tile_rows(row), :] = qs[t]

    def sweep(ref, keep):
        p = q = None
        for k in range(FACTOR):
            rp, rq = ref[0, pl.ds(k, PACKED, stride=8), :], ref[1, pl.ds(k, PACKED, stride=8), :]
            if k == 0:
                p, q = rp, rq
            else:
                p, q = phi_packed(p, q, w1)
                p, q = p + rp, q + rq
            if keep:
                c_ref[0, pl.ds(k, PACKED, stride=8), :] = p
                c_ref[1, pl.ds(k, PACKED, stride=8), :] = q
                if k < FACTOR - 1:
                    prev_ref[0, pl.ds(k + 1, PACKED, stride=8), :] = p
                    prev_ref[1, pl.ds(k + 1, PACKED, stride=8), :] = q
        return p, q

    nothing = jnp.zeros((PACKED, LANES), jnp.float32)
    prev_ref[0, pl.ds(0, PACKED, stride=8), :] = nothing
    prev_ref[1, pl.ds(0, PACKED, stride=8), :] = nothing
    r2p, r2q = sweep(r1_ref, True)
    r2_ref[0] = r2p
    r2_ref[1] = r2q

    ps, qs = tiles_from(prev_ref, 0), tiles_from(prev_ref, 1)
    for j in range(FACTOR):
        ps, qs = phi_tiles(ps, qs, weight_of)
    for field, xs in enumerate((ps, qs)):
        for t, row in spots():
            rows = tile_rows(row)
            r1b_ref[field, rows, :] = xs[t] + (r1_ref[field, rows, :] - c_ref[field, rows, :])
    gp, gq = sweep(r1b_ref, False)

    lane = lanes_of((8, LANES))
    for c, (x, g) in enumerate(((r2p, gp), (r2q, gq))):
        for half in range(2):
            shifted = [
                [y[8 * half : 8 * half + 8] for y in (pltpu.roll(z, 1, 0), z, pltpu.roll(z, PACKED - 1, 0))]
                for z in (x, g)
            ]

            def window(which, offset):
                a, b = shifted[which][0:2] if offset < 0 else shifted[which][1:3]
                start = offset % LANES
                return pltpu.roll(jnp.where(lane >= start, a, b), (LANES - start) % LANES, 1)

            for quarter in range(4):
                origin = SLAB * quarter
                near = window(0, origin + window_start(half))
                far = window(1, origin + share_start(half) - SPAN)
                nat_ref[pl.ds(64 * half + 2 * quarter + c, 8, stride=8), :] = jnp.where(lane < SPAN, near, far)
    by_rank(send_ref, nat_ref)

    @pl.when(place_ref[0] < EARLY)
    def _():
        prepare(place_ref, blocks_ref, kx_ref, scan_ref, dense_ref, fine_ref, states_ref, after_ref)


def window_start(half):
    return -REACH if half else -REACH - 8


def share_start(half):
    return 0 if half else -8


def prepare(place_ref, blocks_ref, kx_ref, scan_ref, dense_ref, fine_ref, states_ref, after_ref):
    place = place_ref[0]
    lane1 = lanes_of((1, LANES))
    origin = place * SLAB + (LANES - REACH - 8) + jnp.where(place >= WINDOWS // 2, 8, 0)
    base = origin // LANES - 1
    start = origin % LANES
    base = jnp.where(base < 0, LEFT, base)
    after = jnp.where(base == LEFT, 0, base + 1)
    a, b = kx_ref[pl.ds(base, 1), :], kx_ref[pl.ds(after, 1), :]
    kind = pltpu.roll(jnp.where(lane1 >= start, a, b), LANES - start, 1)
    kind = jnp.broadcast_to(kind, (8, LANES))
    w0, w1, w2 = (pick(blocks_ref, number, kind) for number in range(3))
    sub = lax.broadcasted_iota(jnp.int32, (8, LANES), 0)
    lane = lanes_of((8, LANES))

    def times(v, w):
        return [
            v[0] * w[0] + v[1] * w[2],
            v[0] * w[1] + v[1] * w[3],
            v[2] * w[0] + v[3] * w[2],
            v[2] * w[1] + v[3] * w[3],
        ]

    one, none = jnp.ones((8, LANES), jnp.float32), jnp.zeros((8, LANES), jnp.float32)
    w = w2
    grown = [one, none, none, one]
    for n, step in enumerate((1, 2, 4)):
        longer = times(grown, w)
        grown = [jnp.where((sub & step) != 0, x, y) for x, y in zip(longer, grown)]
        for e in range(4):
            scan_ref[4 * n + e] = jnp.where(sub >= step, w[e], 0.0)
        w = times(w, w)
    for e in range(4):
        scan_ref[12 + e] = w[e]
        scan_ref[16 + e] = grown[e]

    def combs(gap, teeth):
        made = []
        for n in range(gap // 8):
            hit = lane == sub + 8 * n
            for tooth in range(1, teeth):
                hit = hit | (lane == sub + (8 * n + gap * tooth))
            made.append(jnp.where(hit, 1.0, 0.0))
        blank = [none] * len(made)
        return made + blank, blank + made

    def spread(answers, ref, gap, teeth, reach):
        for n, answer in enumerate(answers):
            field, c = divmod(n, gap // 8)
            for tooth in range(teeth):
                at = sub + (8 * c + gap * tooth)
                near = (lane - at <= reach) & (at - lane <= reach)
                rows = pl.ds(field * LANES + gap * tooth + 8 * c, 8)
                for to in range(2):
                    ref[rows, LANES * to : LANES * (to + 1)] = jnp.where(near, answer[to], 0.0)
        for field in range(2):
            ref[field * LANES + gap * teeth : (field + 1) * LANES, :] = jnp.zeros((LANES - gap * teeth, 2 * LANES), jnp.float32)

    answers = list(zip(*combs(TEETH, 4)))
    for _ in range(FACTOR):
        answers = [phi_slab(p, q, w0) for p, q in answers]
    spread(answers, fine_ref, TEETH, 4, FACTOR)

    def rows_of(k, n):
        return pl.ds((k * GROUPS + n) * 8, 8)

    begin = list(zip(*combs(COMB, 2)))
    states = begin
    for k in range(FACTOR + 1):
        for n, (p, q) in enumerate(states):
            states_ref[rows_of(k, n), 0:LANES] = p
            states_ref[rows_of(k, n), LANES : 2 * LANES] = q
        if k < FACTOR:
            states = [phi_slab(p, q, w1) for p, q in states]
    after_ref[...] = jnp.dot(
        states_ref[0 : FACTOR * GROUPS * 8, :],
        fine_ref[...],
        precision=lax.Precision.HIGHEST,
        preferred_element_type=jnp.float32,
    )

    def residual(k, n):
        return [
            after_ref[rows_of(k, n), LANES * to : LANES * (to + 1)]
            - states_ref[rows_of(k + 1, n), LANES * to : LANES * (to + 1)]
            for to in range(2)
        ]

    m = [residual(0, n) for n in range(GROUPS)]
    for k in range(1, FACTOR):
        stepped = [phi_slab(p, q, w1) for p, q in m]
        m = [[x + y for x, y in zip(stepped[n], residual(k, n))] for n in range(GROUPS)]

    total = []
    for n in range(GROUPS):
        coarse = apply2(*begin[n], w2)
        total.append([m[n][to] + (states[n][to] - coarse[to]) for to in range(2)])
    spread(total, dense_ref, COMB, 2, REACH)


def prepare_kernel(place_ref, blocks_ref, kx_ref, scan_in, dense_in, scan_ref, dense_ref, fine_ref, states_ref, after_ref):
    @pl.when(place_ref[0] >= EARLY)
    def _():
        prepare(place_ref, blocks_ref, kx_ref, scan_ref, dense_ref, fine_ref, states_ref, after_ref)


def slab_kernel(scan_ref, dense_ref, ranked_ref, send_ref, d_ref, got_ref, nat_ref):
    by_member(got_ref, ranked_ref)
    lane = lanes_of((8, LANES))
    masked = [[scan_ref[4 * n + e] for e in range(4)] for n in range(3)]
    w_eight = [scan_ref[12 + e] for e in range(4)]
    grown = [scan_ref[16 + e] for e in range(4)]
    first = lax.broadcasted_iota(jnp.int32, (8, LANES), 0) == 0

    def recurrence(rp, rq):
        yp, yq = list(rp), list(rq)
        for n, step in enumerate((1, 2, 4)):
            for b in range(8):
                sp, sq = apply2(pltpu.roll(yp[b], step, 0), pltpu.roll(yq[b], step, 0), masked[n])
                yp[b], yq[b] = yp[b] + sp, yq[b] + sq
        dp, dq = [], []
        tp = tq = None
        for b in range(8):
            bp, bq = pltpu.roll(yp[b], 1, 0), pltpu.roll(yq[b], 1, 0)
            bp, bq = jnp.where(first, 0.0, bp), jnp.where(first, 0.0, bq)
            ep, eq = yp[b][7:8], yq[b][7:8]
            ep, eq = jnp.broadcast_to(ep, (8, LANES)), jnp.broadcast_to(eq, (8, LANES))
            if b:
                sp, sq = apply2(tp, tq, grown)
                bp, bq = bp + sp, bq + sq
                sp, sq = apply2(tp, tq, w_eight)
                ep, eq = ep + sp, eq + sq
            tp, tq = ep, eq
            dp.append(bp)
            dq.append(bq)
        return dp, dq

    def rows(b, c):
        return pl.ds(b * 16 + c, 8, stride=2)

    gotten = [[got_ref[rows(b, c), :] for b in range(8)] for c in range(2)]
    dp, dq = recurrence(*gotten)
    for b in range(8):
        d_ref[8 * b : 8 * b + 8, 0:LANES] = dp[b]
        d_ref[8 * b : 8 * b + 8, LANES : 2 * LANES] = dq[b]
    answer = jnp.dot(d_ref[...], dense_ref[...], precision=lax.Precision.HIGHEST, preferred_element_type=jnp.float32)
    back = SPAN - REACH
    residual = [
        [
            answer[8 * b : 8 * b + 8, LANES * c : LANES * (c + 1)] + pltpu.roll(gotten[c][b], LANES - back, 1)
            for b in range(8)
        ]
        for c in range(2)
    ]
    ep, eq = recurrence(*residual)
    for b in range(8):
        nat_ref[rows(b, 0), :] = jnp.where(lane < SPAN, dp[b], pltpu.roll(ep[b], back, 1))
        nat_ref[rows(b, 1), :] = jnp.where(lane < SPAN, dq[b], pltpu.roll(eq[b], back, 1))
    by_rank(send_ref, nat_ref)


def last_kernel(f_ref, halo_ref, r1_ref, r2_ref, w_ref, ranked_ref, out_ref, prev_ref, c_ref, r1b_ref, d_ref,
                o_ref, got_ref, sems):
    by_member(got_ref, ranked_ref)

    lane = lanes_of((8, LANES))
    lane1 = lanes_of((1, LANES))
    for c in range(2):
        for cycle in range(2):
            for half in range(2):
                begin = (SPAN - share_start(half)) if cycle else -window_start(half)
                whole = jnp.zeros((8, LANES), jnp.float32)
                for quarter in range(4):
                    piece = got_ref[pl.ds(64 * half + 2 * quarter + c, 8, stride=8), :]
                    piece = pltpu.roll(piece, (SLAB * quarter - begin) % LANES, 1)
                    mine = (lane >= SLAB * quarter) & (lane < SLAB * (quarter + 1))
                    whole = jnp.where(mine, piece, whole)
                d_ref[2 * cycle + c, 8 * half : 8 * half + 8, :] = whole
            d_ref[2 * cycle + c, TILES:PACKED, :] = jnp.zeros((PACKED - TILES, LANES), jnp.float32)
            width = 8 if cycle else 24
            begin = (SPAN - share_start(0)) if cycle else -window_start(0)
            low = pltpu.roll(got_ref[c : c + 1, :], LANES - begin, 1)
            d_ref[2 * cycle + c, LEFT : LEFT + 1, :] = jnp.where(lane1 >= LANES - width, low, 0.0)
            begin = (SPAN - share_start(1)) if cycle else -window_start(1)
            end = (WINDOWS - 1) * 2 + c
            high = pltpu.roll(got_ref[end : end + 1, :], LANES - begin - SLAB, 1)
            d_ref[2 * cycle + c, RIGHT : RIGHT + 1, :] = jnp.where(lane1 < width, high, 0.0)

    weight_of = fine_weights(w_ref)
    w1 = [w_ref[4 + e] for e in range(4)]
    w2 = [w_ref[8 + e] for e in range(4)]
    unused = jnp.zeros(((LEFT - RIGHT - 1) * 8, LANES), jnp.float32)
    for field in range(2):
        r1b_ref[field, (RIGHT + 1) * 8 : LEFT * 8, :] = unused

    p, q = d_ref[0], d_ref[1]
    last_p, last_q = apply2(p, q, w2)
    c_ref[0, pl.ds(FACTOR - 1, PACKED, stride=8), :] = last_p + r2_ref[0]
    c_ref[1, pl.ds(FACTOR - 1, PACKED, stride=8), :] = last_q + r2_ref[1]
    prev_ref[0, pl.ds(0, PACKED, stride=8), :] = p
    prev_ref[1, pl.ds(0, PACKED, stride=8), :] = q
    for k in range(FACTOR - 1):
        p, q = phi_packed(p, q, w1)
        p = p + r1_ref[0, pl.ds(k, PACKED, stride=8), :]
        q = q + r1_ref[1, pl.ds(k, PACKED, stride=8), :]
        c_ref[0, pl.ds(k, PACKED, stride=8), :] = p
        c_ref[1, pl.ds(k, PACKED, stride=8), :] = q
        prev_ref[0, pl.ds(k + 1, PACKED, stride=8), :] = p
        prev_ref[1, pl.ds(k + 1, PACKED, stride=8), :] = q

    ps, qs = tiles_from(prev_ref, 0), tiles_from(prev_ref, 1)
    for j in range(FACTOR):
        ps, qs = phi_tiles(ps, qs, weight_of)
        if j == FACTOR - 1:
            copies = [
                pltpu.make_async_copy(o_ref.at[pl.ds(k * STRIDE, 224)], out_ref.at[pl.ds(k * 256, 224)], sems.at[k])
                for k in range(FACTOR)
            ]
            for copy in copies:
                copy.start()
        for t in range(LISTED):
            ps[t] = ps[t] + load_forcing(f_ref, halo_ref, j, t, 0)
            qs[t] = qs[t] + load_forcing(f_ref, halo_ref, j, t, 1)
            if j < FACTOR - 1 and t < TILES:
                o_ref[pl.ds(j * 32 + t * 2, 8, stride=STRIDE), :] = ps[t]
                o_ref[pl.ds(j * 32 + t * 2 + 1, 8, stride=STRIDE), :] = qs[t]
    for t, row in spots():
        r1b_ref[0, tile_rows(row), :] = ps[t] - c_ref[0, tile_rows(row), :]
        r1b_ref[1, tile_rows(row), :] = qs[t] - c_ref[1, tile_rows(row), :]

    def finish(k, p, q):
        for field, x in enumerate((p, q)):
            done = c_ref[field, pl.ds(k, PACKED, stride=8), :] + x
            o_ref[pl.ds(k * STRIDE + 224 + field, TILES, stride=2), :] = done[0:TILES]
        copy = pltpu.make_async_copy(
            o_ref.at[pl.ds(k * STRIDE + 224, 32)], out_ref.at[pl.ds(k * 256 + 224, 32)], sems.at[FACTOR + k]
        )
        copy.start()
        copies.append(copy)

    p, q = d_ref[2], d_ref[3]
    last_p, last_q = apply2(p, q, w2)
    mp = mq = None
    for k in range(FACTOR):
        rp, rq = r1b_ref[0, pl.ds(k, PACKED, stride=8), :], r1b_ref[1, pl.ds(k, PACKED, stride=8), :]
        if k == 0:
            mp, mq = rp, rq
        else:
            mp, mq = phi_packed(mp, mq, w1)
            mp, mq = mp + rp, mq + rq
        if k < FACTOR - 1:
            p, q = phi_packed(p, q, w1)
            p, q = p + rp, q + rq
            finish(k, p, q)
    finish(FACTOR - 1, last_p + mp, last_q + mq)
    for copy in copies:
        copy.wait()


VMEM = pl.BlockSpec(memory_space=pltpu.VMEM)
SMEM = pl.BlockSpec(memory_space=pltpu.SMEM)
STATE = (2, PACKED * 8, LANES)


def shaped(*shape):
    return jax.ShapeDtypeStruct(shape, jnp.float32)


def scratch(*shape):
    return pltpu.VMEM(shape, jnp.float32)


ANY = pl.BlockSpec(memory_space=pl.ANY)
HBM = pl.BlockSpec(memory_space=pltpu.HBM)
SMALL = pltpu.CompilerParams(vmem_limit_bytes=8 << 20)
DENSE = pltpu.CompilerParams(vmem_limit_bytes=8 << 20)


def edge_stage(flat, friction, compressor):
    return pl.pallas_call(
        edge_kernel,
        out_shape=(shaped(PADDED, LANES), shaped(EDGE_ROWS, LANES), shaped(EDGE_ROWS, LANES), shaped(TILES, LANES)),
        in_specs=[HBM] * 3,
        out_specs=(VMEM,) * 4,
        scratch_shapes=[pltpu.VMEM((TILES, LANES), jnp.int32)] * 2 + [pltpu.SemaphoreType.DMA((FACTOR + 2,))],
        compiler_params=SMALL,
        name="edge",
    )(flat, friction, compressor)


PREPARED = (shaped(20, 8, LANES), shaped(2 * LANES, 2 * LANES))
PREPARING = [
    scratch(2 * LANES, 2 * LANES),
    scratch((FACTOR + 1) * GROUPS * 8, 2 * LANES),
    scratch(FACTOR * GROUPS * 8, 2 * LANES),
]


def first_stage(place, blocks, padded, right, left, kinds):
    return pl.pallas_call(
        first_kernel,
        out_shape=(shaped(*STATE), shaped(2, PACKED, LANES), shaped(12, PACKED, LANES), shaped(PACKED, LANES), shaped(2 * WINDOWS, LANES), shaped(128, LANES), *PREPARED),
        in_specs=[SMEM] * 2 + [VMEM] * 4,
        out_specs=(VMEM,) * 8,
        scratch_shapes=[scratch(*STATE)] * 3 + [scratch(2 * WINDOWS, LANES)] + PREPARING,
        compiler_params=DENSE,
        name="first",
    )(place, blocks, padded, right, left, kinds)


def prepare_stage(place, blocks, kinds, scan, dense):
    return pl.pallas_call(
        prepare_kernel,
        out_shape=PREPARED,
        in_specs=[SMEM, SMEM] + [VMEM] * 3,
        input_output_aliases={3: 0, 4: 1},
        out_specs=(VMEM, VMEM),
        scratch_shapes=PREPARING,
        compiler_params=DENSE,
        name="prepare",
    )(place, blocks, kinds, scan, dense)


def slab_stage(scan, dense, got):
    return pl.pallas_call(
        slab_kernel,
        out_shape=shaped(2 * WINDOWS, LANES),
        in_specs=[VMEM] * 3,
        out_specs=VMEM,
        scratch_shapes=[scratch(WINDOWS, 2 * LANES)] + [scratch(2 * WINDOWS, LANES)] * 2,
        compiler_params=SMALL,
        name="slab",
    )(scan, dense, got)


def last_stage(padded, halo, r1, r2, weights, got):
    return pl.pallas_call(
        last_kernel,
        out_shape=shaped(2048, LANES),
        in_specs=[VMEM] * 6,
        out_specs=ANY,
        scratch_shapes=[scratch(*STATE)] * 3
        + [scratch(4, PACKED, LANES), scratch(PADDED, LANES), scratch(2 * WINDOWS, LANES), pltpu.SemaphoreType.DMA((2 * FACTOR,))],
        compiler_params=DENSE,
        name="last",
    )(padded, halo, r1, r2, weights, got)


def to_rows(forcing):
    return forcing.reshape(64, 2, TILES, LANES).transpose(0, 2, 1, 3).reshape(2048, LANES)


def from_rows(rows):
    return rows.reshape(64, TILES, 2, LANES).transpose(0, 2, 1, 3).reshape(64, 2, TILES * LANES)


def transpose_windows(rows):
    return lax.all_to_all(rows.reshape(WINDOWS, 2, LANES), "tm", 0, 0, axis_index_groups=[ORDER]).reshape(2 * WINDOWS, LANES)


def per_device(forcing, friction_class, compressor, blocks):
    flat = to_rows(forcing)
    friction = friction_class.reshape(TILES, LANES)
    station = compressor.reshape(TILES, LANES)
    count = lax.axis_size("net")
    flat, friction, station = (pltpu.with_memory_space_constraint(x, pltpu.HBM) for x in (flat, friction, station))
    padded, low, high, kinds = edge_stage(flat, friction, station)
    left = lax.ppermute(high, "net", [(i, i + 1) for i in range(count - 1)])
    right = lax.ppermute(low, "net", [(i + 1, i) for i in range(count - 1)])
    place = lax.axis_index("tm").astype(jnp.int32).reshape(1)
    r1, r2, weights, kinds_wide, send, halo, scan, dense = first_stage(place, blocks, padded, right, left, kinds)
    got = transpose_windows(send)
    scan, dense = prepare_stage(place, blocks, kinds_wide, scan, dense)
    got = transpose_windows(slab_stage(scan, dense, got))
    return from_rows(last_stage(padded, halo, r1, r2, weights, got))


def solution(mesh):
    placed = (P("tm", None, "net"), P("net"), P("net"), P())
    return jax.shard_map(
        per_device, mesh=mesh, in_specs=placed, out_specs=P("tm", None, "net"), check_vma=False
    )
```

```python
import jax
import jax.numpy as jnp
from jax import lax
from jax.experimental import pallas as pl
from jax.experimental.pallas import tpu as pltpu
from jax.sharding import PartitionSpec as P

FACTOR = 8
KINDS = 9
LANES = 128
TILES = 16
WINDOWS = 64
PACKED = 24
RIGHT = 16
LEFT = 23
EDGE_ROWS = 72
STRIDE = 264
PADDED = FACTOR * STRIDE
HALF = LANES // 2
LISTED = TILES + 1
PREV = [TILES] + list(range(TILES))
NEXT = list(range(1, TILES + 1)) + [0]
MEET = 40
ORDER = [(MEET + rank) % WINDOWS for rank in range(WINDOWS)]
SLAB = 32
REACH = 22
SPAN = 84
COMB = 48
GROUPS = 2 * COMB // 8
TEETH = 24


def runs():
    found = []
    for rank, member in enumerate(ORDER):
        if found and found[-1][1] + found[-1][2] == member:
            found[-1][2] += 1
        else:
            found.append([rank, member, 1])
    return found


def by_rank(to_ref, from_ref):
    for rank, member, length in runs():
        to_ref[2 * rank : 2 * (rank + length), :] = from_ref[2 * member : 2 * (member + length), :]


def by_member(to_ref, from_ref):
    for rank, member, length in runs():
        to_ref[2 * member : 2 * (member + length), :] = from_ref[2 * rank : 2 * (rank + length), :]


def lanes_of(shape):
    return lax.broadcasted_iota(jnp.int32, shape, len(shape) - 1)


def couple(p, q, p_low, p_high, q_low, q_high, w):
    mixed_p = (p + p) + (q_high - q_low)
    mixed_q = (q + q) + (p_low - p_high)
    return w[0] * mixed_p + w[1] * mixed_q, w[2] * mixed_p + w[3] * mixed_q


def apply2(p, q, w):
    return w[0] * p + w[1] * q, w[2] * p + w[3] * q


def phi_tiles(ps, qs, weight_of, before=PREV, behind=NEXT):
    lane = lanes_of((8, LANES))
    first, last = lane == 0, lane == LANES - 1

    def low(xs, t):
        return pltpu.roll(jnp.where(last, xs[before[t]], xs[t]), 1, 1)

    def high(xs, t):
        return pltpu.roll(jnp.where(first, xs[behind[t]], xs[t]), LANES - 1, 1)

    new_p, new_q = [], []
    for t in range(len(ps)):
        p, q = couple(ps[t], qs[t], low(ps, t), high(ps, t), low(qs, t), high(qs, t), weight_of(t))
        new_p.append(p)
        new_q.append(q)
    return new_p, new_q


def phi_packed(p, q, w):
    lane = lanes_of((PACKED, LANES))
    first, last = lane == 0, lane == LANES - 1

    def low(x):
        return pltpu.roll(jnp.where(last, pltpu.roll(x, 1, 0), x), 1, 1)

    def high(x):
        return pltpu.roll(jnp.where(first, pltpu.roll(x, PACKED - 1, 0), x), LANES - 1, 1)

    return couple(p, q, low(p), high(p), low(q), high(q), w)


def phi_slab(p, q, w):
    return couple(
        p, q, pltpu.roll(p, 1, 1), pltpu.roll(p, LANES - 1, 1), pltpu.roll(q, 1, 1), pltpu.roll(q, LANES - 1, 1), w
    )


def pick(blocks_ref, number, kind):
    scale = 1.0 if number == 2 else 0.25
    masks = [kind == float(k + 1) for k in range(KINDS)]
    picked = []
    for entry in range(4):
        chosen = jnp.zeros_like(kind)
        for k in range(KINDS):
            chosen = jnp.where(masks[k], blocks_ref[number, entry // 2, entry % 2, k] * scale, chosen)
        picked.append(chosen)
    return picked


def load_forcing(f_ref, halo_ref, j, t, field):
    if t < TILES:
        return f_ref[pl.ds(j * 32 + t * 2 + field, 8, stride=STRIDE), :]
    return halo_ref[pl.ds((j * 2 + field) * 8, 8), :]


def tile_rows(row):
    return pl.ds(row * 8, 8)


def tiles_from(ref, field):
    both = jnp.where(lanes_of((8, LANES)) < HALF, ref[field, tile_rows(RIGHT), :], ref[field, tile_rows(LEFT), :])
    return [ref[field, tile_rows(t), :] for t in range(TILES)] + [both]


def spots():
    return [(t, t) for t in range(TILES)] + [(TILES, RIGHT), (TILES, LEFT)]


def fine_weights(w_ref):
    def weight_of(t):
        return [jnp.broadcast_to(w_ref[e, t : t + 1, :], (8, LANES)) for e in range(4)]

    return weight_of


def edge_kernel(source_ref, fc_hbm, comp_hbm, f_ref, low_ref, high_ref, kind_ref, fc_ref, comp_ref, sems):
    copies = [
        pltpu.make_async_copy(source_ref.at[pl.ds(k * 256, 256)], f_ref.at[pl.ds(k * STRIDE, 256)], sems.at[k])
        for k in range(FACTOR)
    ]
    labels = [
        pltpu.make_async_copy(fc_hbm, fc_ref, sems.at[FACTOR]),
        pltpu.make_async_copy(comp_hbm, comp_ref, sems.at[FACTOR + 1]),
    ]
    for copy in labels + copies:
        copy.start()
    for copy in labels:
        copy.wait()
    kinds = jnp.where(comp_ref[...] == 1, KINDS, fc_ref[...] + 1).astype(jnp.float32)
    kind_ref[...] = kinds
    low_ref[64:EDGE_ROWS, :] = jnp.broadcast_to(kinds[0:1], (8, LANES))
    high_ref[64:EDGE_ROWS, :] = jnp.broadcast_to(kinds[TILES - 1 : TILES], (8, LANES))
    left_half = lanes_of((8, LANES)) < HALF
    for copy in copies:
        copy.wait()
    for j in range(FACTOR):
        rows = pl.ds(j * 8, 8)
        p, q = (f_ref[pl.ds(j * 32 + field, 8, stride=STRIDE), :] for field in range(2))
        low_ref[rows, :] = jnp.where(left_half, p, pltpu.roll(q, HALF, 1))
        p, q = (f_ref[pl.ds(j * 32 + 2 * (TILES - 1) + field, 8, stride=STRIDE), :] for field in range(2))
        high_ref[rows, :] = jnp.where(left_half, pltpu.roll(q, HALF, 1), p)


def fine_weights_at(w_ref, rows):
    def weight_of(t):
        return [jnp.broadcast_to(w_ref[e, rows[t] : rows[t] + 1, :], (8, LANES)) for e in range(4)]

    return weight_of


def relax_from_zero(f_ref, halo_ref, w_ref, tiles, before, behind):
    weight_of = fine_weights_at(w_ref, tiles)
    ps, qs = ([load_forcing(f_ref, halo_ref, 0, t, field) for t in tiles] for field in range(2))
    for j in range(1, FACTOR):
        ps, qs = phi_tiles(ps, qs, weight_of, before, behind)
        ps = [x + load_forcing(f_ref, halo_ref, j, t, 0) for x, t in zip(ps, tiles)]
        qs = [x + load_forcing(f_ref, halo_ref, j, t, 1) for x, t in zip(qs, tiles)]
    return ps, qs


def main_kernel(blocks_ref, f_ref, kind_ref, r1_ref, w_ref):
    kind = kind_ref[...]
    for number in range(3):
        for entry, chosen in enumerate(pick(blocks_ref, number, kind)):
            w_ref[number * 4 + entry, 0:TILES, :] = chosen
    tiles = list(range(TILES))
    before, behind = [(t - 1) % TILES for t in tiles], [(t + 1) % TILES for t in tiles]
    ps, qs = relax_from_zero(f_ref, None, w_ref, tiles, before, behind)
    for t in tiles:
        r1_ref[0, tile_rows(t), :] = ps[t]
        r1_ref[1, tile_rows(t), :] = qs[t]


def first_kernel(blocks_ref, f_ref, right_ref, left_ref, kind_ref, r1_in, w_in, r1_ref, w_ref, r2_ref, kx_ref, send_ref,
                 halo_ref, prev_ref, c_ref, r1b_ref, nat_ref):
    kx_ref[0:TILES, :] = kind_ref[...]
    kx_ref[TILES:PACKED, :] = jnp.zeros((PACKED - TILES, LANES), jnp.float32)
    beyond = jnp.where(lanes_of((1, LANES)) < HALF, right_ref[64:65, :], left_ref[64:65, :])
    kx_ref[RIGHT : RIGHT + 1, :] = beyond
    kx_ref[LEFT : LEFT + 1, :] = beyond
    kind = kx_ref[TILES:PACKED, :]
    for number in range(3):
        for entry, chosen in enumerate(pick(blocks_ref, number, kind)):
            w_ref[number * 4 + entry, TILES:PACKED, :] = chosen
    weight_of = fine_weights(w_ref)
    w1 = [w_ref[4 + e] for e in range(4)]

    left_half = lanes_of((8, LANES)) < HALF
    for j in range(FACTOR):
        x, y = right_ref[pl.ds(j * 8, 8), :], left_ref[pl.ds(j * 8, 8), :]
        halo_ref[pl.ds(j * 16, 8), :] = jnp.where(left_half, x, y)
        halo_ref[pl.ds(j * 16 + 8, 8), :] = pltpu.roll(jnp.where(left_half, y, x), HALF, 1)

    unused = jnp.zeros(((LEFT - RIGHT - 1) * 8, LANES), jnp.float32)
    for field in range(2):
        for ref in (r1_ref, r1b_ref):
            ref[field, (RIGHT + 1) * 8 : LEFT * 8, :] = unused

    strip = [TILES - 2, TILES - 1, TILES, 0, 1]
    ps, qs = relax_from_zero(f_ref, halo_ref, w_ref, strip, [0, 0, 1, 2, 3], [1, 2, 3, 4, 4])
    for at, row in ((1, TILES - 1), (2, RIGHT), (2, LEFT), (3, 0)):
        r1_ref[0, tile_rows(row), :] = ps[at]
        r1_ref[1, tile_rows(row), :] = qs[at]

    def sweep(ref, keep):
        p = q = None
        for k in range(FACTOR):
            rp, rq = ref[0, pl.ds(k, PACKED, stride=8), :], ref[1, pl.ds(k, PACKED, stride=8), :]
            if k == 0:
                p, q = rp, rq
            else:
                p, q = phi_packed(p, q, w1)
                p, q = p + rp, q + rq
            if keep:
                c_ref[0, pl.ds(k, PACKED, stride=8), :] = p
                c_ref[1, pl.ds(k, PACKED, stride=8), :] = q
                if k < FACTOR - 1:
                    prev_ref[0, pl.ds(k + 1, PACKED, stride=8), :] = p
                    prev_ref[1, pl.ds(k + 1, PACKED, stride=8), :] = q
        return p, q

    nothing = jnp.zeros((PACKED, LANES), jnp.float32)
    prev_ref[0, pl.ds(0, PACKED, stride=8), :] = nothing
    prev_ref[1, pl.ds(0, PACKED, stride=8), :] = nothing
    r2p, r2q = sweep(r1_ref, True)
    r2_ref[0] = r2p
    r2_ref[1] = r2q

    ps, qs = tiles_from(prev_ref, 0), tiles_from(prev_ref, 1)
    for j in range(FACTOR):
        ps, qs = phi_tiles(ps, qs, weight_of)
    for field, xs in enumerate((ps, qs)):
        for t, row in spots():
            rows = tile_rows(row)
            r1b_ref[field, rows, :] = xs[t] + (r1_ref[field, rows, :] - c_ref[field, rows, :])
    gp, gq = sweep(r1b_ref, False)

    lane = lanes_of((8, LANES))
    for c, (x, g) in enumerate(((r2p, gp), (r2q, gq))):
        for half in range(2):
            shifted = [
                [y[8 * half : 8 * half + 8] for y in (pltpu.roll(z, 1, 0), z, pltpu.roll(z, PACKED - 1, 0))]
                for z in (x, g)
            ]

            def window(which, offset):
                a, b = shifted[which][0:2] if offset < 0 else shifted[which][1:3]
                start = offset % LANES
                return pltpu.roll(jnp.where(lane >= start, a, b), (LANES - start) % LANES, 1)

            for quarter in range(4):
                origin = SLAB * quarter
                near = window(0, origin + window_start(half))
                far = window(1, origin + share_start(half) - SPAN)
                nat_ref[pl.ds(64 * half + 2 * quarter + c, 8, stride=8), :] = jnp.where(lane < SPAN, near, far)
    by_rank(send_ref, nat_ref)


def window_start(half):
    return -REACH if half else -REACH - 8


def share_start(half):
    return 0 if half else -8


def prepare_kernel(place_ref, blocks_ref, kx_ref, scan_ref, dense_ref, fine_ref, states_ref, after_ref):
    place = place_ref[0]
    lane1 = lanes_of((1, LANES))
    origin = place * SLAB + (LANES - REACH - 8) + jnp.where(place >= WINDOWS // 2, 8, 0)
    base = origin // LANES - 1
    start = origin % LANES
    base = jnp.where(base < 0, LEFT, base)
    after = jnp.where(base == LEFT, 0, base + 1)
    a, b = kx_ref[pl.ds(base, 1), :], kx_ref[pl.ds(after, 1), :]
    kind = pltpu.roll(jnp.where(lane1 >= start, a, b), LANES - start, 1)
    kind = jnp.broadcast_to(kind, (8, LANES))
    w0, w1, w2 = (pick(blocks_ref, number, kind) for number in range(3))
    sub = lax.broadcasted_iota(jnp.int32, (8, LANES), 0)
    lane = lanes_of((8, LANES))

    def times(v, w):
        return [
            v[0] * w[0] + v[1] * w[2],
            v[0] * w[1] + v[1] * w[3],
            v[2] * w[0] + v[3] * w[2],
            v[2] * w[1] + v[3] * w[3],
        ]

    one, none = jnp.ones((8, LANES), jnp.float32), jnp.zeros((8, LANES), jnp.float32)
    w = w2
    grown = [one, none, none, one]
    for n, step in enumerate((1, 2, 4)):
        longer = times(grown, w)
        grown = [jnp.where((sub & step) != 0, x, y) for x, y in zip(longer, grown)]
        for e in range(4):
            scan_ref[4 * n + e] = jnp.where(sub >= step, w[e], 0.0)
        w = times(w, w)
    for e in range(4):
        scan_ref[12 + e] = w[e]
        scan_ref[16 + e] = grown[e]

    def combs(gap, teeth):
        made = []
        for n in range(gap // 8):
            hit = lane == sub + 8 * n
            for tooth in range(1, teeth):
                hit = hit | (lane == sub + (8 * n + gap * tooth))
            made.append(jnp.where(hit, 1.0, 0.0))
        blank = [none] * len(made)
        return made + blank, blank + made

    def spread(answers, ref, gap, teeth, reach):
        for n, answer in enumerate(answers):
            field, c = divmod(n, gap // 8)
            for tooth in range(teeth):
                at = sub + (8 * c + gap * tooth)
                near = (lane - at <= reach) & (at - lane <= reach)
                rows = pl.ds(field * LANES + gap * tooth + 8 * c, 8)
                for to in range(2):
                    ref[rows, LANES * to : LANES * (to + 1)] = jnp.where(near, answer[to], 0.0)
        for field in range(2):
            ref[field * LANES + gap * teeth : (field + 1) * LANES, :] = jnp.zeros((LANES - gap * teeth, 2 * LANES), jnp.float32)

    answers = list(zip(*combs(TEETH, 4)))
    for _ in range(FACTOR):
        answers = [phi_slab(p, q, w0) for p, q in answers]
    spread(answers, fine_ref, TEETH, 4, FACTOR)

    def rows_of(k, n):
        return pl.ds((k * GROUPS + n) * 8, 8)

    begin = list(zip(*combs(COMB, 2)))
    states = begin
    for k in range(FACTOR + 1):
        for n, (p, q) in enumerate(states):
            states_ref[rows_of(k, n), 0:LANES] = p
            states_ref[rows_of(k, n), LANES : 2 * LANES] = q
        if k < FACTOR:
            states = [phi_slab(p, q, w1) for p, q in states]
    after_ref[...] = jnp.dot(
        states_ref[0 : FACTOR * GROUPS * 8, :],
        fine_ref[...],
        precision=lax.Precision.HIGHEST,
        preferred_element_type=jnp.float32,
    )

    def residual(k, n):
        return [
            after_ref[rows_of(k, n), LANES * to : LANES * (to + 1)]
            - states_ref[rows_of(k + 1, n), LANES * to : LANES * (to + 1)]
            for to in range(2)
        ]

    m = [residual(0, n) for n in range(GROUPS)]
    for k in range(1, FACTOR):
        stepped = [phi_slab(p, q, w1) for p, q in m]
        m = [[x + y for x, y in zip(stepped[n], residual(k, n))] for n in range(GROUPS)]

    total = []
    for n in range(GROUPS):
        coarse = apply2(*begin[n], w2)
        total.append([m[n][to] + (states[n][to] - coarse[to]) for to in range(2)])
    spread(total, dense_ref, COMB, 2, REACH)


def slab_kernel(scan_ref, dense_ref, ranked_ref, send_ref, d_ref, got_ref, nat_ref):
    by_member(got_ref, ranked_ref)
    lane = lanes_of((8, LANES))
    masked = [[scan_ref[4 * n + e] for e in range(4)] for n in range(3)]
    w_eight = [scan_ref[12 + e] for e in range(4)]
    grown = [scan_ref[16 + e] for e in range(4)]
    first = lax.broadcasted_iota(jnp.int32, (8, LANES), 0) == 0

    def recurrence(rp, rq):
        yp, yq = list(rp), list(rq)
        for n, step in enumerate((1, 2, 4)):
            for b in range(8):
                sp, sq = apply2(pltpu.roll(yp[b], step, 0), pltpu.roll(yq[b], step, 0), masked[n])
                yp[b], yq[b] = yp[b] + sp, yq[b] + sq
        dp, dq = [], []
        tp = tq = None
        for b in range(8):
            bp, bq = pltpu.roll(yp[b], 1, 0), pltpu.roll(yq[b], 1, 0)
            bp, bq = jnp.where(first, 0.0, bp), jnp.where(first, 0.0, bq)
            ep, eq = yp[b][7:8], yq[b][7:8]
            ep, eq = jnp.broadcast_to(ep, (8, LANES)), jnp.broadcast_to(eq, (8, LANES))
            if b:
                sp, sq = apply2(tp, tq, grown)
                bp, bq = bp + sp, bq + sq
                sp, sq = apply2(tp, tq, w_eight)
                ep, eq = ep + sp, eq + sq
            tp, tq = ep, eq
            dp.append(bp)
            dq.append(bq)
        return dp, dq

    def rows(b, c):
        return pl.ds(b * 16 + c, 8, stride=2)

    gotten = [[got_ref[rows(b, c), :] for b in range(8)] for c in range(2)]
    dp, dq = recurrence(*gotten)
    for b in range(8):
        d_ref[8 * b : 8 * b + 8, 0:LANES] = dp[b]
        d_ref[8 * b : 8 * b + 8, LANES : 2 * LANES] = dq[b]
    answer = jnp.dot(d_ref[...], dense_ref[...], precision=lax.Precision.HIGHEST, preferred_element_type=jnp.float32)
    back = SPAN - REACH
    residual = [
        [
            answer[8 * b : 8 * b + 8, LANES * c : LANES * (c + 1)] + pltpu.roll(gotten[c][b], LANES - back, 1)
            for b in range(8)
        ]
        for c in range(2)
    ]
    ep, eq = recurrence(*residual)
    for b in range(8):
        nat_ref[rows(b, 0), :] = jnp.where(lane < SPAN, dp[b], pltpu.roll(ep[b], back, 1))
        nat_ref[rows(b, 1), :] = jnp.where(lane < SPAN, dq[b], pltpu.roll(eq[b], back, 1))
    by_rank(send_ref, nat_ref)


def last_kernel(f_ref, halo_ref, r1_ref, r2_ref, w_ref, ranked_ref, out_ref, prev_ref, c_ref, r1b_ref, d_ref,
                o_ref, got_ref, sems):
    by_member(got_ref, ranked_ref)

    lane = lanes_of((8, LANES))
    lane1 = lanes_of((1, LANES))
    for c in range(2):
        for cycle in range(2):
            for half in range(2):
                begin = (SPAN - share_start(half)) if cycle else -window_start(half)
                whole = jnp.zeros((8, LANES), jnp.float32)
                for quarter in range(4):
                    piece = got_ref[pl.ds(64 * half + 2 * quarter + c, 8, stride=8), :]
                    piece = pltpu.roll(piece, (SLAB * quarter - begin) % LANES, 1)
                    mine = (lane >= SLAB * quarter) & (lane < SLAB * (quarter + 1))
                    whole = jnp.where(mine, piece, whole)
                d_ref[2 * cycle + c, 8 * half : 8 * half + 8, :] = whole
            d_ref[2 * cycle + c, TILES:PACKED, :] = jnp.zeros((PACKED - TILES, LANES), jnp.float32)
            width = 8 if cycle else 24
            begin = (SPAN - share_start(0)) if cycle else -window_start(0)
            low = pltpu.roll(got_ref[c : c + 1, :], LANES - begin, 1)
            d_ref[2 * cycle + c, LEFT : LEFT + 1, :] = jnp.where(lane1 >= LANES - width, low, 0.0)
            begin = (SPAN - share_start(1)) if cycle else -window_start(1)
            end = (WINDOWS - 1) * 2 + c
            high = pltpu.roll(got_ref[end : end + 1, :], LANES - begin - SLAB, 1)
            d_ref[2 * cycle + c, RIGHT : RIGHT + 1, :] = jnp.where(lane1 < width, high, 0.0)

    weight_of = fine_weights(w_ref)
    w1 = [w_ref[4 + e] for e in range(4)]
    w2 = [w_ref[8 + e] for e in range(4)]
    unused = jnp.zeros(((LEFT - RIGHT - 1) * 8, LANES), jnp.float32)
    for field in range(2):
        r1b_ref[field, (RIGHT + 1) * 8 : LEFT * 8, :] = unused

    p, q = d_ref[0], d_ref[1]
    last_p, last_q = apply2(p, q, w2)
    c_ref[0, pl.ds(FACTOR - 1, PACKED, stride=8), :] = last_p + r2_ref[0]
    c_ref[1, pl.ds(FACTOR - 1, PACKED, stride=8), :] = last_q + r2_ref[1]
    prev_ref[0, pl.ds(0, PACKED, stride=8), :] = p
    prev_ref[1, pl.ds(0, PACKED, stride=8), :] = q
    for k in range(FACTOR - 1):
        p, q = phi_packed(p, q, w1)
        p = p + r1_ref[0, pl.ds(k, PACKED, stride=8), :]
        q = q + r1_ref[1, pl.ds(k, PACKED, stride=8), :]
        c_ref[0, pl.ds(k, PACKED, stride=8), :] = p
        c_ref[1, pl.ds(k, PACKED, stride=8), :] = q
        prev_ref[0, pl.ds(k + 1, PACKED, stride=8), :] = p
        prev_ref[1, pl.ds(k + 1, PACKED, stride=8), :] = q

    ps, qs = tiles_from(prev_ref, 0), tiles_from(prev_ref, 1)
    for j in range(FACTOR):
        ps, qs = phi_tiles(ps, qs, weight_of)
        if j == FACTOR - 1:
            copies = [
                pltpu.make_async_copy(o_ref.at[pl.ds(k * STRIDE, 224)], out_ref.at[pl.ds(k * 256, 224)], sems.at[k])
                for k in range(FACTOR)
            ]
            for copy in copies:
                copy.start()
        for t in range(LISTED):
            ps[t] = ps[t] + load_forcing(f_ref, halo_ref, j, t, 0)
            qs[t] = qs[t] + load_forcing(f_ref, halo_ref, j, t, 1)
            if j < FACTOR - 1 and t < TILES:
                o_ref[pl.ds(j * 32 + t * 2, 8, stride=STRIDE), :] = ps[t]
                o_ref[pl.ds(j * 32 + t * 2 + 1, 8, stride=STRIDE), :] = qs[t]
    for t, row in spots():
        r1b_ref[0, tile_rows(row), :] = ps[t] - c_ref[0, tile_rows(row), :]
        r1b_ref[1, tile_rows(row), :] = qs[t] - c_ref[1, tile_rows(row), :]

    def finish(k, p, q):
        for field, x in enumerate((p, q)):
            done = c_ref[field, pl.ds(k, PACKED, stride=8), :] + x
            o_ref[pl.ds(k * STRIDE + 224 + field, TILES, stride=2), :] = done[0:TILES]
        copy = pltpu.make_async_copy(
            o_ref.at[pl.ds(k * STRIDE + 224, 32)], out_ref.at[pl.ds(k * 256 + 224, 32)], sems.at[FACTOR + k]
        )
        copy.start()
        copies.append(copy)

    p, q = d_ref[2], d_ref[3]
    last_p, last_q = apply2(p, q, w2)
    mp = mq = None
    for k in range(FACTOR):
        rp, rq = r1b_ref[0, pl.ds(k, PACKED, stride=8), :], r1b_ref[1, pl.ds(k, PACKED, stride=8), :]
        if k == 0:
            mp, mq = rp, rq
        else:
            mp, mq = phi_packed(mp, mq, w1)
            mp, mq = mp + rp, mq + rq
        if k < FACTOR - 1:
            p, q = phi_packed(p, q, w1)
            p, q = p + rp, q + rq
            finish(k, p, q)
    finish(FACTOR - 1, last_p + mp, last_q + mq)
    for copy in copies:
        copy.wait()


VMEM = pl.BlockSpec(memory_space=pltpu.VMEM)
SMEM = pl.BlockSpec(memory_space=pltpu.SMEM)
STATE = (2, PACKED * 8, LANES)


def shaped(*shape):
    return jax.ShapeDtypeStruct(shape, jnp.float32)


def scratch(*shape):
    return pltpu.VMEM(shape, jnp.float32)


ANY = pl.BlockSpec(memory_space=pl.ANY)
HBM = pl.BlockSpec(memory_space=pltpu.HBM)
SMALL = pltpu.CompilerParams(vmem_limit_bytes=8 << 20)
DENSE = pltpu.CompilerParams(vmem_limit_bytes=8 << 20)


def edge_stage(flat, friction, compressor):
    return pl.pallas_call(
        edge_kernel,
        out_shape=(shaped(PADDED, LANES), shaped(EDGE_ROWS, LANES), shaped(EDGE_ROWS, LANES), shaped(TILES, LANES)),
        in_specs=[HBM] * 3,
        out_specs=(VMEM,) * 4,
        scratch_shapes=[pltpu.VMEM((TILES, LANES), jnp.int32)] * 2 + [pltpu.SemaphoreType.DMA((FACTOR + 2,))],
        compiler_params=SMALL,
        name="edge",
    )(flat, friction, compressor)


PREPARED = (shaped(20, 8, LANES), shaped(2 * LANES, 2 * LANES))
PREPARING = [
    scratch(2 * LANES, 2 * LANES),
    scratch((FACTOR + 1) * GROUPS * 8, 2 * LANES),
    scratch(FACTOR * GROUPS * 8, 2 * LANES),
]


def main_stage(blocks, padded, kinds):
    return pl.pallas_call(
        main_kernel,
        out_shape=(shaped(*STATE), shaped(12, PACKED, LANES)),
        in_specs=[SMEM, VMEM, VMEM],
        out_specs=(VMEM,) * 2,
        compiler_params=DENSE,
        name="main",
    )(blocks, padded, kinds)


def first_stage(blocks, padded, right, left, kinds, r1, weights):
    return pl.pallas_call(
        first_kernel,
        out_shape=(
            shaped(*STATE),
            shaped(12, PACKED, LANES),
            shaped(2, PACKED, LANES),
            shaped(PACKED, LANES),
            shaped(2 * WINDOWS, LANES),
            shaped(128, LANES),
        ),
        in_specs=[SMEM] + [VMEM] * 6,
        out_specs=(VMEM,) * 6,
        input_output_aliases={5: 0, 6: 1},
        scratch_shapes=[scratch(*STATE)] * 3 + [scratch(2 * WINDOWS, LANES)],
        compiler_params=DENSE,
        name="first",
    )(blocks, padded, right, left, kinds, r1, weights)


def prepare_stage(place, blocks, kinds):
    return pl.pallas_call(
        prepare_kernel,
        out_shape=PREPARED,
        in_specs=[SMEM, SMEM, VMEM],
        out_specs=(VMEM, VMEM),
        scratch_shapes=PREPARING,
        compiler_params=DENSE,
        name="prepare",
    )(place, blocks, kinds)


def slab_stage(scan, dense, got):
    return pl.pallas_call(
        slab_kernel,
        out_shape=shaped(2 * WINDOWS, LANES),
        in_specs=[VMEM] * 3,
        out_specs=VMEM,
        scratch_shapes=[scratch(WINDOWS, 2 * LANES)] + [scratch(2 * WINDOWS, LANES)] * 2,
        compiler_params=SMALL,
        name="slab",
    )(scan, dense, got)


def last_stage(padded, halo, r1, r2, weights, got):
    return pl.pallas_call(
        last_kernel,
        out_shape=shaped(2048, LANES),
        in_specs=[VMEM] * 6,
        out_specs=ANY,
        scratch_shapes=[scratch(*STATE)] * 3
        + [scratch(4, PACKED, LANES), scratch(PADDED, LANES), scratch(2 * WINDOWS, LANES), pltpu.SemaphoreType.DMA((2 * FACTOR,))],
        compiler_params=DENSE,
        name="last",
    )(padded, halo, r1, r2, weights, got)


def to_rows(forcing):
    return forcing.reshape(64, 2, TILES, LANES).transpose(0, 2, 1, 3).reshape(2048, LANES)


def from_rows(rows):
    return rows.reshape(64, TILES, 2, LANES).transpose(0, 2, 1, 3).reshape(64, 2, TILES * LANES)


def transpose_windows(rows):
    return lax.all_to_all(rows.reshape(WINDOWS, 2, LANES), "tm", 0, 0, axis_index_groups=[ORDER]).reshape(2 * WINDOWS, LANES)


def per_device(forcing, friction_class, compressor, blocks):
    flat = to_rows(forcing)
    friction = friction_class.reshape(TILES, LANES)
    station = compressor.reshape(TILES, LANES)
    count = lax.axis_size("net")
    flat, friction, station = (pltpu.with_memory_space_constraint(x, pltpu.HBM) for x in (flat, friction, station))
    padded, low, high, kinds = edge_stage(flat, friction, station)
    left = lax.ppermute(high, "net", [(i, i + 1) for i in range(count - 1)])
    right = lax.ppermute(low, "net", [(i + 1, i) for i in range(count - 1)])
    r1, weights = main_stage(blocks, padded, kinds)
    r1, weights, r2, kinds_wide, send, halo = first_stage(blocks, padded, right, left, kinds, r1, weights)
    got = transpose_windows(send)
    place = lax.axis_index("tm").astype(jnp.int32).reshape(1)
    scan, dense = prepare_stage(place, blocks, kinds_wide)
    got = transpose_windows(slab_stage(scan, dense, got))
    return from_rows(last_stage(padded, halo, r1, r2, weights, got))


def solution(mesh):
    placed = (P("tm", None, "net"), P("net"), P("net"), P())
    return jax.shard_map(
        per_device, mesh=mesh, in_specs=placed, out_specs=P("tm", None, "net"), check_vma=False
    )
```

```python
import jax
import jax.numpy as jnp
from jax import lax
from jax.experimental import pallas as pl
from jax.experimental.pallas import tpu as pltpu
from jax.sharding import PartitionSpec as P

FACTOR = 8
KINDS = 9
TABLE = 12 * KINDS
LANES = 128
TILES = 16
WINDOWS = 64
PACKED = 24
RIGHT = 16
LEFT = 23
EDGE_ROWS = 72
STRIDE = 264
PADDED = FACTOR * STRIDE
HALF = LANES // 2
LISTED = TILES + 1
PREV = [TILES] + list(range(TILES))
NEXT = list(range(1, TILES + 1)) + [0]
MEET = 40
ORDER = [(MEET + rank) % WINDOWS for rank in range(WINDOWS)]
SLAB = 32
REACH = 22
SPAN = 84
COMB = 48
GROUPS = 2 * COMB // 8
TEETH = 24


def runs():
    found = []
    for rank, member in enumerate(ORDER):
        if found and found[-1][1] + found[-1][2] == member:
            found[-1][2] += 1
        else:
            found.append([rank, member, 1])
    return found


def by_rank(to_ref, from_ref):
    for rank, member, length in runs():
        to_ref[2 * rank : 2 * (rank + length), :] = from_ref[2 * member : 2 * (member + length), :]


def by_member(to_ref, from_ref):
    for rank, member, length in runs():
        to_ref[2 * member : 2 * (member + length), :] = from_ref[2 * rank : 2 * (rank + length), :]


def lanes_of(shape):
    return lax.broadcasted_iota(jnp.int32, shape, len(shape) - 1)


def couple(p, q, p_low, p_high, q_low, q_high, w):
    mixed_p = (p + p) + (q_high - q_low)
    mixed_q = (q + q) + (p_low - p_high)
    return w[0] * mixed_p + w[1] * mixed_q, w[2] * mixed_p + w[3] * mixed_q


def apply2(p, q, w):
    return w[0] * p + w[1] * q, w[2] * p + w[3] * q


def phi_tiles(ps, qs, weight_of, before=PREV, behind=NEXT):
    lane = lanes_of((8, LANES))
    first, last = lane == 0, lane == LANES - 1

    def low(xs, t):
        return pltpu.roll(jnp.where(last, xs[before[t]], xs[t]), 1, 1)

    def high(xs, t):
        return pltpu.roll(jnp.where(first, xs[behind[t]], xs[t]), LANES - 1, 1)

    new_p, new_q = [], []
    for t in range(len(ps)):
        p, q = couple(ps[t], qs[t], low(ps, t), high(ps, t), low(qs, t), high(qs, t), weight_of(t))
        new_p.append(p)
        new_q.append(q)
    return new_p, new_q


def phi_packed(p, q, w):
    lane = lanes_of((PACKED, LANES))
    first, last = lane == 0, lane == LANES - 1

    def low(x):
        return pltpu.roll(jnp.where(last, pltpu.roll(x, 1, 0), x), 1, 1)

    def high(x):
        return pltpu.roll(jnp.where(first, pltpu.roll(x, PACKED - 1, 0), x), LANES - 1, 1)

    return couple(p, q, low(p), high(p), low(q), high(q), w)


def phi_slab(p, q, w):
    return couple(
        p, q, pltpu.roll(p, 1, 1), pltpu.roll(p, LANES - 1, 1), pltpu.roll(q, 1, 1), pltpu.roll(q, LANES - 1, 1), w
    )


def pick(table_ref, number, kind):
    masks = [kind == float(k + 1) for k in range(KINDS)]
    picked = []
    for entry in range(4):
        chosen = jnp.zeros_like(kind)
        for k in range(KINDS):
            choice = table_ref[(number * 4 + entry) * KINDS + k]
            if kind.shape[0] != 8:
                choice = jnp.concatenate([choice] * (kind.shape[0] // 8))
            chosen = jnp.where(masks[k], choice, chosen)
        picked.append(chosen)
    return picked


def load_forcing(f_ref, halo_ref, j, t, field):
    if t < TILES:
        return f_ref[pl.ds(j * 32 + t * 2 + field, 8, stride=STRIDE), :]
    return halo_ref[pl.ds((j * 2 + field) * 8, 8), :]


def tile_rows(row):
    return pl.ds(row * 8, 8)


def tiles_from(ref, field):
    both = jnp.where(lanes_of((8, LANES)) < HALF, ref[field, tile_rows(RIGHT), :], ref[field, tile_rows(LEFT), :])
    return [ref[field, tile_rows(t), :] for t in range(TILES)] + [both]


def spots():
    return [(t, t) for t in range(TILES)] + [(TILES, RIGHT), (TILES, LEFT)]


def fine_weights(w_ref):
    def weight_of(t):
        return [jnp.broadcast_to(w_ref[e, t : t + 1, :], (8, LANES)) for e in range(4)]

    return weight_of


def edge_kernel(source_ref, fc_hbm, comp_hbm, blocks_hbm, f_ref, low_ref, high_ref, kind_ref, table_ref, fc_ref, comp_ref,
                blocks_ref, sems):
    copies = [
        pltpu.make_async_copy(source_ref.at[pl.ds(k * 256, 256)], f_ref.at[pl.ds(k * STRIDE, 256)], sems.at[k])
        for k in range(FACTOR)
    ]
    labels = [
        pltpu.make_async_copy(fc_hbm, fc_ref, sems.at[FACTOR]),
        pltpu.make_async_copy(comp_hbm, comp_ref, sems.at[FACTOR + 1]),
        pltpu.make_async_copy(blocks_hbm, blocks_ref, sems.at[FACTOR + 2]),
    ]
    for copy in labels + copies:
        copy.start()
    for copy in labels:
        copy.wait()
    kinds = jnp.where(comp_ref[...] == 1, KINDS, fc_ref[...] + 1).astype(jnp.float32)
    kind_ref[...] = kinds
    low_ref[64:EDGE_ROWS, :] = jnp.broadcast_to(kinds[0:1], (8, LANES))
    high_ref[64:EDGE_ROWS, :] = jnp.broadcast_to(kinds[TILES - 1 : TILES], (8, LANES))
    for number in range(3):
        scale = 1.0 if number == 2 else 0.25
        for entry in range(4):
            for k in range(KINDS):
                value = blocks_ref[number, entry // 2, entry % 2, k] * scale
                table_ref[(number * 4 + entry) * KINDS + k] = jnp.full((8, LANES), value, jnp.float32)
    left_half = lanes_of((8, LANES)) < HALF
    for copy in copies:
        copy.wait()
    for j in range(FACTOR):
        rows = pl.ds(j * 8, 8)
        p, q = (f_ref[pl.ds(j * 32 + field, 8, stride=STRIDE), :] for field in range(2))
        low_ref[rows, :] = jnp.where(left_half, p, pltpu.roll(q, HALF, 1))
        p, q = (f_ref[pl.ds(j * 32 + 2 * (TILES - 1) + field, 8, stride=STRIDE), :] for field in range(2))
        high_ref[rows, :] = jnp.where(left_half, pltpu.roll(q, HALF, 1), p)


def fine_weights_at(w_ref, rows):
    def weight_of(t):
        return [jnp.broadcast_to(w_ref[e, rows[t] : rows[t] + 1, :], (8, LANES)) for e in range(4)]

    return weight_of


def relax_from_zero(f_ref, halo_ref, w_ref, tiles, before, behind):
    weight_of = fine_weights_at(w_ref, tiles)
    ps, qs = ([load_forcing(f_ref, halo_ref, 0, t, field) for t in tiles] for field in range(2))
    for j in range(1, FACTOR):
        ps, qs = phi_tiles(ps, qs, weight_of, before, behind)
        ps = [x + load_forcing(f_ref, halo_ref, j, t, 0) for x, t in zip(ps, tiles)]
        qs = [x + load_forcing(f_ref, halo_ref, j, t, 1) for x, t in zip(qs, tiles)]
    return ps, qs


def main_kernel(table_ref, f_ref, kind_ref, r1_ref, w_ref):
    kind = kind_ref[...]
    for number in range(3):
        for entry, chosen in enumerate(pick(table_ref, number, kind)):
            w_ref[number * 4 + entry, 0:TILES, :] = chosen
    tiles = list(range(TILES))
    before, behind = [(t - 1) % TILES for t in tiles], [(t + 1) % TILES for t in tiles]
    ps, qs = relax_from_zero(f_ref, None, w_ref, tiles, before, behind)
    for t in tiles:
        r1_ref[0, tile_rows(t), :] = ps[t]
        r1_ref[1, tile_rows(t), :] = qs[t]


def first_kernel(table_ref, f_ref, right_ref, left_ref, kind_ref, r1_in, w_in, r1_ref, w_ref, r2_ref, kx_ref, send_ref,
                 halo_ref, prev_ref, c_ref, r1b_ref, nat_ref):
    kx_ref[0:TILES, :] = kind_ref[...]
    kx_ref[TILES:PACKED, :] = jnp.zeros((PACKED - TILES, LANES), jnp.float32)
    beyond = jnp.where(lanes_of((1, LANES)) < HALF, right_ref[64:65, :], left_ref[64:65, :])
    kx_ref[RIGHT : RIGHT + 1, :] = beyond
    kx_ref[LEFT : LEFT + 1, :] = beyond
    kind = kx_ref[TILES:PACKED, :]
    for number in range(3):
        for entry, chosen in enumerate(pick(table_ref, number, kind)):
            w_ref[number * 4 + entry, TILES:PACKED, :] = chosen
    weight_of = fine_weights(w_ref)
    w1 = [w_ref[4 + e] for e in range(4)]

    left_half = lanes_of((8, LANES)) < HALF
    for j in range(FACTOR):
        x, y = right_ref[pl.ds(j * 8, 8), :], left_ref[pl.ds(j * 8, 8), :]
        halo_ref[pl.ds(j * 16, 8), :] = jnp.where(left_half, x, y)
        halo_ref[pl.ds(j * 16 + 8, 8), :] = pltpu.roll(jnp.where(left_half, y, x), HALF, 1)

    unused = jnp.zeros(((LEFT - RIGHT - 1) * 8, LANES), jnp.float32)
    for field in range(2):
        for ref in (r1_ref, r1b_ref):
            ref[field, (RIGHT + 1) * 8 : LEFT * 8, :] = unused

    strip = [TILES - 2, TILES - 1, TILES, 0, 1]
    ps, qs = relax_from_zero(f_ref, halo_ref, w_ref, strip, [0, 0, 1, 2, 3], [1, 2, 3, 4, 4])
    for at, row in ((1, TILES - 1), (2, RIGHT), (2, LEFT), (3, 0)):
        r1_ref[0, tile_rows(row), :] = ps[at]
        r1_ref[1, tile_rows(row), :] = qs[at]

    def sweep(ref, keep):
        p = q = None
        for k in range(FACTOR):
            rp, rq = ref[0, pl.ds(k, PACKED, stride=8), :], ref[1, pl.ds(k, PACKED, stride=8), :]
            if k == 0:
                p, q = rp, rq
            else:
                p, q = phi_packed(p, q, w1)
                p, q = p + rp, q + rq
            if keep:
                c_ref[0, pl.ds(k, PACKED, stride=8), :] = p
                c_ref[1, pl.ds(k, PACKED, stride=8), :] = q
                if k < FACTOR - 1:
                    prev_ref[0, pl.ds(k + 1, PACKED, stride=8), :] = p
                    prev_ref[1, pl.ds(k + 1, PACKED, stride=8), :] = q
        return p, q

    nothing = jnp.zeros((PACKED, LANES), jnp.float32)
    prev_ref[0, pl.ds(0, PACKED, stride=8), :] = nothing
    prev_ref[1, pl.ds(0, PACKED, stride=8), :] = nothing
    r2p, r2q = sweep(r1_ref, True)
    r2_ref[0] = r2p
    r2_ref[1] = r2q

    ps, qs = tiles_from(prev_ref, 0), tiles_from(prev_ref, 1)
    for j in range(FACTOR):
        ps, qs = phi_tiles(ps, qs, weight_of)
    for field, xs in enumerate((ps, qs)):
        for t, row in spots():
            rows = tile_rows(row)
            r1b_ref[field, rows, :] = xs[t] + (r1_ref[field, rows, :] - c_ref[field, rows, :])
    gp, gq = sweep(r1b_ref, False)

    lane = lanes_of((8, LANES))
    for c, (x, g) in enumerate(((r2p, gp), (r2q, gq))):
        for half in range(2):
            shifted = [
                [y[8 * half : 8 * half + 8] for y in (pltpu.roll(z, 1, 0), z, pltpu.roll(z, PACKED - 1, 0))]
                for z in (x, g)
            ]

            def window(which, offset):
                a, b = shifted[which][0:2] if offset < 0 else shifted[which][1:3]
                start = offset % LANES
                return pltpu.roll(jnp.where(lane >= start, a, b), (LANES - start) % LANES, 1)

            for quarter in range(4):
                origin = SLAB * quarter
                near = window(0, origin + window_start(half))
                far = window(1, origin + share_start(half) - SPAN)
                nat_ref[pl.ds(64 * half + 2 * quarter + c, 8, stride=8), :] = jnp.where(lane < SPAN, near, far)
    by_rank(send_ref, nat_ref)


def window_start(half):
    return -REACH if half else -REACH - 8


def share_start(half):
    return 0 if half else -8


def prepare_kernel(place_ref, table_ref, kx_ref, scan_ref, dense_ref, fine_ref, states_ref, after_ref):
    place = place_ref[0]
    lane1 = lanes_of((1, LANES))
    origin = place * SLAB + (LANES - REACH - 8) + jnp.where(place >= WINDOWS // 2, 8, 0)
    base = origin // LANES - 1
    start = origin % LANES
    base = jnp.where(base < 0, LEFT, base)
    after = jnp.where(base == LEFT, 0, base + 1)
    a, b = kx_ref[pl.ds(base, 1), :], kx_ref[pl.ds(after, 1), :]
    kind = pltpu.roll(jnp.where(lane1 >= start, a, b), LANES - start, 1)
    kind = jnp.broadcast_to(kind, (8, LANES))
    w0, w1, w2 = (pick(table_ref, number, kind) for number in range(3))
    sub = lax.broadcasted_iota(jnp.int32, (8, LANES), 0)
    lane = lanes_of((8, LANES))

    def times(v, w):
        return [
            v[0] * w[0] + v[1] * w[2],
            v[0] * w[1] + v[1] * w[3],
            v[2] * w[0] + v[3] * w[2],
            v[2] * w[1] + v[3] * w[3],
        ]

    one, none = jnp.ones((8, LANES), jnp.float32), jnp.zeros((8, LANES), jnp.float32)
    w = w2
    grown = [one, none, none, one]
    for n, step in enumerate((1, 2, 4)):
        longer = times(grown, w)
        grown = [jnp.where((sub & step) != 0, x, y) for x, y in zip(longer, grown)]
        for e in range(4):
            scan_ref[4 * n + e] = jnp.where(sub >= step, w[e], 0.0)
        w = times(w, w)
    for e in range(4):
        scan_ref[12 + e] = w[e]
        scan_ref[16 + e] = grown[e]

    def combs(gap, teeth):
        made = []
        for n in range(gap // 8):
            hit = lane == sub + 8 * n
            for tooth in range(1, teeth):
                hit = hit | (lane == sub + (8 * n + gap * tooth))
            made.append(jnp.where(hit, 1.0, 0.0))
        blank = [none] * len(made)
        return made + blank, blank + made

    def spread(answers, ref, gap, teeth, reach):
        for n, answer in enumerate(answers):
            field, c = divmod(n, gap // 8)
            for tooth in range(teeth):
                at = sub + (8 * c + gap * tooth)
                near = (lane - at <= reach) & (at - lane <= reach)
                rows = pl.ds(field * LANES + gap * tooth + 8 * c, 8)
                for to in range(2):
                    ref[rows, LANES * to : LANES * (to + 1)] = jnp.where(near, answer[to], 0.0)
        for field in range(2):
            ref[field * LANES + gap * teeth : (field + 1) * LANES, :] = jnp.zeros((LANES - gap * teeth, 2 * LANES), jnp.float32)

    answers = list(zip(*combs(TEETH, 4)))
    for _ in range(FACTOR):
        answers = [phi_slab(p, q, w0) for p, q in answers]
    spread(answers, fine_ref, TEETH, 4, FACTOR)

    def rows_of(k, n):
        return pl.ds((k * GROUPS + n) * 8, 8)

    begin = list(zip(*combs(COMB, 2)))
    states = begin
    for k in range(FACTOR + 1):
        for n, (p, q) in enumerate(states):
            states_ref[rows_of(k, n), 0:LANES] = p
            states_ref[rows_of(k, n), LANES : 2 * LANES] = q
        if k < FACTOR:
            states = [phi_slab(p, q, w1) for p, q in states]
    after_ref[...] = jnp.dot(
        states_ref[0 : FACTOR * GROUPS * 8, :],
        fine_ref[...],
        precision=lax.Precision.HIGHEST,
        preferred_element_type=jnp.float32,
    )

    def residual(k, n):
        return [
            after_ref[rows_of(k, n), LANES * to : LANES * (to + 1)]
            - states_ref[rows_of(k + 1, n), LANES * to : LANES * (to + 1)]
            for to in range(2)
        ]

    m = [residual(0, n) for n in range(GROUPS)]
    for k in range(1, FACTOR):
        stepped = [phi_slab(p, q, w1) for p, q in m]
        m = [[x + y for x, y in zip(stepped[n], residual(k, n))] for n in range(GROUPS)]

    total = []
    for n in range(GROUPS):
        coarse = apply2(*begin[n], w2)
        total.append([m[n][to] + (states[n][to] - coarse[to]) for to in range(2)])
    spread(total, dense_ref, COMB, 2, REACH)


def slab_kernel(scan_ref, dense_ref, ranked_ref, send_ref, d_ref, got_ref, nat_ref):
    by_member(got_ref, ranked_ref)
    lane = lanes_of((8, LANES))
    masked = [[scan_ref[4 * n + e] for e in range(4)] for n in range(3)]
    w_eight = [scan_ref[12 + e] for e in range(4)]
    grown = [scan_ref[16 + e] for e in range(4)]
    first = lax.broadcasted_iota(jnp.int32, (8, LANES), 0) == 0

    def recurrence(rp, rq):
        yp, yq = list(rp), list(rq)
        for n, step in enumerate((1, 2, 4)):
            for b in range(8):
                sp, sq = apply2(pltpu.roll(yp[b], step, 0), pltpu.roll(yq[b], step, 0), masked[n])
                yp[b], yq[b] = yp[b] + sp, yq[b] + sq
        dp, dq = [], []
        tp = tq = None
        for b in range(8):
            bp, bq = pltpu.roll(yp[b], 1, 0), pltpu.roll(yq[b], 1, 0)
            bp, bq = jnp.where(first, 0.0, bp), jnp.where(first, 0.0, bq)
            ep, eq = yp[b][7:8], yq[b][7:8]
            ep, eq = jnp.broadcast_to(ep, (8, LANES)), jnp.broadcast_to(eq, (8, LANES))
            if b:
                sp, sq = apply2(tp, tq, grown)
                bp, bq = bp + sp, bq + sq
                sp, sq = apply2(tp, tq, w_eight)
                ep, eq = ep + sp, eq + sq
            tp, tq = ep, eq
            dp.append(bp)
            dq.append(bq)
        return dp, dq

    def rows(b, c):
        return pl.ds(b * 16 + c, 8, stride=2)

    gotten = [[got_ref[rows(b, c), :] for b in range(8)] for c in range(2)]
    dp, dq = recurrence(*gotten)
    for b in range(8):
        d_ref[8 * b : 8 * b + 8, 0:LANES] = dp[b]
        d_ref[8 * b : 8 * b + 8, LANES : 2 * LANES] = dq[b]
    answer = jnp.dot(d_ref[...], dense_ref[...], precision=lax.Precision.HIGHEST, preferred_element_type=jnp.float32)
    back = SPAN - REACH
    residual = [
        [
            answer[8 * b : 8 * b + 8, LANES * c : LANES * (c + 1)] + pltpu.roll(gotten[c][b], LANES - back, 1)
            for b in range(8)
        ]
        for c in range(2)
    ]
    ep, eq = recurrence(*residual)
    for b in range(8):
        nat_ref[rows(b, 0), :] = jnp.where(lane < SPAN, dp[b], pltpu.roll(ep[b], back, 1))
        nat_ref[rows(b, 1), :] = jnp.where(lane < SPAN, dq[b], pltpu.roll(eq[b], back, 1))
    by_rank(send_ref, nat_ref)


def last_kernel(f_ref, halo_ref, r1_ref, r2_ref, w_ref, ranked_ref, out_ref, prev_ref, c_ref, r1b_ref, d_ref,
                o_ref, got_ref, sems):
    by_member(got_ref, ranked_ref)

    lane = lanes_of((8, LANES))
    lane1 = lanes_of((1, LANES))
    for c in range(2):
        for cycle in range(2):
            for half in range(2):
                begin = (SPAN - share_start(half)) if cycle else -window_start(half)
                whole = jnp.zeros((8, LANES), jnp.float32)
                for quarter in range(4):
                    piece = got_ref[pl.ds(64 * half + 2 * quarter + c, 8, stride=8), :]
                    piece = pltpu.roll(piece, (SLAB * quarter - begin) % LANES, 1)
                    mine = (lane >= SLAB * quarter) & (lane < SLAB * (quarter + 1))
                    whole = jnp.where(mine, piece, whole)
                d_ref[2 * cycle + c, 8 * half : 8 * half + 8, :] = whole
            d_ref[2 * cycle + c, TILES:PACKED, :] = jnp.zeros((PACKED - TILES, LANES), jnp.float32)
            width = 8 if cycle else 24
            begin = (SPAN - share_start(0)) if cycle else -window_start(0)
            low = pltpu.roll(got_ref[c : c + 1, :], LANES - begin, 1)
            d_ref[2 * cycle + c, LEFT : LEFT + 1, :] = jnp.where(lane1 >= LANES - width, low, 0.0)
            begin = (SPAN - share_start(1)) if cycle else -window_start(1)
            end = (WINDOWS - 1) * 2 + c
            high = pltpu.roll(got_ref[end : end + 1, :], LANES - begin - SLAB, 1)
            d_ref[2 * cycle + c, RIGHT : RIGHT + 1, :] = jnp.where(lane1 < width, high, 0.0)

    weight_of = fine_weights(w_ref)
    w1 = [w_ref[4 + e] for e in range(4)]
    w2 = [w_ref[8 + e] for e in range(4)]
    unused = jnp.zeros(((LEFT - RIGHT - 1) * 8, LANES), jnp.float32)
    for field in range(2):
        r1b_ref[field, (RIGHT + 1) * 8 : LEFT * 8, :] = unused

    p, q = d_ref[0], d_ref[1]
    last_p, last_q = apply2(p, q, w2)
    c_ref[0, pl.ds(FACTOR - 1, PACKED, stride=8), :] = last_p + r2_ref[0]
    c_ref[1, pl.ds(FACTOR - 1, PACKED, stride=8), :] = last_q + r2_ref[1]
    prev_ref[0, pl.ds(0, PACKED, stride=8), :] = p
    prev_ref[1, pl.ds(0, PACKED, stride=8), :] = q
    for k in range(FACTOR - 1):
        p, q = phi_packed(p, q, w1)
        p = p + r1_ref[0, pl.ds(k, PACKED, stride=8), :]
        q = q + r1_ref[1, pl.ds(k, PACKED, stride=8), :]
        c_ref[0, pl.ds(k, PACKED, stride=8), :] = p
        c_ref[1, pl.ds(k, PACKED, stride=8), :] = q
        prev_ref[0, pl.ds(k + 1, PACKED, stride=8), :] = p
        prev_ref[1, pl.ds(k + 1, PACKED, stride=8), :] = q

    ps, qs = tiles_from(prev_ref, 0), tiles_from(prev_ref, 1)
    for j in range(FACTOR):
        ps, qs = phi_tiles(ps, qs, weight_of)
        if j == FACTOR - 1:
            copies = [
                pltpu.make_async_copy(o_ref.at[pl.ds(k * STRIDE, 224)], out_ref.at[pl.ds(k * 256, 224)], sems.at[k])
                for k in range(FACTOR)
            ]
            for copy in copies:
                copy.start()
        for t in range(LISTED):
            ps[t] = ps[t] + load_forcing(f_ref, halo_ref, j, t, 0)
            qs[t] = qs[t] + load_forcing(f_ref, halo_ref, j, t, 1)
            if j < FACTOR - 1 and t < TILES:
                o_ref[pl.ds(j * 32 + t * 2, 8, stride=STRIDE), :] = ps[t]
                o_ref[pl.ds(j * 32 + t * 2 + 1, 8, stride=STRIDE), :] = qs[t]
    for t, row in spots():
        r1b_ref[0, tile_rows(row), :] = ps[t] - c_ref[0, tile_rows(row), :]
        r1b_ref[1, tile_rows(row), :] = qs[t] - c_ref[1, tile_rows(row), :]

    def finish(k, p, q):
        for field, x in enumerate((p, q)):
            done = c_ref[field, pl.ds(k, PACKED, stride=8), :] + x
            o_ref[pl.ds(k * STRIDE + 224 + field, TILES, stride=2), :] = done[0:TILES]
        copy = pltpu.make_async_copy(
            o_ref.at[pl.ds(k * STRIDE + 224, 32)], out_ref.at[pl.ds(k * 256 + 224, 32)], sems.at[FACTOR + k]
        )
        copy.start()
        copies.append(copy)

    p, q = d_ref[2], d_ref[3]
    last_p, last_q = apply2(p, q, w2)
    mp = mq = None
    for k in range(FACTOR):
        rp, rq = r1b_ref[0, pl.ds(k, PACKED, stride=8), :], r1b_ref[1, pl.ds(k, PACKED, stride=8), :]
        if k == 0:
            mp, mq = rp, rq
        else:
            mp, mq = phi_packed(mp, mq, w1)
            mp, mq = mp + rp, mq + rq
        if k < FACTOR - 1:
            p, q = phi_packed(p, q, w1)
            p, q = p + rp, q + rq
            finish(k, p, q)
    finish(FACTOR - 1, last_p + mp, last_q + mq)
    for copy in copies:
        copy.wait()


VMEM = pl.BlockSpec(memory_space=pltpu.VMEM)
SMEM = pl.BlockSpec(memory_space=pltpu.SMEM)
STATE = (2, PACKED * 8, LANES)


def shaped(*shape):
    return jax.ShapeDtypeStruct(shape, jnp.float32)


def scratch(*shape):
    return pltpu.VMEM(shape, jnp.float32)


ANY = pl.BlockSpec(memory_space=pl.ANY)
HBM = pl.BlockSpec(memory_space=pltpu.HBM)
SMALL = pltpu.CompilerParams(vmem_limit_bytes=8 << 20)
DENSE = pltpu.CompilerParams(vmem_limit_bytes=8 << 20)


def edge_stage(flat, friction, compressor, blocks):
    return pl.pallas_call(
        edge_kernel,
        out_shape=(shaped(PADDED, LANES), shaped(EDGE_ROWS, LANES), shaped(EDGE_ROWS, LANES), shaped(TILES, LANES), shaped(TABLE, 8, LANES)),
        in_specs=[HBM] * 4,
        out_specs=(VMEM,) * 5,
        scratch_shapes=[pltpu.VMEM((TILES, LANES), jnp.int32)] * 2
        + [pltpu.SMEM((3, 2, 2, KINDS), jnp.float32), pltpu.SemaphoreType.DMA((FACTOR + 3,))],
        compiler_params=SMALL,
        name="edge",
    )(flat, friction, compressor, blocks)


PREPARED = (shaped(20, 8, LANES), shaped(2 * LANES, 2 * LANES))
PREPARING = [
    scratch(2 * LANES, 2 * LANES),
    scratch((FACTOR + 1) * GROUPS * 8, 2 * LANES),
    scratch(FACTOR * GROUPS * 8, 2 * LANES),
]


def main_stage(table, padded, kinds):
    return pl.pallas_call(
        main_kernel,
        out_shape=(shaped(*STATE), shaped(12, PACKED, LANES)),
        in_specs=[VMEM] * 3,
        out_specs=(VMEM,) * 2,
        compiler_params=DENSE,
        name="main",
    )(table, padded, kinds)


def first_stage(table, padded, right, left, kinds, r1, weights):
    return pl.pallas_call(
        first_kernel,
        out_shape=(
            shaped(*STATE),
            shaped(12, PACKED, LANES),
            shaped(2, PACKED, LANES),
            shaped(PACKED, LANES),
            shaped(2 * WINDOWS, LANES),
            shaped(128, LANES),
        ),
        in_specs=[VMEM] * 7,
        out_specs=(VMEM,) * 6,
        input_output_aliases={5: 0, 6: 1},
        scratch_shapes=[scratch(*STATE)] * 3 + [scratch(2 * WINDOWS, LANES)],
        compiler_params=DENSE,
        name="first",
    )(table, padded, right, left, kinds, r1, weights)


def prepare_stage(place, table, kinds):
    return pl.pallas_call(
        prepare_kernel,
        out_shape=PREPARED,
        in_specs=[SMEM, VMEM, VMEM],
        out_specs=(VMEM, VMEM),
        scratch_shapes=PREPARING,
        compiler_params=DENSE,
        name="prepare",
    )(place, table, kinds)


def slab_stage(scan, dense, got):
    return pl.pallas_call(
        slab_kernel,
        out_shape=shaped(2 * WINDOWS, LANES),
        in_specs=[VMEM] * 3,
        out_specs=VMEM,
        scratch_shapes=[scratch(WINDOWS, 2 * LANES)] + [scratch(2 * WINDOWS, LANES)] * 2,
        compiler_params=SMALL,
        name="slab",
    )(scan, dense, got)


def last_stage(padded, halo, r1, r2, weights, got):
    return pl.pallas_call(
        last_kernel,
        out_shape=shaped(2048, LANES),
        in_specs=[VMEM] * 6,
        out_specs=ANY,
        scratch_shapes=[scratch(*STATE)] * 3
        + [scratch(4, PACKED, LANES), scratch(PADDED, LANES), scratch(2 * WINDOWS, LANES), pltpu.SemaphoreType.DMA((2 * FACTOR,))],
        compiler_params=DENSE,
        name="last",
    )(padded, halo, r1, r2, weights, got)


def to_rows(forcing):
    return forcing.reshape(64, 2, TILES, LANES).transpose(0, 2, 1, 3).reshape(2048, LANES)


def from_rows(rows):
    return rows.reshape(64, TILES, 2, LANES).transpose(0, 2, 1, 3).reshape(64, 2, TILES * LANES)


def transpose_windows(rows):
    return lax.all_to_all(rows.reshape(WINDOWS, 2, LANES), "tm", 0, 0, axis_index_groups=[ORDER]).reshape(2 * WINDOWS, LANES)


def per_device(forcing, friction_class, compressor, blocks):
    flat = to_rows(forcing)
    friction = friction_class.reshape(TILES, LANES)
    station = compressor.reshape(TILES, LANES)
    count = lax.axis_size("net")
    flat, friction, station, blocks = (
        pltpu.with_memory_space_constraint(x, pltpu.HBM) for x in (flat, friction, station, blocks)
    )
    padded, low, high, kinds, table = edge_stage(flat, friction, station, blocks)
    left = lax.ppermute(high, "net", [(i, i + 1) for i in range(count - 1)])
    right = lax.ppermute(low, "net", [(i + 1, i) for i in range(count - 1)])
    r1, weights = main_stage(table, padded, kinds)
    r1, weights, r2, kinds_wide, send, halo = first_stage(table, padded, right, left, kinds, r1, weights)
    got = transpose_windows(send)
    place = lax.axis_index("tm").astype(jnp.int32).reshape(1)
    scan, dense = prepare_stage(place, table, kinds_wide)
    got = transpose_windows(slab_stage(scan, dense, got))
    return from_rows(last_stage(padded, halo, r1, r2, weights, got))


def solution(mesh):
    placed = (P("tm", None, "net"), P("net"), P("net"), P())
    return jax.shard_map(
        per_device, mesh=mesh, in_specs=placed, out_specs=P("tm", None, "net"), check_vma=False
    )
```

```python
import jax
import jax.numpy as jnp
from jax import lax
from jax.experimental import pallas as pl
from jax.experimental.pallas import tpu as pltpu
from jax.sharding import PartitionSpec as P

FACTOR = 8
KINDS = 9
TABLE = 12 * KINDS
LANES = 128
TILES = 16
WINDOWS = 64
PACKED = 24
RIGHT = 16
LEFT = 23
EDGE_ROWS = 72
STRIDE = 264
PADDED = FACTOR * STRIDE
HALF = LANES // 2
LISTED = TILES + 1
PREV = [TILES] + list(range(TILES))
NEXT = list(range(1, TILES + 1)) + [0]
MEET = 41
ORDER = [(MEET + rank) % WINDOWS for rank in range(WINDOWS)]
SLAB = 32
REACH = 22
SPAN = 84
COMB = 48
GROUPS = 2 * COMB // 8
TEETH = 24


def runs():
    found = []
    for rank, member in enumerate(ORDER):
        if found and found[-1][1] + found[-1][2] == member:
            found[-1][2] += 1
        else:
            found.append([rank, member, 1])
    return found


def by_rank(to_ref, from_ref):
    for rank, member, length in runs():
        to_ref[2 * rank : 2 * (rank + length), :] = from_ref[2 * member : 2 * (member + length), :]


def by_member(to_ref, from_ref):
    for rank, member, length in runs():
        to_ref[2 * member : 2 * (member + length), :] = from_ref[2 * rank : 2 * (rank + length), :]


def lanes_of(shape):
    return lax.broadcasted_iota(jnp.int32, shape, len(shape) - 1)


def couple(p, q, p_low, p_high, q_low, q_high, w):
    mixed_p = (p + p) + (q_high - q_low)
    mixed_q = (q + q) + (p_low - p_high)
    return w[0] * mixed_p + w[1] * mixed_q, w[2] * mixed_p + w[3] * mixed_q


def apply2(p, q, w):
    return w[0] * p + w[1] * q, w[2] * p + w[3] * q


def phi_tiles(ps, qs, weight_of, before=PREV, behind=NEXT):
    lane = lanes_of((8, LANES))
    first, last = lane == 0, lane == LANES - 1

    def low(xs, t):
        return pltpu.roll(jnp.where(last, xs[before[t]], xs[t]), 1, 1)

    def high(xs, t):
        return pltpu.roll(jnp.where(first, xs[behind[t]], xs[t]), LANES - 1, 1)

    new_p, new_q = [], []
    for t in range(len(ps)):
        p, q = couple(ps[t], qs[t], low(ps, t), high(ps, t), low(qs, t), high(qs, t), weight_of(t))
        new_p.append(p)
        new_q.append(q)
    return new_p, new_q


def phi_packed(p, q, w):
    lane = lanes_of((PACKED, LANES))
    first, last = lane == 0, lane == LANES - 1

    def low(x):
        return pltpu.roll(jnp.where(last, pltpu.roll(x, 1, 0), x), 1, 1)

    def high(x):
        return pltpu.roll(jnp.where(first, pltpu.roll(x, PACKED - 1, 0), x), LANES - 1, 1)

    return couple(p, q, low(p), high(p), low(q), high(q), w)


def phi_slab(p, q, w):
    return couple(
        p, q, pltpu.roll(p, 1, 1), pltpu.roll(p, LANES - 1, 1), pltpu.roll(q, 1, 1), pltpu.roll(q, LANES - 1, 1), w
    )


def pick(table_ref, number, kind):
    masks = [kind == float(k + 1) for k in range(KINDS)]
    picked = []
    for entry in range(4):
        chosen = jnp.zeros_like(kind)
        for k in range(KINDS):
            choice = table_ref[(number * 4 + entry) * KINDS + k]
            if kind.shape[0] != 8:
                choice = jnp.concatenate([choice] * (kind.shape[0] // 8))
            chosen = jnp.where(masks[k], choice, chosen)
        picked.append(chosen)
    return picked


def load_forcing(f_ref, halo_ref, j, t, field):
    if t < TILES:
        return f_ref[pl.ds(j * 32 + t * 2 + field, 8, stride=STRIDE), :]
    return halo_ref[pl.ds((j * 2 + field) * 8, 8), :]


def tile_rows(row):
    return pl.ds(row * 8, 8)


def tiles_from(ref, field):
    both = jnp.where(lanes_of((8, LANES)) < HALF, ref[field, tile_rows(RIGHT), :], ref[field, tile_rows(LEFT), :])
    return [ref[field, tile_rows(t), :] for t in range(TILES)] + [both]


def spots():
    return [(t, t) for t in range(TILES)] + [(TILES, RIGHT), (TILES, LEFT)]


def fine_weights(w_ref):
    def weight_of(t):
        return [jnp.broadcast_to(w_ref[e, t : t + 1, :], (8, LANES)) for e in range(4)]

    return weight_of


def edge_kernel(source_ref, fc_hbm, comp_hbm, blocks_hbm, f_ref, low_ref, high_ref, kind_ref, table_ref, fc_ref, comp_ref,
                blocks_ref, sems):
    copies = [
        pltpu.make_async_copy(source_ref.at[pl.ds(k * 256, 256)], f_ref.at[pl.ds(k * STRIDE, 256)], sems.at[k])
        for k in range(FACTOR)
    ]
    labels = [
        pltpu.make_async_copy(fc_hbm, fc_ref, sems.at[FACTOR]),
        pltpu.make_async_copy(comp_hbm, comp_ref, sems.at[FACTOR + 1]),
        pltpu.make_async_copy(blocks_hbm, blocks_ref, sems.at[FACTOR + 2]),
    ]
    for copy in labels + copies:
        copy.start()
    for copy in labels:
        copy.wait()
    kinds = jnp.where(comp_ref[...] == 1, KINDS, fc_ref[...] + 1).astype(jnp.float32)
    kind_ref[...] = kinds
    low_ref[64:EDGE_ROWS, :] = jnp.broadcast_to(kinds[0:1], (8, LANES))
    high_ref[64:EDGE_ROWS, :] = jnp.broadcast_to(kinds[TILES - 1 : TILES], (8, LANES))
    for number in range(3):
        scale = 1.0 if number == 2 else 0.25
        for entry in range(4):
            for k in range(KINDS):
                value = blocks_ref[number, entry // 2, entry % 2, k] * scale
                table_ref[(number * 4 + entry) * KINDS + k] = jnp.full((8, LANES), value, jnp.float32)
    left_half = lanes_of((8, LANES)) < HALF
    for copy in copies:
        copy.wait()
    for j in range(FACTOR):
        rows = pl.ds(j * 8, 8)
        p, q = (f_ref[pl.ds(j * 32 + field, 8, stride=STRIDE), :] for field in range(2))
        low_ref[rows, :] = jnp.where(left_half, p, pltpu.roll(q, HALF, 1))
        p, q = (f_ref[pl.ds(j * 32 + 2 * (TILES - 1) + field, 8, stride=STRIDE), :] for field in range(2))
        high_ref[rows, :] = jnp.where(left_half, pltpu.roll(q, HALF, 1), p)


def fine_weights_at(w_ref, rows):
    def weight_of(t):
        return [jnp.broadcast_to(w_ref[e, rows[t] : rows[t] + 1, :], (8, LANES)) for e in range(4)]

    return weight_of


def relax_from_zero(f_ref, halo_ref, w_ref, tiles, before, behind):
    weight_of = fine_weights_at(w_ref, tiles)
    ps, qs = ([load_forcing(f_ref, halo_ref, 0, t, field) for t in tiles] for field in range(2))
    for j in range(1, FACTOR):
        ps, qs = phi_tiles(ps, qs, weight_of, before, behind)
        ps = [x + load_forcing(f_ref, halo_ref, j, t, 0) for x, t in zip(ps, tiles)]
        qs = [x + load_forcing(f_ref, halo_ref, j, t, 1) for x, t in zip(qs, tiles)]
    return ps, qs


def main_kernel(table_ref, f_ref, kind_ref, r1_ref, w_ref):
    kind = kind_ref[...]
    for number in range(3):
        for entry, chosen in enumerate(pick(table_ref, number, kind)):
            w_ref[number * 4 + entry, 0:TILES, :] = chosen
    tiles = list(range(TILES))
    before, behind = [(t - 1) % TILES for t in tiles], [(t + 1) % TILES for t in tiles]
    ps, qs = relax_from_zero(f_ref, None, w_ref, tiles, before, behind)
    for t in tiles:
        r1_ref[0, tile_rows(t), :] = ps[t]
        r1_ref[1, tile_rows(t), :] = qs[t]


def first_kernel(table_ref, f_ref, right_ref, left_ref, kind_ref, r1_in, w_in, r1_ref, w_ref, r2_ref, kx_ref, send_ref,
                 halo_ref, prev_ref, c_ref, r1b_ref, nat_ref):
    kx_ref[0:TILES, :] = kind_ref[...]
    kx_ref[TILES:PACKED, :] = jnp.zeros((PACKED - TILES, LANES), jnp.float32)
    beyond = jnp.where(lanes_of((1, LANES)) < HALF, right_ref[64:65, :], left_ref[64:65, :])
    kx_ref[RIGHT : RIGHT + 1, :] = beyond
    kx_ref[LEFT : LEFT + 1, :] = beyond
    kind = kx_ref[TILES:PACKED, :]
    for number in range(3):
        for entry, chosen in enumerate(pick(table_ref, number, kind)):
            w_ref[number * 4 + entry, TILES:PACKED, :] = chosen
    weight_of = fine_weights(w_ref)
    w1 = [w_ref[4 + e] for e in range(4)]

    left_half = lanes_of((8, LANES)) < HALF
    for j in range(FACTOR):
        x, y = right_ref[pl.ds(j * 8, 8), :], left_ref[pl.ds(j * 8, 8), :]
        halo_ref[pl.ds(j * 16, 8), :] = jnp.where(left_half, x, y)
        halo_ref[pl.ds(j * 16 + 8, 8), :] = pltpu.roll(jnp.where(left_half, y, x), HALF, 1)

    unused = jnp.zeros(((LEFT - RIGHT - 1) * 8, LANES), jnp.float32)
    for field in range(2):
        for ref in (r1_ref, r1b_ref):
            ref[field, (RIGHT + 1) * 8 : LEFT * 8, :] = unused

    strip = [TILES - 2, TILES - 1, TILES, 0, 1]
    ps, qs = relax_from_zero(f_ref, halo_ref, w_ref, strip, [0, 0, 1, 2, 3], [1, 2, 3, 4, 4])
    for at, row in ((1, TILES - 1), (2, RIGHT), (2, LEFT), (3, 0)):
        r1_ref[0, tile_rows(row), :] = ps[at]
        r1_ref[1, tile_rows(row), :] = qs[at]

    def sweep(ref, keep):
        p = q = None
        for k in range(FACTOR):
            rp, rq = ref[0, pl.ds(k, PACKED, stride=8), :], ref[1, pl.ds(k, PACKED, stride=8), :]
            if k == 0:
                p, q = rp, rq
            else:
                p, q = phi_packed(p, q, w1)
                p, q = p + rp, q + rq
            if keep:
                c_ref[0, pl.ds(k, PACKED, stride=8), :] = p
                c_ref[1, pl.ds(k, PACKED, stride=8), :] = q
                if k < FACTOR - 1:
                    prev_ref[0, pl.ds(k + 1, PACKED, stride=8), :] = p
                    prev_ref[1, pl.ds(k + 1, PACKED, stride=8), :] = q
        return p, q

    nothing = jnp.zeros((PACKED, LANES), jnp.float32)
    prev_ref[0, pl.ds(0, PACKED, stride=8), :] = nothing
    prev_ref[1, pl.ds(0, PACKED, stride=8), :] = nothing
    r2p, r2q = sweep(r1_ref, True)
    r2_ref[0] = r2p
    r2_ref[1] = r2q

    ps, qs = tiles_from(prev_ref, 0), tiles_from(prev_ref, 1)
    for j in range(FACTOR):
        ps, qs = phi_tiles(ps, qs, weight_of)
    for field, xs in enumerate((ps, qs)):
        for t, row in spots():
            rows = tile_rows(row)
            r1b_ref[field, rows, :] = xs[t] + (r1_ref[field, rows, :] - c_ref[field, rows, :])
    gp, gq = sweep(r1b_ref, False)

    lane = lanes_of((8, LANES))
    for c, (x, g) in enumerate(((r2p, gp), (r2q, gq))):
        for half in range(2):
            shifted = [
                [y[8 * half : 8 * half + 8] for y in (pltpu.roll(z, 1, 0), z, pltpu.roll(z, PACKED - 1, 0))]
                for z in (x, g)
            ]

            def window(which, offset):
                a, b = shifted[which][0:2] if offset < 0 else shifted[which][1:3]
                start = offset % LANES
                return pltpu.roll(jnp.where(lane >= start, a, b), (LANES - start) % LANES, 1)

            for quarter in range(4):
                origin = SLAB * quarter
                near = window(0, origin + window_start(half))
                far = window(1, origin + share_start(half) - SPAN)
                nat_ref[pl.ds(64 * half + 2 * quarter + c, 8, stride=8), :] = jnp.where(lane < SPAN, near, far)
    by_rank(send_ref, nat_ref)


def window_start(half):
    return -REACH if half else -REACH - 8


def share_start(half):
    return 0 if half else -8


def prepare_kernel(place_ref, table_ref, kx_ref, scan_ref, dense_ref, fine_ref, states_ref, after_ref):
    place = place_ref[0]
    lane1 = lanes_of((1, LANES))
    origin = place * SLAB + (LANES - REACH - 8) + jnp.where(place >= WINDOWS // 2, 8, 0)
    base = origin // LANES - 1
    start = origin % LANES
    base = jnp.where(base < 0, LEFT, base)
    after = jnp.where(base == LEFT, 0, base + 1)
    a, b = kx_ref[pl.ds(base, 1), :], kx_ref[pl.ds(after, 1), :]
    kind = pltpu.roll(jnp.where(lane1 >= start, a, b), LANES - start, 1)
    kind = jnp.broadcast_to(kind, (8, LANES))
    w0, w1, w2 = (pick(table_ref, number, kind) for number in range(3))
    sub = lax.broadcasted_iota(jnp.int32, (8, LANES), 0)
    lane = lanes_of((8, LANES))

    def times(v, w):
        return [
            v[0] * w[0] + v[1] * w[2],
            v[0] * w[1] + v[1] * w[3],
            v[2] * w[0] + v[3] * w[2],
            v[2] * w[1] + v[3] * w[3],
        ]

    one, none = jnp.ones((8, LANES), jnp.float32), jnp.zeros((8, LANES), jnp.float32)
    w = w2
    grown = [one, none, none, one]
    for n, step in enumerate((1, 2, 4)):
        longer = times(grown, w)
        grown = [jnp.where((sub & step) != 0, x, y) for x, y in zip(longer, grown)]
        for e in range(4):
            scan_ref[4 * n + e] = jnp.where(sub >= step, w[e], 0.0)
        w = times(w, w)
    for e in range(4):
        scan_ref[12 + e] = w[e]
        scan_ref[16 + e] = grown[e]

    def combs(gap, teeth):
        made = []
        for n in range(gap // 8):
            hit = lane == sub + 8 * n
            for tooth in range(1, teeth):
                hit = hit | (lane == sub + (8 * n + gap * tooth))
            made.append(jnp.where(hit, 1.0, 0.0))
        blank = [none] * len(made)
        return made + blank, blank + made

    def spread(answers, ref, gap, teeth, reach):
        for n, answer in enumerate(answers):
            field, c = divmod(n, gap // 8)
            for tooth in range(teeth):
                at = sub + (8 * c + gap * tooth)
                near = (lane - at <= reach) & (at - lane <= reach)
                rows = pl.ds(field * LANES + gap * tooth + 8 * c, 8)
                for to in range(2):
                    ref[rows, LANES * to : LANES * (to + 1)] = jnp.where(near, answer[to], 0.0)
        for field in range(2):
            ref[field * LANES + gap * teeth : (field + 1) * LANES, :] = jnp.zeros((LANES - gap * teeth, 2 * LANES), jnp.float32)

    answers = list(zip(*combs(TEETH, 4)))
    for _ in range(FACTOR):
        answers = [phi_slab(p, q, w0) for p, q in answers]
    spread(answers, fine_ref, TEETH, 4, FACTOR)

    def rows_of(k, n):
        return pl.ds((k * GROUPS + n) * 8, 8)

    begin = list(zip(*combs(COMB, 2)))
    states = begin
    for k in range(FACTOR + 1):
        for n, (p, q) in enumerate(states):
            states_ref[rows_of(k, n), 0:LANES] = p
            states_ref[rows_of(k, n), LANES : 2 * LANES] = q
        if k < FACTOR:
            states = [phi_slab(p, q, w1) for p, q in states]
    after_ref[...] = jnp.dot(
        states_ref[0 : FACTOR * GROUPS * 8, :],
        fine_ref[...],
        precision=lax.Precision.HIGHEST,
        preferred_element_type=jnp.float32,
    )

    def residual(k, n):
        return [
            after_ref[rows_of(k, n), LANES * to : LANES * (to + 1)]
            - states_ref[rows_of(k + 1, n), LANES * to : LANES * (to + 1)]
            for to in range(2)
        ]

    m = [residual(0, n) for n in range(GROUPS)]
    for k in range(1, FACTOR):
        stepped = [phi_slab(p, q, w1) for p, q in m]
        m = [[x + y for x, y in zip(stepped[n], residual(k, n))] for n in range(GROUPS)]

    total = []
    for n in range(GROUPS):
        coarse = apply2(*begin[n], w2)
        total.append([m[n][to] + (states[n][to] - coarse[to]) for to in range(2)])
    spread(total, dense_ref, COMB, 2, REACH)


def slab_kernel(scan_ref, dense_ref, ranked_ref, send_ref, d_ref, got_ref, nat_ref):
    by_member(got_ref, ranked_ref)
    lane = lanes_of((8, LANES))
    masked = [[scan_ref[4 * n + e] for e in range(4)] for n in range(3)]
    w_eight = [scan_ref[12 + e] for e in range(4)]
    grown = [scan_ref[16 + e] for e in range(4)]
    first = lax.broadcasted_iota(jnp.int32, (8, LANES), 0) == 0

    def recurrence(rp, rq):
        yp, yq = list(rp), list(rq)
        for n, step in enumerate((1, 2, 4)):
            for b in range(8):
                sp, sq = apply2(pltpu.roll(yp[b], step, 0), pltpu.roll(yq[b], step, 0), masked[n])
                yp[b], yq[b] = yp[b] + sp, yq[b] + sq
        dp, dq = [], []
        tp = tq = None
        for b in range(8):
            bp, bq = pltpu.roll(yp[b], 1, 0), pltpu.roll(yq[b], 1, 0)
            bp, bq = jnp.where(first, 0.0, bp), jnp.where(first, 0.0, bq)
            ep, eq = yp[b][7:8], yq[b][7:8]
            ep, eq = jnp.broadcast_to(ep, (8, LANES)), jnp.broadcast_to(eq, (8, LANES))
            if b:
                sp, sq = apply2(tp, tq, grown)
                bp, bq = bp + sp, bq + sq
                sp, sq = apply2(tp, tq, w_eight)
                ep, eq = ep + sp, eq + sq
            tp, tq = ep, eq
            dp.append(bp)
            dq.append(bq)
        return dp, dq

    def rows(b, c):
        return pl.ds(b * 16 + c, 8, stride=2)

    gotten = [[got_ref[rows(b, c), :] for b in range(8)] for c in range(2)]
    dp, dq = recurrence(*gotten)
    for b in range(8):
        d_ref[8 * b : 8 * b + 8, 0:LANES] = dp[b]
        d_ref[8 * b : 8 * b + 8, LANES : 2 * LANES] = dq[b]
    answer = jnp.dot(d_ref[...], dense_ref[...], precision=lax.Precision.HIGHEST, preferred_element_type=jnp.float32)
    back = SPAN - REACH
    residual = [
        [
            answer[8 * b : 8 * b + 8, LANES * c : LANES * (c + 1)] + pltpu.roll(gotten[c][b], LANES - back, 1)
            for b in range(8)
        ]
        for c in range(2)
    ]
    ep, eq = recurrence(*residual)
    for b in range(8):
        nat_ref[rows(b, 0), :] = jnp.where(lane < SPAN, dp[b], pltpu.roll(ep[b], back, 1))
        nat_ref[rows(b, 1), :] = jnp.where(lane < SPAN, dq[b], pltpu.roll(eq[b], back, 1))
    by_rank(send_ref, nat_ref)


def last_kernel(f_ref, halo_ref, r1_ref, r2_ref, w_ref, ranked_ref, out_ref, prev_ref, c_ref, r1b_ref, d_ref,
                o_ref, got_ref, sems):
    by_member(got_ref, ranked_ref)

    lane = lanes_of((8, LANES))
    lane1 = lanes_of((1, LANES))
    for c in range(2):
        for cycle in range(2):
            for half in range(2):
                begin = (SPAN - share_start(half)) if cycle else -window_start(half)
                whole = jnp.zeros((8, LANES), jnp.float32)
                for quarter in range(4):
                    piece = got_ref[pl.ds(64 * half + 2 * quarter + c, 8, stride=8), :]
                    piece = pltpu.roll(piece, (SLAB * quarter - begin) % LANES, 1)
                    mine = (lane >= SLAB * quarter) & (lane < SLAB * (quarter + 1))
                    whole = jnp.where(mine, piece, whole)
                d_ref[2 * cycle + c, 8 * half : 8 * half + 8, :] = whole
            d_ref[2 * cycle + c, TILES:PACKED, :] = jnp.zeros((PACKED - TILES, LANES), jnp.float32)
            width = 8 if cycle else 24
            begin = (SPAN - share_start(0)) if cycle else -window_start(0)
            low = pltpu.roll(got_ref[c : c + 1, :], LANES - begin, 1)
            d_ref[2 * cycle + c, LEFT : LEFT + 1, :] = jnp.where(lane1 >= LANES - width, low, 0.0)
            begin = (SPAN - share_start(1)) if cycle else -window_start(1)
            end = (WINDOWS - 1) * 2 + c
            high = pltpu.roll(got_ref[end : end + 1, :], LANES - begin - SLAB, 1)
            d_ref[2 * cycle + c, RIGHT : RIGHT + 1, :] = jnp.where(lane1 < width, high, 0.0)

    weight_of = fine_weights(w_ref)
    w1 = [w_ref[4 + e] for e in range(4)]
    w2 = [w_ref[8 + e] for e in range(4)]
    unused = jnp.zeros(((LEFT - RIGHT - 1) * 8, LANES), jnp.float32)
    for field in range(2):
        r1b_ref[field, (RIGHT + 1) * 8 : LEFT * 8, :] = unused

    p, q = d_ref[0], d_ref[1]
    last_p, last_q = apply2(p, q, w2)
    c_ref[0, pl.ds(FACTOR - 1, PACKED, stride=8), :] = last_p + r2_ref[0]
    c_ref[1, pl.ds(FACTOR - 1, PACKED, stride=8), :] = last_q + r2_ref[1]
    prev_ref[0, pl.ds(0, PACKED, stride=8), :] = p
    prev_ref[1, pl.ds(0, PACKED, stride=8), :] = q
    for k in range(FACTOR - 1):
        p, q = phi_packed(p, q, w1)
        p = p + r1_ref[0, pl.ds(k, PACKED, stride=8), :]
        q = q + r1_ref[1, pl.ds(k, PACKED, stride=8), :]
        c_ref[0, pl.ds(k, PACKED, stride=8), :] = p
        c_ref[1, pl.ds(k, PACKED, stride=8), :] = q
        prev_ref[0, pl.ds(k + 1, PACKED, stride=8), :] = p
        prev_ref[1, pl.ds(k + 1, PACKED, stride=8), :] = q

    ps, qs = tiles_from(prev_ref, 0), tiles_from(prev_ref, 1)
    for j in range(FACTOR):
        ps, qs = phi_tiles(ps, qs, weight_of)
        if j == FACTOR - 1:
            copies = [
                pltpu.make_async_copy(o_ref.at[pl.ds(k * STRIDE, 224)], out_ref.at[pl.ds(k * 256, 224)], sems.at[k])
                for k in range(FACTOR)
            ]
            for copy in copies:
                copy.start()
        for t in range(LISTED):
            ps[t] = ps[t] + load_forcing(f_ref, halo_ref, j, t, 0)
            qs[t] = qs[t] + load_forcing(f_ref, halo_ref, j, t, 1)
            if j < FACTOR - 1 and t < TILES:
                o_ref[pl.ds(j * 32 + t * 2, 8, stride=STRIDE), :] = ps[t]
                o_ref[pl.ds(j * 32 + t * 2 + 1, 8, stride=STRIDE), :] = qs[t]
    for t, row in spots():
        r1b_ref[0, tile_rows(row), :] = ps[t] - c_ref[0, tile_rows(row), :]
        r1b_ref[1, tile_rows(row), :] = qs[t] - c_ref[1, tile_rows(row), :]

    def finish(k, p, q):
        for field, x in enumerate((p, q)):
            done = c_ref[field, pl.ds(k, PACKED, stride=8), :] + x
            o_ref[pl.ds(k * STRIDE + 224 + field, TILES, stride=2), :] = done[0:TILES]
        copy = pltpu.make_async_copy(
            o_ref.at[pl.ds(k * STRIDE + 224, 32)], out_ref.at[pl.ds(k * 256 + 224, 32)], sems.at[FACTOR + k]
        )
        copy.start()
        copies.append(copy)

    p, q = d_ref[2], d_ref[3]
    last_p, last_q = apply2(p, q, w2)
    mp = mq = None
    for k in range(FACTOR):
        rp, rq = r1b_ref[0, pl.ds(k, PACKED, stride=8), :], r1b_ref[1, pl.ds(k, PACKED, stride=8), :]
        if k == 0:
            mp, mq = rp, rq
        else:
            mp, mq = phi_packed(mp, mq, w1)
            mp, mq = mp + rp, mq + rq
        if k < FACTOR - 1:
            p, q = phi_packed(p, q, w1)
            p, q = p + rp, q + rq
            finish(k, p, q)
    finish(FACTOR - 1, last_p + mp, last_q + mq)
    for copy in copies:
        copy.wait()


VMEM = pl.BlockSpec(memory_space=pltpu.VMEM)
SMEM = pl.BlockSpec(memory_space=pltpu.SMEM)
STATE = (2, PACKED * 8, LANES)


def shaped(*shape):
    return jax.ShapeDtypeStruct(shape, jnp.float32)


def scratch(*shape):
    return pltpu.VMEM(shape, jnp.float32)


ANY = pl.BlockSpec(memory_space=pl.ANY)
HBM = pl.BlockSpec(memory_space=pltpu.HBM)
SMALL = pltpu.CompilerParams(vmem_limit_bytes=8 << 20)
DENSE = pltpu.CompilerParams(vmem_limit_bytes=8 << 20)


def edge_stage(flat, friction, compressor, blocks):
    return pl.pallas_call(
        edge_kernel,
        out_shape=(shaped(PADDED, LANES), shaped(EDGE_ROWS, LANES), shaped(EDGE_ROWS, LANES), shaped(TILES, LANES), shaped(TABLE, 8, LANES)),
        in_specs=[HBM] * 4,
        out_specs=(VMEM,) * 5,
        scratch_shapes=[pltpu.VMEM((TILES, LANES), jnp.int32)] * 2
        + [pltpu.SMEM((3, 2, 2, KINDS), jnp.float32), pltpu.SemaphoreType.DMA((FACTOR + 3,))],
        compiler_params=SMALL,
        name="edge",
    )(flat, friction, compressor, blocks)


PREPARED = (shaped(20, 8, LANES), shaped(2 * LANES, 2 * LANES))
PREPARING = [
    scratch(2 * LANES, 2 * LANES),
    scratch((FACTOR + 1) * GROUPS * 8, 2 * LANES),
    scratch(FACTOR * GROUPS * 8, 2 * LANES),
]


def main_stage(table, padded, kinds):
    return pl.pallas_call(
        main_kernel,
        out_shape=(shaped(*STATE), shaped(12, PACKED, LANES)),
        in_specs=[VMEM] * 3,
        out_specs=(VMEM,) * 2,
        compiler_params=DENSE,
        name="main",
    )(table, padded, kinds)


def first_stage(table, padded, right, left, kinds, r1, weights):
    return pl.pallas_call(
        first_kernel,
        out_shape=(
            shaped(*STATE),
            shaped(12, PACKED, LANES),
            shaped(2, PACKED, LANES),
            shaped(PACKED, LANES),
            shaped(2 * WINDOWS, LANES),
            shaped(128, LANES),
        ),
        in_specs=[VMEM] * 7,
        out_specs=(VMEM,) * 6,
        input_output_aliases={5: 0, 6: 1},
        scratch_shapes=[scratch(*STATE)] * 3 + [scratch(2 * WINDOWS, LANES)],
        compiler_params=DENSE,
        name="first",
    )(table, padded, right, left, kinds, r1, weights)


def prepare_stage(place, table, kinds):
    return pl.pallas_call(
        prepare_kernel,
        out_shape=PREPARED,
        in_specs=[SMEM, VMEM, VMEM],
        out_specs=(VMEM, VMEM),
        scratch_shapes=PREPARING,
        compiler_params=DENSE,
        name="prepare",
    )(place, table, kinds)


def slab_stage(scan, dense, got):
    return pl.pallas_call(
        slab_kernel,
        out_shape=shaped(2 * WINDOWS, LANES),
        in_specs=[VMEM] * 3,
        out_specs=VMEM,
        scratch_shapes=[scratch(WINDOWS, 2 * LANES)] + [scratch(2 * WINDOWS, LANES)] * 2,
        compiler_params=SMALL,
        name="slab",
    )(scan, dense, got)


def last_stage(padded, halo, r1, r2, weights, got):
    return pl.pallas_call(
        last_kernel,
        out_shape=shaped(2048, LANES),
        in_specs=[VMEM] * 6,
        out_specs=ANY,
        scratch_shapes=[scratch(*STATE)] * 3
        + [scratch(4, PACKED, LANES), scratch(PADDED, LANES), scratch(2 * WINDOWS, LANES), pltpu.SemaphoreType.DMA((2 * FACTOR,))],
        compiler_params=DENSE,
        name="last",
    )(padded, halo, r1, r2, weights, got)


def to_rows(forcing):
    return forcing.reshape(64, 2, TILES, LANES).transpose(0, 2, 1, 3).reshape(2048, LANES)


def from_rows(rows):
    return rows.reshape(64, TILES, 2, LANES).transpose(0, 2, 1, 3).reshape(64, 2, TILES * LANES)


def transpose_windows(rows):
    return lax.all_to_all(rows.reshape(WINDOWS, 2, LANES), "tm", 0, 0, axis_index_groups=[ORDER]).reshape(2 * WINDOWS, LANES)


def per_device(forcing, friction_class, compressor, blocks):
    flat = to_rows(forcing)
    friction = friction_class.reshape(TILES, LANES)
    station = compressor.reshape(TILES, LANES)
    count = lax.axis_size("net")
    flat, friction, station, blocks = (
        pltpu.with_memory_space_constraint(x, pltpu.HBM) for x in (flat, friction, station, blocks)
    )
    padded, low, high, kinds, table = edge_stage(flat, friction, station, blocks)
    left = lax.ppermute(high, "net", [(i, i + 1) for i in range(count - 1)])
    right = lax.ppermute(low, "net", [(i + 1, i) for i in range(count - 1)])
    r1, weights = main_stage(table, padded, kinds)
    r1, weights, r2, kinds_wide, send, halo = first_stage(table, padded, right, left, kinds, r1, weights)
    got = transpose_windows(send)
    place = lax.axis_index("tm").astype(jnp.int32).reshape(1)
    scan, dense = prepare_stage(place, table, kinds_wide)
    got = transpose_windows(slab_stage(scan, dense, got))
    return from_rows(last_stage(padded, halo, r1, r2, weights, got))


def solution(mesh):
    placed = (P("tm", None, "net"), P("net"), P("net"), P())
    return jax.shard_map(
        per_device, mesh=mesh, in_specs=placed, out_specs=P("tm", None, "net"), check_vma=False
    )
```

```python
import jax
import jax.numpy as jnp
from jax import lax
from jax.experimental import pallas as pl
from jax.experimental.pallas import tpu as pltpu
from jax.sharding import PartitionSpec as P

FACTOR = 8
KINDS = 9
TABLE = 12 * KINDS
LANES = 128
TILES = 16
WINDOWS = 64
PACKED = 24
RIGHT = 16
LEFT = 23
EDGE_ROWS = 72
STRIDE = 264
PADDED = FACTOR * STRIDE
HALF = LANES // 2
LISTED = TILES + 1
PREV = [TILES] + list(range(TILES))
NEXT = list(range(1, TILES + 1)) + [0]
MEET = 41
ORDER = [(MEET + rank) % WINDOWS for rank in range(WINDOWS)]
SLAB = 32
REACH = 22
SPAN = 84
COMB = 48
GROUPS = 2 * COMB // 8
TEETH = 24


def runs():
    found = []
    for rank, member in enumerate(ORDER):
        if found and found[-1][1] + found[-1][2] == member:
            found[-1][2] += 1
        else:
            found.append([rank, member, 1])
    return found


def by_rank(to_ref, from_ref):
    for rank, member, length in runs():
        to_ref[2 * rank : 2 * (rank + length), :] = from_ref[2 * member : 2 * (member + length), :]


def by_member(to_ref, from_ref):
    for rank, member, length in runs():
        to_ref[2 * member : 2 * (member + length), :] = from_ref[2 * rank : 2 * (rank + length), :]


def lanes_of(shape):
    return lax.broadcasted_iota(jnp.int32, shape, len(shape) - 1)


def couple(p, q, p_low, p_high, q_low, q_high, w):
    mixed_p = (p + p) + (q_high - q_low)
    mixed_q = (q + q) + (p_low - p_high)
    return w[0] * mixed_p + w[1] * mixed_q, w[2] * mixed_p + w[3] * mixed_q


def apply2(p, q, w):
    return w[0] * p + w[1] * q, w[2] * p + w[3] * q


def phi_tiles(ps, qs, weight_of, before=PREV, behind=NEXT):
    lane = lanes_of((8, LANES))
    first, last = lane == 0, lane == LANES - 1

    def low(xs, t):
        return pltpu.roll(jnp.where(last, xs[before[t]], xs[t]), 1, 1)

    def high(xs, t):
        return pltpu.roll(jnp.where(first, xs[behind[t]], xs[t]), LANES - 1, 1)

    new_p, new_q = [], []
    for t in range(len(ps)):
        p, q = couple(ps[t], qs[t], low(ps, t), high(ps, t), low(qs, t), high(qs, t), weight_of(t))
        new_p.append(p)
        new_q.append(q)
    return new_p, new_q


def phi_packed(p, q, w):
    lane = lanes_of((PACKED, LANES))
    first, last = lane == 0, lane == LANES - 1

    def low(x):
        return pltpu.roll(jnp.where(last, pltpu.roll(x, 1, 0), x), 1, 1)

    def high(x):
        return pltpu.roll(jnp.where(first, pltpu.roll(x, PACKED - 1, 0), x), LANES - 1, 1)

    return couple(p, q, low(p), high(p), low(q), high(q), w)


def phi_slab(p, q, w):
    return couple(
        p, q, pltpu.roll(p, 1, 1), pltpu.roll(p, LANES - 1, 1), pltpu.roll(q, 1, 1), pltpu.roll(q, LANES - 1, 1), w
    )


def pick(table_ref, number, kind):
    masks = [kind == float(k + 1) for k in range(KINDS)]
    picked = []
    for entry in range(4):
        chosen = jnp.zeros_like(kind)
        for k in range(KINDS):
            choice = table_ref[(number * 4 + entry) * KINDS + k]
            if kind.shape[0] != 8:
                choice = jnp.concatenate([choice] * (kind.shape[0] // 8))
            chosen = jnp.where(masks[k], choice, chosen)
        picked.append(chosen)
    return picked


def load_forcing(f_ref, halo_ref, j, t, field):
    if t < TILES:
        return f_ref[pl.ds(j * 32 + t * 2 + field, 8, stride=STRIDE), :]
    return halo_ref[pl.ds((j * 2 + field) * 8, 8), :]


def tile_rows(row):
    return pl.ds(row * 8, 8)


def tiles_from(ref, field):
    both = jnp.where(lanes_of((8, LANES)) < HALF, ref[field, tile_rows(RIGHT), :], ref[field, tile_rows(LEFT), :])
    return [ref[field, tile_rows(t), :] for t in range(TILES)] + [both]


def spots():
    return [(t, t) for t in range(TILES)] + [(TILES, RIGHT), (TILES, LEFT)]


def fine_weights(w_ref):
    def weight_of(t):
        return [jnp.broadcast_to(w_ref[e, t : t + 1, :], (8, LANES)) for e in range(4)]

    return weight_of


def edge_kernel(source_ref, fc_hbm, comp_hbm, blocks_hbm, f_ref, low_ref, high_ref, kind_ref, table_ref, fc_ref, comp_ref,
                blocks_ref, sems):
    copies = [
        pltpu.make_async_copy(source_ref.at[pl.ds(k * 256, 256)], f_ref.at[pl.ds(k * STRIDE, 256)], sems.at[k])
        for k in range(FACTOR)
    ]
    labels = [
        pltpu.make_async_copy(fc_hbm, fc_ref, sems.at[FACTOR]),
        pltpu.make_async_copy(comp_hbm, comp_ref, sems.at[FACTOR + 1]),
        pltpu.make_async_copy(blocks_hbm, blocks_ref, sems.at[FACTOR + 2]),
    ]
    for copy in copies + labels:
        copy.start()
    for copy in labels:
        copy.wait()
    kinds = jnp.where(comp_ref[...] == 1, KINDS, fc_ref[...] + 1).astype(jnp.float32)
    kind_ref[...] = kinds
    low_ref[64:EDGE_ROWS, :] = jnp.broadcast_to(kinds[0:1], (8, LANES))
    high_ref[64:EDGE_ROWS, :] = jnp.broadcast_to(kinds[TILES - 1 : TILES], (8, LANES))
    for number in range(3):
        scale = 1.0 if number == 2 else 0.25
        for entry in range(4):
            for k in range(KINDS):
                value = blocks_ref[number, entry // 2, entry % 2, k] * scale
                table_ref[(number * 4 + entry) * KINDS + k] = jnp.full((8, LANES), value, jnp.float32)
    left_half = lanes_of((8, LANES)) < HALF
    for copy in copies:
        copy.wait()
    for j in range(FACTOR):
        rows = pl.ds(j * 8, 8)
        p, q = (f_ref[pl.ds(j * 32 + field, 8, stride=STRIDE), :] for field in range(2))
        low_ref[rows, :] = jnp.where(left_half, p, pltpu.roll(q, HALF, 1))
        p, q = (f_ref[pl.ds(j * 32 + 2 * (TILES - 1) + field, 8, stride=STRIDE), :] for field in range(2))
        high_ref[rows, :] = jnp.where(left_half, pltpu.roll(q, HALF, 1), p)


def fine_weights_at(w_ref, rows):
    def weight_of(t):
        return [jnp.broadcast_to(w_ref[e, rows[t] : rows[t] + 1, :], (8, LANES)) for e in range(4)]

    return weight_of


def relax_from_zero(f_ref, halo_ref, w_ref, tiles, before, behind):
    weight_of = fine_weights_at(w_ref, tiles)
    ps, qs = ([load_forcing(f_ref, halo_ref, 0, t, field) for t in tiles] for field in range(2))
    for j in range(1, FACTOR):
        ps, qs = phi_tiles(ps, qs, weight_of, before, behind)
        ps = [x + load_forcing(f_ref, halo_ref, j, t, 0) for x, t in zip(ps, tiles)]
        qs = [x + load_forcing(f_ref, halo_ref, j, t, 1) for x, t in zip(qs, tiles)]
    return ps, qs


def main_kernel(table_ref, f_ref, kind_ref, r1_ref, w_ref):
    kind = kind_ref[...]
    for number in range(3):
        for entry, chosen in enumerate(pick(table_ref, number, kind)):
            w_ref[number * 4 + entry, 0:TILES, :] = chosen
    tiles = list(range(TILES))
    before, behind = [(t - 1) % TILES for t in tiles], [(t + 1) % TILES for t in tiles]
    ps, qs = relax_from_zero(f_ref, None, w_ref, tiles, before, behind)
    for t in tiles:
        r1_ref[0, tile_rows(t), :] = ps[t]
        r1_ref[1, tile_rows(t), :] = qs[t]


def first_kernel(table_ref, f_ref, right_ref, left_ref, kind_ref, r1_in, w_in, r1_ref, w_ref, r2_ref, kx_ref, send_ref,
                 halo_ref, prev_ref, c_ref, r1b_ref, nat_ref):
    kx_ref[0:TILES, :] = kind_ref[...]
    kx_ref[TILES:PACKED, :] = jnp.zeros((PACKED - TILES, LANES), jnp.float32)
    beyond = jnp.where(lanes_of((1, LANES)) < HALF, right_ref[64:65, :], left_ref[64:65, :])
    kx_ref[RIGHT : RIGHT + 1, :] = beyond
    kx_ref[LEFT : LEFT + 1, :] = beyond
    kind = kx_ref[TILES:PACKED, :]
    for number in range(3):
        for entry, chosen in enumerate(pick(table_ref, number, kind)):
            w_ref[number * 4 + entry, TILES:PACKED, :] = chosen
    weight_of = fine_weights(w_ref)
    w1 = [w_ref[4 + e] for e in range(4)]

    left_half = lanes_of((8, LANES)) < HALF
    for j in range(FACTOR):
        x, y = right_ref[pl.ds(j * 8, 8), :], left_ref[pl.ds(j * 8, 8), :]
        halo_ref[pl.ds(j * 16, 8), :] = jnp.where(left_half, x, y)
        halo_ref[pl.ds(j * 16 + 8, 8), :] = pltpu.roll(jnp.where(left_half, y, x), HALF, 1)

    unused = jnp.zeros(((LEFT - RIGHT - 1) * 8, LANES), jnp.float32)
    for field in range(2):
        for ref in (r1_ref, r1b_ref):
            ref[field, (RIGHT + 1) * 8 : LEFT * 8, :] = unused

    strip = [TILES - 2, TILES - 1, TILES, 0, 1]
    ps, qs = relax_from_zero(f_ref, halo_ref, w_ref, strip, [0, 0, 1, 2, 3], [1, 2, 3, 4, 4])
    for at, row in ((1, TILES - 1), (2, RIGHT), (2, LEFT), (3, 0)):
        r1_ref[0, tile_rows(row), :] = ps[at]
        r1_ref[1, tile_rows(row), :] = qs[at]

    def sweep(ref, keep):
        p = q = None
        for k in range(FACTOR):
            rp, rq = ref[0, pl.ds(k, PACKED, stride=8), :], ref[1, pl.ds(k, PACKED, stride=8), :]
            if k == 0:
                p, q = rp, rq
            else:
                p, q = phi_packed(p, q, w1)
                p, q = p + rp, q + rq
            if keep:
                c_ref[0, pl.ds(k, PACKED, stride=8), :] = p
                c_ref[1, pl.ds(k, PACKED, stride=8), :] = q
                if k < FACTOR - 1:
                    prev_ref[0, pl.ds(k + 1, PACKED, stride=8), :] = p
                    prev_ref[1, pl.ds(k + 1, PACKED, stride=8), :] = q
        return p, q

    nothing = jnp.zeros((PACKED, LANES), jnp.float32)
    prev_ref[0, pl.ds(0, PACKED, stride=8), :] = nothing
    prev_ref[1, pl.ds(0, PACKED, stride=8), :] = nothing
    r2p, r2q = sweep(r1_ref, True)
    r2_ref[0] = r2p
    r2_ref[1] = r2q

    ps, qs = tiles_from(prev_ref, 0), tiles_from(prev_ref, 1)
    for j in range(FACTOR):
        ps, qs = phi_tiles(ps, qs, weight_of)
    for field, xs in enumerate((ps, qs)):
        for t, row in spots():
            rows = tile_rows(row)
            r1b_ref[field, rows, :] = xs[t] + (r1_ref[field, rows, :] - c_ref[field, rows, :])
    gp, gq = sweep(r1b_ref, False)

    lane = lanes_of((8, LANES))
    for c, (x, g) in enumerate(((r2p, gp), (r2q, gq))):
        for half in range(2):
            shifted = [
                [y[8 * half : 8 * half + 8] for y in (pltpu.roll(z, 1, 0), z, pltpu.roll(z, PACKED - 1, 0))]
                for z in (x, g)
            ]

            def window(which, offset):
                a, b = shifted[which][0:2] if offset < 0 else shifted[which][1:3]
                start = offset % LANES
                return pltpu.roll(jnp.where(lane >= start, a, b), (LANES - start) % LANES, 1)

            for quarter in range(4):
                origin = SLAB * quarter
                near = window(0, origin + window_start(half))
                far = window(1, origin + share_start(half) - SPAN)
                nat_ref[pl.ds(64 * half + 2 * quarter + c, 8, stride=8), :] = jnp.where(lane < SPAN, near, far)
    by_rank(send_ref, nat_ref)


def window_start(half):
    return -REACH if half else -REACH - 8


def share_start(half):
    return 0 if half else -8


def prepare_kernel(place_ref, table_ref, kx_ref, scan_ref, dense_ref, fine_ref, states_ref, after_ref):
    place = place_ref[0]
    lane1 = lanes_of((1, LANES))
    origin = place * SLAB + (LANES - REACH - 8) + jnp.where(place >= WINDOWS // 2, 8, 0)
    base = origin // LANES - 1
    start = origin % LANES
    base = jnp.where(base < 0, LEFT, base)
    after = jnp.where(base == LEFT, 0, base + 1)
    a, b = kx_ref[pl.ds(base, 1), :], kx_ref[pl.ds(after, 1), :]
    kind = pltpu.roll(jnp.where(lane1 >= start, a, b), LANES - start, 1)
    kind = jnp.broadcast_to(kind, (8, LANES))
    w0, w1, w2 = (pick(table_ref, number, kind) for number in range(3))
    sub = lax.broadcasted_iota(jnp.int32, (8, LANES), 0)
    lane = lanes_of((8, LANES))

    def times(v, w):
        return [
            v[0] * w[0] + v[1] * w[2],
            v[0] * w[1] + v[1] * w[3],
            v[2] * w[0] + v[3] * w[2],
            v[2] * w[1] + v[3] * w[3],
        ]

    one, none = jnp.ones((8, LANES), jnp.float32), jnp.zeros((8, LANES), jnp.float32)
    w = w2
    grown = [one, none, none, one]
    for n, step in enumerate((1, 2, 4)):
        longer = times(grown, w)
        grown = [jnp.where((sub & step) != 0, x, y) for x, y in zip(longer, grown)]
        for e in range(4):
            scan_ref[4 * n + e] = jnp.where(sub >= step, w[e], 0.0)
        w = times(w, w)
    for e in range(4):
        scan_ref[12 + e] = w[e]
        scan_ref[16 + e] = grown[e]

    def combs(gap, teeth):
        made = []
        for n in range(gap // 8):
            hit = lane == sub + 8 * n
            for tooth in range(1, teeth):
                hit = hit | (lane == sub + (8 * n + gap * tooth))
            made.append(jnp.where(hit, 1.0, 0.0))
        blank = [none] * len(made)
        return made + blank, blank + made

    def spread(answers, ref, gap, teeth, reach):
        for n, answer in enumerate(answers):
            field, c = divmod(n, gap // 8)
            for tooth in range(teeth):
                at = sub + (8 * c + gap * tooth)
                near = (lane - at <= reach) & (at - lane <= reach)
                rows = pl.ds(field * LANES + gap * tooth + 8 * c, 8)
                for to in range(2):
                    ref[rows, LANES * to : LANES * (to + 1)] = jnp.where(near, answer[to], 0.0)
        for field in range(2):
            ref[field * LANES + gap * teeth : (field + 1) * LANES, :] = jnp.zeros((LANES - gap * teeth, 2 * LANES), jnp.float32)

    answers = list(zip(*combs(TEETH, 4)))
    for _ in range(FACTOR):
        answers = [phi_slab(p, q, w0) for p, q in answers]
    spread(answers, fine_ref, TEETH, 4, FACTOR)

    def rows_of(k, n):
        return pl.ds((k * GROUPS + n) * 8, 8)

    begin = list(zip(*combs(COMB, 2)))
    states = begin
    for k in range(FACTOR + 1):
        for n, (p, q) in enumerate(states):
            states_ref[rows_of(k, n), 0:LANES] = p
            states_ref[rows_of(k, n), LANES : 2 * LANES] = q
        if k < FACTOR:
            states = [phi_slab(p, q, w1) for p, q in states]
    after_ref[...] = jnp.dot(
        states_ref[0 : FACTOR * GROUPS * 8, :],
        fine_ref[...],
        precision=lax.Precision.HIGHEST,
        preferred_element_type=jnp.float32,
    )

    def residual(k, n):
        return [
            after_ref[rows_of(k, n), LANES * to : LANES * (to + 1)]
            - states_ref[rows_of(k + 1, n), LANES * to : LANES * (to + 1)]
            for to in range(2)
        ]

    m = [residual(0, n) for n in range(GROUPS)]
    for k in range(1, FACTOR):
        stepped = [phi_slab(p, q, w1) for p, q in m]
        m = [[x + y for x, y in zip(stepped[n], residual(k, n))] for n in range(GROUPS)]

    total = []
    for n in range(GROUPS):
        coarse = apply2(*begin[n], w2)
        total.append([m[n][to] + (states[n][to] - coarse[to]) for to in range(2)])
    spread(total, dense_ref, COMB, 2, REACH)


def slab_kernel(scan_ref, dense_ref, ranked_ref, send_ref, d_ref, got_ref, nat_ref):
    by_member(got_ref, ranked_ref)
    lane = lanes_of((8, LANES))
    masked = [[scan_ref[4 * n + e] for e in range(4)] for n in range(3)]
    w_eight = [scan_ref[12 + e] for e in range(4)]
    grown = [scan_ref[16 + e] for e in range(4)]
    first = lax.broadcasted_iota(jnp.int32, (8, LANES), 0) == 0

    def recurrence(rp, rq):
        yp, yq = list(rp), list(rq)
        for n, step in enumerate((1, 2, 4)):
            for b in range(8):
                sp, sq = apply2(pltpu.roll(yp[b], step, 0), pltpu.roll(yq[b], step, 0), masked[n])
                yp[b], yq[b] = yp[b] + sp, yq[b] + sq
        dp, dq = [], []
        tp = tq = None
        for b in range(8):
            bp, bq = pltpu.roll(yp[b], 1, 0), pltpu.roll(yq[b], 1, 0)
            bp, bq = jnp.where(first, 0.0, bp), jnp.where(first, 0.0, bq)
            ep, eq = yp[b][7:8], yq[b][7:8]
            ep, eq = jnp.broadcast_to(ep, (8, LANES)), jnp.broadcast_to(eq, (8, LANES))
            if b:
                sp, sq = apply2(tp, tq, grown)
                bp, bq = bp + sp, bq + sq
                sp, sq = apply2(tp, tq, w_eight)
                ep, eq = ep + sp, eq + sq
            tp, tq = ep, eq
            dp.append(bp)
            dq.append(bq)
        return dp, dq

    def rows(b, c):
        return pl.ds(b * 16 + c, 8, stride=2)

    gotten = [[got_ref[rows(b, c), :] for b in range(8)] for c in range(2)]
    dp, dq = recurrence(*gotten)
    for b in range(8):
        d_ref[8 * b : 8 * b + 8, 0:LANES] = dp[b]
        d_ref[8 * b : 8 * b + 8, LANES : 2 * LANES] = dq[b]
    answer = jnp.dot(d_ref[...], dense_ref[...], precision=lax.Precision.HIGHEST, preferred_element_type=jnp.float32)
    back = SPAN - REACH
    residual = [
        [
            answer[8 * b : 8 * b + 8, LANES * c : LANES * (c + 1)] + pltpu.roll(gotten[c][b], LANES - back, 1)
            for b in range(8)
        ]
        for c in range(2)
    ]
    ep, eq = recurrence(*residual)
    for b in range(8):
        nat_ref[rows(b, 0), :] = jnp.where(lane < SPAN, dp[b], pltpu.roll(ep[b], back, 1))
        nat_ref[rows(b, 1), :] = jnp.where(lane < SPAN, dq[b], pltpu.roll(eq[b], back, 1))
    by_rank(send_ref, nat_ref)


def last_kernel(f_ref, halo_ref, r1_ref, r2_ref, w_ref, ranked_ref, out_ref, prev_ref, c_ref, r1b_ref, d_ref,
                o_ref, got_ref, sems):
    by_member(got_ref, ranked_ref)

    lane = lanes_of((8, LANES))
    lane1 = lanes_of((1, LANES))
    for c in range(2):
        for cycle in range(2):
            for half in range(2):
                begin = (SPAN - share_start(half)) if cycle else -window_start(half)
                whole = jnp.zeros((8, LANES), jnp.float32)
                for quarter in range(4):
                    piece = got_ref[pl.ds(64 * half + 2 * quarter + c, 8, stride=8), :]
                    piece = pltpu.roll(piece, (SLAB * quarter - begin) % LANES, 1)
                    mine = (lane >= SLAB * quarter) & (lane < SLAB * (quarter + 1))
                    whole = jnp.where(mine, piece, whole)
                d_ref[2 * cycle + c, 8 * half : 8 * half + 8, :] = whole
            d_ref[2 * cycle + c, TILES:PACKED, :] = jnp.zeros((PACKED - TILES, LANES), jnp.float32)
            width = 8 if cycle else 24
            begin = (SPAN - share_start(0)) if cycle else -window_start(0)
            low = pltpu.roll(got_ref[c : c + 1, :], LANES - begin, 1)
            d_ref[2 * cycle + c, LEFT : LEFT + 1, :] = jnp.where(lane1 >= LANES - width, low, 0.0)
            begin = (SPAN - share_start(1)) if cycle else -window_start(1)
            end = (WINDOWS - 1) * 2 + c
            high = pltpu.roll(got_ref[end : end + 1, :], LANES - begin - SLAB, 1)
            d_ref[2 * cycle + c, RIGHT : RIGHT + 1, :] = jnp.where(lane1 < width, high, 0.0)

    weight_of = fine_weights(w_ref)
    w1 = [w_ref[4 + e] for e in range(4)]
    w2 = [w_ref[8 + e] for e in range(4)]
    unused = jnp.zeros(((LEFT - RIGHT - 1) * 8, LANES), jnp.float32)
    for field in range(2):
        r1b_ref[field, (RIGHT + 1) * 8 : LEFT * 8, :] = unused

    p, q = d_ref[0], d_ref[1]
    last_p, last_q = apply2(p, q, w2)
    c_ref[0, pl.ds(FACTOR - 1, PACKED, stride=8), :] = last_p + r2_ref[0]
    c_ref[1, pl.ds(FACTOR - 1, PACKED, stride=8), :] = last_q + r2_ref[1]
    prev_ref[0, pl.ds(0, PACKED, stride=8), :] = p
    prev_ref[1, pl.ds(0, PACKED, stride=8), :] = q
    for k in range(FACTOR - 1):
        p, q = phi_packed(p, q, w1)
        p = p + r1_ref[0, pl.ds(k, PACKED, stride=8), :]
        q = q + r1_ref[1, pl.ds(k, PACKED, stride=8), :]
        c_ref[0, pl.ds(k, PACKED, stride=8), :] = p
        c_ref[1, pl.ds(k, PACKED, stride=8), :] = q
        prev_ref[0, pl.ds(k + 1, PACKED, stride=8), :] = p
        prev_ref[1, pl.ds(k + 1, PACKED, stride=8), :] = q

    ps, qs = tiles_from(prev_ref, 0), tiles_from(prev_ref, 1)
    for j in range(FACTOR):
        ps, qs = phi_tiles(ps, qs, weight_of)
        if j == FACTOR - 1:
            copies = [
                pltpu.make_async_copy(o_ref.at[pl.ds(k * STRIDE, 224)], out_ref.at[pl.ds(k * 256, 224)], sems.at[k])
                for k in range(FACTOR)
            ]
            for copy in copies:
                copy.start()
        for t in range(LISTED):
            ps[t] = ps[t] + load_forcing(f_ref, halo_ref, j, t, 0)
            qs[t] = qs[t] + load_forcing(f_ref, halo_ref, j, t, 1)
            if j < FACTOR - 1 and t < TILES:
                o_ref[pl.ds(j * 32 + t * 2, 8, stride=STRIDE), :] = ps[t]
                o_ref[pl.ds(j * 32 + t * 2 + 1, 8, stride=STRIDE), :] = qs[t]
    for t, row in spots():
        r1b_ref[0, tile_rows(row), :] = ps[t] - c_ref[0, tile_rows(row), :]
        r1b_ref[1, tile_rows(row), :] = qs[t] - c_ref[1, tile_rows(row), :]

    def finish(k, p, q):
        for field, x in enumerate((p, q)):
            done = c_ref[field, pl.ds(k, PACKED, stride=8), :] + x
            o_ref[pl.ds(k * STRIDE + 224 + field, TILES, stride=2), :] = done[0:TILES]
        copy = pltpu.make_async_copy(
            o_ref.at[pl.ds(k * STRIDE + 224, 32)], out_ref.at[pl.ds(k * 256 + 224, 32)], sems.at[FACTOR + k]
        )
        copy.start()
        copies.append(copy)

    p, q = d_ref[2], d_ref[3]
    last_p, last_q = apply2(p, q, w2)
    mp = mq = None
    for k in range(FACTOR):
        rp, rq = r1b_ref[0, pl.ds(k, PACKED, stride=8), :], r1b_ref[1, pl.ds(k, PACKED, stride=8), :]
        if k == 0:
            mp, mq = rp, rq
        else:
            mp, mq = phi_packed(mp, mq, w1)
            mp, mq = mp + rp, mq + rq
        if k < FACTOR - 1:
            p, q = phi_packed(p, q, w1)
            p, q = p + rp, q + rq
            finish(k, p, q)
    finish(FACTOR - 1, last_p + mp, last_q + mq)
    for copy in copies:
        copy.wait()


VMEM = pl.BlockSpec(memory_space=pltpu.VMEM)
SMEM = pl.BlockSpec(memory_space=pltpu.SMEM)
STATE = (2, PACKED * 8, LANES)


def shaped(*shape):
    return jax.ShapeDtypeStruct(shape, jnp.float32)


def scratch(*shape):
    return pltpu.VMEM(shape, jnp.float32)


ANY = pl.BlockSpec(memory_space=pl.ANY)
HBM = pl.BlockSpec(memory_space=pltpu.HBM)
SMALL = pltpu.CompilerParams(vmem_limit_bytes=8 << 20)
DENSE = pltpu.CompilerParams(vmem_limit_bytes=8 << 20)


def edge_stage(flat, friction, compressor, blocks):
    return pl.pallas_call(
        edge_kernel,
        out_shape=(shaped(PADDED, LANES), shaped(EDGE_ROWS, LANES), shaped(EDGE_ROWS, LANES), shaped(TILES, LANES), shaped(TABLE, 8, LANES)),
        in_specs=[HBM] * 4,
        out_specs=(VMEM,) * 5,
        scratch_shapes=[pltpu.VMEM((TILES, LANES), jnp.int32)] * 2
        + [pltpu.SMEM((3, 2, 2, KINDS), jnp.float32), pltpu.SemaphoreType.DMA((FACTOR + 3,))],
        compiler_params=SMALL,
        name="edge",
    )(flat, friction, compressor, blocks)


PREPARED = (shaped(20, 8, LANES), shaped(2 * LANES, 2 * LANES))
PREPARING = [
    scratch(2 * LANES, 2 * LANES),
    scratch((FACTOR + 1) * GROUPS * 8, 2 * LANES),
    scratch(FACTOR * GROUPS * 8, 2 * LANES),
]


def main_stage(table, padded, kinds):
    return pl.pallas_call(
        main_kernel,
        out_shape=(shaped(*STATE), shaped(12, PACKED, LANES)),
        in_specs=[VMEM] * 3,
        out_specs=(VMEM,) * 2,
        compiler_params=DENSE,
        name="main",
    )(table, padded, kinds)


def first_stage(table, padded, right, left, kinds, r1, weights):
    return pl.pallas_call(
        first_kernel,
        out_shape=(
            shaped(*STATE),
            shaped(12, PACKED, LANES),
            shaped(2, PACKED, LANES),
            shaped(PACKED, LANES),
            shaped(2 * WINDOWS, LANES),
            shaped(128, LANES),
        ),
        in_specs=[VMEM] * 7,
        out_specs=(VMEM,) * 6,
        input_output_aliases={5: 0, 6: 1},
        scratch_shapes=[scratch(*STATE)] * 3 + [scratch(2 * WINDOWS, LANES)],
        compiler_params=DENSE,
        name="first",
    )(table, padded, right, left, kinds, r1, weights)


def prepare_stage(place, table, kinds):
    return pl.pallas_call(
        prepare_kernel,
        out_shape=PREPARED,
        in_specs=[SMEM, VMEM, VMEM],
        out_specs=(VMEM, VMEM),
        scratch_shapes=PREPARING,
        compiler_params=DENSE,
        name="prepare",
    )(place, table, kinds)


def slab_stage(scan, dense, got):
    return pl.pallas_call(
        slab_kernel,
        out_shape=shaped(2 * WINDOWS, LANES),
        in_specs=[VMEM] * 3,
        out_specs=VMEM,
        scratch_shapes=[scratch(WINDOWS, 2 * LANES)] + [scratch(2 * WINDOWS, LANES)] * 2,
        compiler_params=SMALL,
        name="slab",
    )(scan, dense, got)


def last_stage(padded, halo, r1, r2, weights, got):
    return pl.pallas_call(
        last_kernel,
        out_shape=shaped(2048, LANES),
        in_specs=[VMEM] * 6,
        out_specs=ANY,
        scratch_shapes=[scratch(*STATE)] * 3
        + [scratch(4, PACKED, LANES), scratch(PADDED, LANES), scratch(2 * WINDOWS, LANES), pltpu.SemaphoreType.DMA((2 * FACTOR,))],
        compiler_params=DENSE,
        name="last",
    )(padded, halo, r1, r2, weights, got)


def to_rows(forcing):
    return forcing.reshape(64, 2, TILES, LANES).transpose(0, 2, 1, 3).reshape(2048, LANES)


def from_rows(rows):
    return rows.reshape(64, TILES, 2, LANES).transpose(0, 2, 1, 3).reshape(64, 2, TILES * LANES)


def transpose_windows(rows):
    return lax.all_to_all(rows.reshape(WINDOWS, 2, LANES), "tm", 0, 0, axis_index_groups=[ORDER]).reshape(2 * WINDOWS, LANES)


def per_device(forcing, friction_class, compressor, blocks):
    flat = to_rows(forcing)
    friction = friction_class.reshape(TILES, LANES)
    station = compressor.reshape(TILES, LANES)
    count = lax.axis_size("net")
    flat, friction, station, blocks = (
        pltpu.with_memory_space_constraint(x, pltpu.HBM) for x in (flat, friction, station, blocks)
    )
    padded, low, high, kinds, table = edge_stage(flat, friction, station, blocks)
    left = lax.ppermute(high, "net", [(i, i + 1) for i in range(count - 1)])
    right = lax.ppermute(low, "net", [(i + 1, i) for i in range(count - 1)])
    r1, weights = main_stage(table, padded, kinds)
    r1, weights, r2, kinds_wide, send, halo = first_stage(table, padded, right, left, kinds, r1, weights)
    got = transpose_windows(send)
    place = lax.axis_index("tm").astype(jnp.int32).reshape(1)
    scan, dense = prepare_stage(place, table, kinds_wide)
    got = transpose_windows(slab_stage(scan, dense, got))
    return from_rows(last_stage(padded, halo, r1, r2, weights, got))


def solution(mesh):
    placed = (P("tm", None, "net"), P("net"), P("net"), P())
    return jax.shard_map(
        per_device, mesh=mesh, in_specs=placed, out_specs=P("tm", None, "net"), check_vma=False
    )
```
